32 devices in a mesh: groups: 2 (over y), row: 16 (over z, x, core).
Axes of the slice: x: 2, y: 2, z: 4, core: 2. Of those that a mesh axis runs over, the one named last changes fastest.
Arguments:
- object_tiles: bfloat16 [8192, 2, 2048], P(('groups', 'row')), parts along dimension 0, may hold values from -4 to 4
- probe: float32 [4, 256, 2, 256], replicated, may hold values from -3 to 3
- measured: bfloat16 [192, 256, 256], P(('groups', 'row')), parts along dimension 0, may hold values from 0.19921875 to 2.5
- offset_row: int32 [192], P(('groups', 'row')), parts along dimension 0, may hold values from 0 to 255
- offset_col: int32 [192], P(('groups', 'row')), parts along dimension 0, may hold values from 0 to 1791
- subpixel: int32 [192], P(('groups', 'row')), parts along dimension 0, may hold values from 0 to 15
- live_count: int32 [32], P(('groups', 'row')), parts along dimension 0, may hold values from 1 to 6, 48 in all
Outputs:
- object_grad: float32 [8192, 2, 2048], P(('groups', 'row')), parts along dimension 0
- probe_grad: float32 [8, 256, 2, 256], P('groups'), parts along dimension 0
- position_grad: float32 [2, 192], P(None, ('groups', 'row')), parts along dimension 1
The draws below stay inside these ranges and needn't reach their ends.
There are 2 independent parts, one for each index of `groups`. The reference program is written for one: setup_inputs(seed, part) draws one part's arguments, and reference() takes and returns one part's arrays. A program takes and returns all parts, laid end to end along the dimension named above; an argument that names none is the same for every part. Nothing has to cross between parts.
Inputs may be any that keep to these rules, and one draw needn't show every extreme that they name: Device d's live slots are its first live_count[d] slots; live_count sums to 48 and reaches 6 on some device.
All inputs are finite; a program needn't handle non-finite values.
Results may differ from the reference program's by a relative error of at most 0.0099.
Values may be sent and summed in bfloat16 or wider, within the bound.
A program may use at most 128 MiB of HBM per device.

```python
import math
import jax
import jax.numpy as jnp
import numpy as np
from jax import lax

PATCH = 256
MODES = 4
ROWS_DEV = 256
OW = 2048
SLOTS = 6
OH = 4096
NPOS = 96
MINI = 48
N_ROW = 16


def set_ends(array, key, low, high):
    dims = array.shape
    spot = [jax.random.randint(jax.random.fold_in(key, axis), (), 0, dims[axis]) for axis in range(len(dims))]
    array = array.at[tuple(spot)].set(low)
    longest = dims.index(max(dims))
    spot[longest] = (spot[longest] + 1) % dims[longest]
    return array.at[tuple(spot)].set(high)


def block_scale(rng, dims, shards, least, high):
    factor_of = 1.0
    for dim, shards_of in shards:
        heights = jax.random.uniform(jax.random.fold_in(jax.random.fold_in(rng, 6), dim), (shards_of,), jnp.float32, least / len(shards), high / len(shards))
        factor_of = factor_of * jnp.repeat(jnp.exp(heights), dims[dim] // shards_of).reshape((-1,) + (1,) * (len(dims) - 1 - dim))
    return factor_of


def split_up(number_of, total, reach, lean):
    portions = [(1 << 20) // math.isqrt(grade ** lean) + 1 for grade in range(2, number_of + 1)]
    spare, counts = total - reach - (number_of - 1), [1] * (number_of - 1)
    while spare > 0:
        movable = [i for i in range(number_of - 1) if counts[i] < reach]
        mass, budget = sum([portions[i] for i in movable]), spare
        for i in movable:
            more = min(reach - counts[i], max(1, budget * portions[i] // mass), spare)
            counts[i] = counts[i] + more
            spare = spare - more
    return np.array([reach] + counts)


def uneven(stream_key, amount, total, most, lean):
    if amount == 2:
        one = jax.random.randint(stream_key, (), max(1, total - most), min(most, total - 1) + 1)
        return jnp.stack([one, total - one])
    tallies = jnp.asarray(split_up(amount, total, most, lean), jnp.int32)
    pairs = (amount - 1) // 2
    source_of, sink = tallies[1:1 + 2 * pairs:2], tallies[2:2 + 2 * pairs:2]
    slack = jnp.minimum(source_of - 1, most - sink)
    moved = jax.random.randint(jax.random.fold_in(stream_key, 1), (pairs,), 0, 1 << 20) % (slack + 1)
    tallies = tallies.at[1:1 + 2 * pairs:2].set(source_of - moved).at[2:2 + 2 * pairs:2].set(sink + moved)
    return tallies[jax.random.permutation(jax.random.fold_in(stream_key, 2), amount)]


def centred(stream_key, extent, width, most, pieces=(), held_as=jnp.bfloat16):
    entries = jax.random.normal(stream_key, extent, jnp.float32) * width
    if len(pieces) > 0:
        entries = block_scale(stream_key, extent, pieces, -0.22, 0.18) * entries
    return jnp.clip(entries, min=-most, max=most).astype(held_as)


def setup_inputs(seed: int = 0, part: int = 0) -> dict:
    key_of = jax.random.split(jax.random.key(seed), 8)
    part_splits = jax.random.split(jax.random.fold_in(key_of[7], part), 8)
    object_tiles = centred(part_splits[0], (OH, 2, OW), 0.7, 4.0, ((0, 16),))
    probe = centred(key_of[1], (MODES, PATCH, 2, PATCH), 0.5, 3.0, (), jnp.float32)
    measured = jnp.clip(0.19921875 + 2.3007812 * jax.random.uniform(part_splits[2], (NPOS, PATCH, PATCH), jnp.float32) ** block_scale(part_splits[2], (NPOS, PATCH, PATCH), ((0, 16),), -0.2, 0.2), 0.19921875, 2.5).astype(jnp.bfloat16)
    offset_row = set_ends(jax.random.randint(part_splits[3], (NPOS,), 0, ROWS_DEV), jax.random.fold_in(part_splits[3], 1), 0, ROWS_DEV - 1).astype(jnp.int32)
    offset_col = set_ends(jax.random.randint(part_splits[4], (NPOS,), 0, OW - PATCH), jax.random.fold_in(part_splits[4], 1), 0, (OW - PATCH) - 1).astype(jnp.int32)
    subpixel = set_ends(jax.random.randint(part_splits[5], (NPOS,), 0, 16), jax.random.fold_in(part_splits[5], 1), 0, 15).astype(jnp.int32)
    live_count = uneven(part_splits[6], N_ROW, MINI, SLOTS, 2).astype(jnp.int32)
    return {"object_tiles": object_tiles, "probe": probe, "measured": measured, "offset_row": offset_row, "offset_col": offset_col, "subpixel": subpixel, "live_count": live_count}


def dft_tables(patch):
    index = jnp.arange(patch, dtype=jnp.int32)
    phase = index[:, None] * index[None, :] % patch
    angle = phase.astype(jnp.float32) * (2.0 * math.pi / patch)
    scale = 1.0 / math.sqrt(patch)
    cosine = (jnp.cos(angle) * scale).astype(jnp.bfloat16)
    sine = (jnp.sin(angle) * scale).astype(jnp.bfloat16)
    along_x = jnp.concatenate([jnp.concatenate([cosine, -sine], 1), jnp.concatenate([sine, cosine], 1)], 0)
    along_y = jnp.concatenate([jnp.stack([cosine, sine], -1).reshape(patch, 2 * patch), jnp.stack([-sine, cosine], -1).reshape(patch, 2 * patch)], 0)
    inverse_y = jnp.stack([jnp.concatenate([cosine, -sine], 1), jnp.concatenate([sine, cosine], 1)], 1).reshape(2 * patch, 2 * patch)
    inverse_x = jnp.concatenate([jnp.concatenate([cosine, sine], 1), jnp.concatenate([-sine, cosine], 1)], 0)
    return (along_x, along_y, inverse_y, inverse_x)

def fractions(code):
    return ((code // 4).astype(jnp.float32) * 0.25, (code % 4).astype(jnp.float32) * 0.25)

def interpolate(window, code):
    frac_y, frac_x = fractions(code)
    cells = window.astype(jnp.float32)
    size = cells.shape[0] - 1
    upper = (1.0 - frac_x) * cells[:size, :, :size] + frac_x * cells[:size, :, 1:]
    lower = (1.0 - frac_x) * cells[1:, :, :size] + frac_x * cells[1:, :, 1:]
    return (1.0 - frac_y) * upper + frac_y * lower

def spread(grad_patch, frac_y, frac_x):

    def sideways(part):
        return jnp.pad((1.0 - frac_x) * part, ((0, 0), (0, 0), (0, 1))) + jnp.pad(frac_x * part, ((0, 0), (0, 0), (1, 0)))
    upper = sideways((1.0 - frac_y) * grad_patch)
    lower = sideways(frac_y * grad_patch)
    return jnp.pad(upper, ((0, 1), (0, 0), (0, 0))) + jnp.pad(lower, ((1, 0), (0, 0), (0, 0)))

def slopes(window, grad_patch, frac_y, frac_x):
    cells = window.astype(jnp.float32)
    size = cells.shape[0] - 1
    down = cells[1:] - cells[:size]
    slope_y = (1.0 - frac_x) * down[:, :, :size] + frac_x * down[:, :, 1:]
    across = cells[:, :, 1:] - cells[:, :, :size]
    slope_x = (1.0 - frac_y) * across[:size] + frac_y * across[1:]
    return (jnp.sum(grad_patch * slope_y) / size, jnp.sum(grad_patch * slope_x) / size)

def matmul(left, right):
    return jnp.dot(left.astype(jnp.float32), right.astype(jnp.float32), precision=lax.Precision.HIGHEST)

def batched(left, right):
    return jnp.einsum('ab,mbk->mak', left.astype(jnp.float32), right.astype(jnp.float32), precision=lax.Precision.HIGHEST)

def project(patch_obj, amplitude, probe, tables):
    along_x, along_y, inverse_y, inverse_x = tables
    modes = probe.shape[0]
    size = probe.shape[1]
    preal = probe[:, :, 0, :]
    pimag = probe[:, :, 1, :]
    oreal = patch_obj[:, 0, :]
    oimag = patch_obj[:, 1, :]
    wave = jnp.stack([preal * oreal - pimag * oimag, preal * oimag + pimag * oreal], axis=2).astype(jnp.bfloat16)
    first = matmul(wave.reshape(modes * size, 2 * size), along_x).astype(jnp.bfloat16)
    far = batched(along_y, first.reshape(modes, 2 * size, size)).reshape(modes, 2, size, size)
    modulus = jnp.maximum(jnp.sqrt(lax.optimization_barrier(jnp.sum(far * far, axis=(0, 1)))), 0.5)
    ratio = 1.0 - amplitude.astype(jnp.float32) / modulus
    error = (far * ratio).astype(jnp.bfloat16)
    back = batched(inverse_y, error.reshape(modes, 2 * size, size)).astype(jnp.bfloat16)
    exit_grad = matmul(back.reshape(modes * size, 2 * size), inverse_x).reshape(modes, size, 2, size)
    ureal = exit_grad[:, :, 0, :]
    uimag = exit_grad[:, :, 1, :]
    obj_grad = jnp.stack([lax.optimization_barrier(jnp.sum(preal * ureal + pimag * uimag, 0)), lax.optimization_barrier(jnp.sum(preal * uimag - pimag * ureal, 0))], axis=1)
    probe_term = jnp.stack([oreal * ureal + oimag * uimag, oreal * uimag - oimag * ureal], axis=2)
    return (obj_grad, probe_term)

def reference(object_tiles, probe, measured, offset_row, offset_col, subpixel, live_count):
    size = PATCH
    padded = jnp.concatenate([object_tiles, jnp.zeros((size, 2, OW), object_tiles.dtype)], axis=0)
    tables = dft_tables(size)
    start = (jnp.zeros((OH + size, 2, OW), jnp.float32), jnp.zeros(probe.shape, jnp.float32), jnp.zeros((2, NPOS), jnp.float32))

    def device_pass(device, carry):
        device = jnp.asarray(device).astype(jnp.int32)

        def slot_pass(slot, inner):
            grad, probe_acc, moved = inner
            index = device * SLOTS + jnp.asarray(slot).astype(jnp.int32)
            top = (device * ROWS_DEV + offset_row[index]).astype(jnp.int32)
            left = offset_col[index].astype(jnp.int32)
            corner = (top, jnp.int32(0), left)
            window = lax.dynamic_slice(padded, corner, (size + 1, 2, size + 1))
            code = subpixel[index]
            frac_y, frac_x = fractions(code)
            obj_grad, probe_term = project(interpolate(window, code), measured[index], probe, tables)
            region = lax.dynamic_slice(grad, corner, (size + 1, 2, size + 1))
            grad = lax.dynamic_update_slice(grad, region + spread(obj_grad, frac_y, frac_x), corner)
            slope_y, slope_x = slopes(window, obj_grad, frac_y, frac_x)
            moved = moved.at[:, index].set(jnp.stack([slope_y, slope_x]))
            return (grad, probe_acc + probe_term, moved)
        return lax.fori_loop(0, live_count[device], slot_pass, carry)
    grad, probe_acc, moved = lax.fori_loop(0, N_ROW, device_pass, start)
    return (grad[:OH], probe_acc, moved)
```

```python
import functools
import math

import jax
import jax.numpy as jnp
import numpy as np
from jax import lax
from jax.experimental import pallas as pl
from jax.experimental.pallas import tpu as pltpu
from jax.sharding import PartitionSpec as P

LANES = 128
ROWS = 16


def passed_along(x, axis, by):
    length = lax.axis_size(axis)
    pairs = [(i, i + by) for i in range(length) if 0 <= i + by < length]
    return lax.ppermute(x, axis, pairs)


def total_kernel(length, pieces, x_ref, out_ref, near, send1, send2, got0, got1, got2, full, sends, recvs):
    f32, bf16 = jnp.float32, jnp.bfloat16
    lines, width = x_ref.shape
    deep = length // 4
    me = lax.axis_index("row")
    c, b, k = me % 2, (me // 2) % 2, me // 4
    part = lines // pieces
    half, quarter = part // 2, part // 4
    leaf = quarter // deep

    def peer(stage, o):
        if stage in (0, 5):
            return {"row": me + 1 - 2 * c}
        if stage in (1, 4):
            return {"row": me + 2 - 4 * b}
        return {"row": ((k + o) % deep) * 4 + me % 4}

    barrier = pltpu.get_barrier_semaphore()
    others = [(0, 0), (1, 0)] + [(2, o) for o in range(1, deep)]
    for stage, o in others:
        pl.semaphore_signal(barrier, inc=1, device_id=peer(stage, o), device_id_type=pl.DeviceIdType.MESH)
    pl.semaphore_wait(barrier, len(others))

    base = [0, pieces, 2 * pieces, (2 + deep) * pieces, (2 + 2 * deep) * pieces, (3 + 2 * deep) * pieces]

    def rows(start, size):
        return pl.ds(pl.multiple_of(start, ROWS), size)

    def place(q, stage):
        start = q * part
        if stage == 0:
            return start
        start = start + c * half
        if stage == 1:
            return start
        start = start + b * quarter
        return start if stage == 2 else start + k * leaf

    def link(stage, q, o=0):
        at = rows(q * quarter, quarter)
        if stage == 0:
            src, dst = near.at[rows(q * half, half)], got0.at[rows(q * half, half)]
        elif stage == 1:
            src, dst = send1.at[at], got1.at[at]
        elif stage == 2:
            src = send2.at[rows(q * quarter + ((k + o) % deep) * leaf, leaf)]
            dst = got2.at[rows((q * deep + o) * leaf, leaf)]
        elif stage == 3:
            src = dst = full.at[rows(place(q, 3), leaf)]
        elif stage == 4:
            src = dst = full.at[rows(place(q, 2), quarter)]
        else:
            src = dst = full.at[rows(place(q, 1), half)]
        sem = base[stage] + (q * deep + o if stage in (2, 3) else q)
        return pltpu.make_async_remote_copy(
            src_ref=src, dst_ref=dst, send_sem=sends.at[sem], recv_sem=recvs.at[sem],
            device_id=peer(stage, o), device_id_type=pl.DeviceIdType.MESH,
        )

    started = []

    def begin(stage, q):
        for o in range(1, deep) if stage in (2, 3) else (0,):
            copy = link(stage, q, o)
            copy.start()
            started.append(copy)

    def arrive(stage, q):
        for o in range(1, deep) if stage in (2, 3) else (0,):
            link(stage, q, o).wait_recv()

    def act(stage, q):
        if stage == 0:
            near[rows(q * half, half)] = x_ref[rows(q * part + (1 - c) * half, half)].astype(bf16)
        elif stage == 1:
            arrive(0, q)
            away = q * part + c * half + (1 - b) * quarter
            send1[rows(q * quarter, quarter)] = (
                x_ref[rows(away, quarter)] + got0[rows(q * half + (1 - b) * quarter, quarter)].astype(f32)
            ).astype(bf16)
        elif stage == 2:
            arrive(1, q)
            own = (
                x_ref[rows(place(q, 2), quarter)]
                + got0[rows(q * half + b * quarter, quarter)].astype(f32)
                + got1[rows(q * quarter, quarter)].astype(f32)
            )
            send2[rows(q * quarter, quarter)] = own.astype(bf16)
        elif stage == 3:
            arrive(2, q)
            own = (
                x_ref[rows(place(q, 3), leaf)]
                + got0[rows(q * half + b * quarter + k * leaf, leaf)].astype(f32)
                + got1[rows(q * quarter + k * leaf, leaf)].astype(f32)
            )
            for o in range(1, deep):
                own = own + got2[rows((q * deep + o) * leaf, leaf)].astype(f32)
            full[rows(place(q, 3), leaf)] = own.astype(bf16)
        elif stage == 6:
            arrive(5, q)
            at = rows(q * part, part)
            out_ref[at] = full[at].astype(f32)
            return
        else:
            arrive(stage - 1, q)
        begin(stage, q)

    for q in range(pieces):
        act(0, q)
    for t in range(pieces + 6):
        for stage in range(6, 0, -1):
            q = t - stage
            if 0 <= q < pieces:
                act(stage, q)
    for copy in started:
        copy.wait_send()


def summed(x, axis):
    length = lax.axis_size(axis)
    lines = x.size // x.shape[-1]
    if length % 4 or lines % (length * ROWS):
        return lax.psum(x, axis)
    f32, bf16 = jnp.float32, jnp.bfloat16
    width = x.shape[-1]
    pieces = 4 if lines % (length * ROWS * 4) == 0 else 1
    flat = x.reshape(lines, width)
    vmem = pl.BlockSpec(memory_space=pltpu.VMEM)
    count = pieces * (4 + 2 * (length // 4))
    out = pl.pallas_call(
        functools.partial(total_kernel, length, pieces),
        out_shape=jax.ShapeDtypeStruct((lines, width), f32),
        in_specs=[vmem],
        out_specs=vmem,
        scratch_shapes=[
            pltpu.VMEM((lines // 2, width), bf16),
            pltpu.VMEM((lines // 4, width), bf16),
            pltpu.VMEM((lines // 4, width), bf16),
            pltpu.VMEM((lines // 2, width), bf16),
            pltpu.VMEM((lines // 4, width), bf16),
            pltpu.VMEM((lines // 4, width), bf16),
            pltpu.VMEM((lines, width), bf16),
            pltpu.SemaphoreType.DMA((count,)),
            pltpu.SemaphoreType.DMA((count,)),
        ],
        compiler_params=pltpu.CompilerParams(collective_id=0, has_side_effects=True, vmem_limit_bytes=32 << 20),
        name="total",
    )(flat)
    return out.reshape(x.shape)


def dft_tables(patch):
    index = np.arange(patch)
    angle = ((index[:, None] * index[None, :]) % patch).astype(np.float64) * (2.0 * math.pi / patch)
    scale = 1.0 / math.sqrt(patch)
    cosine = jnp.asarray((np.cos(angle) * scale).astype(np.float32)).astype(jnp.bfloat16)
    sine = jnp.asarray((np.sin(angle) * scale).astype(np.float32)).astype(jnp.bfloat16)
    return cosine, sine


def pulled(x, by, tiles):
    lane = lax.broadcasted_iota(jnp.int32, x[0].shape, 1)
    back = lax.rem(LANES - by, LANES)
    parts = [pltpu.roll(x[k], back, 1) for k in range(tiles + 1)]
    keep = lane < LANES - by
    return [jnp.where(keep, parts[k], parts[k + 1]) for k in range(tiles)]


def pushed(x, by, tiles):
    lane = lax.broadcasted_iota(jnp.int32, (x.shape[0], LANES), 1)
    ahead = lax.rem(by, LANES)
    parts = [pltpu.roll(x[:, k * LANES : (k + 1) * LANES], ahead, 1) for k in range(tiles)]
    zero = jnp.zeros_like(parts[0])
    keep = lane >= by
    left = [zero] + parts
    right = parts + [zero]
    return [jnp.where(keep, right[k], left[k]) for k in range(tiles + 1)]


def step_kernel(
    modes, size, rows,
    count_ref, top_ref, left_ref, code_ref,
    own_hbm, rim_hbm, probe_ref, measured_ref, cos_ref, sin_ref,
    grad_ref, below_ref, pgrad_ref, moved_ref,
    ext, win, acc, table_a, table_b, patch, slope, far, power, gsum, sems,
):
    f32, bf16 = jnp.float32, jnp.bfloat16
    tiles = size // LANES
    slots = measured_ref.shape[0]
    wide = size + LANES
    copies = [
        pltpu.make_async_copy(own_hbm, ext.at[:, pl.ds(0, rows), :], sems.at[0]),
        pltpu.make_async_copy(rim_hbm, ext.at[:, pl.ds(rows, size), :], sems.at[1]),
    ]
    for copy in copies:
        copy.start()
    cosine, sine = cos_ref[...], sin_ref[...]
    table_a[0:size, 0:size] = cosine
    table_a[0:size, size : 2 * size] = -sine
    table_a[size : 2 * size, 0:size] = sine
    table_a[size : 2 * size, size : 2 * size] = cosine
    table_b[0:size, 0:size] = cosine
    table_b[0:size, size : 2 * size] = sine
    table_b[size : 2 * size, 0:size] = -sine
    table_b[size : 2 * size, size : 2 * size] = cosine
    pgrad_ref[...] = jnp.zeros_like(pgrad_ref)
    span = 32

    @pl.loop(0, (rows + size) // span)
    def _(i):
        at = pl.ds(pl.multiple_of(i * span, span), span)
        acc[:, :, at, :] = jnp.zeros((2, acc.shape[1], span, LANES), f32)

    for j in range(slots):
        moved_ref[0, j] = 0.0
        moved_ref[1, j] = 0.0
    for copy in copies:
        copy.wait()

    @pl.loop(0, count_ref[0])
    def _(j):
        top, left, code = top_ref[j], left_ref[j], code_ref[j]
        base_row = pl.multiple_of(top // ROWS * ROWS, ROWS)
        row = top - base_row
        base_col = pl.multiple_of(left // LANES * LANES, LANES)
        col = left - base_col
        fy = (code // 4).astype(f32) * 0.25
        fx = (code % 4).astype(f32) * 0.25
        cols = pl.ds(base_col, wide)
        chunk = 64

        for p in range(2):
            cut = ext[p, pl.ds(base_row, size + ROWS), cols].astype(f32)
            for k in range(tiles + 1):
                win[p, k] = cut[:, k * LANES : (k + 1) * LANES]

        @pl.loop(0, size // chunk)
        def _(i):
            at = pl.multiple_of(i * chunk, chunk)
            here = pl.ds(at, chunk)
            for p in range(2):
                v, d = [], []
                for k in range(tiles + 1):
                    upper = win[p, k, pl.ds(at + row, chunk), :]
                    lower = win[p, k, pl.ds(at + row + 1, chunk), :]
                    v.append((1.0 - fy) * upper + fy * lower)
                    d.append(lower - upper)
                v0, v1 = pulled(v, col, tiles), pulled(v, col + 1, tiles)
                d0, d1 = pulled(d, col, tiles), pulled(d, col + 1, tiles)
                for k in range(tiles):
                    to = pl.ds(k * LANES, LANES)
                    patch[p, here, to] = (1.0 - fx) * v0[k] + fx * v1[k]
                    slope[0, p, here, to] = (1.0 - fx) * d0[k] + fx * d1[k]
                    slope[1, p, here, to] = v1[k] - v0[k]

        power[...] = jnp.zeros_like(power)
        gsum[...] = jnp.zeros_like(gsum)

        @pl.loop(0, modes, unroll=True)
        def _(m):
            pr, pi = probe_ref[m, 0], probe_ref[m, 1]
            re, im = patch[0], patch[1]
            wave = jnp.concatenate(
                [(pr * re - pi * im).astype(bf16), (pr * im + pi * re).astype(bf16)], axis=1
            )
            half = jnp.dot(wave, table_a[...], preferred_element_type=f32).astype(bf16)
            stacked = jnp.concatenate([half[:, :size], half[:, size:]], axis=0)
            both = jnp.dot(table_b[...], stacked, preferred_element_type=f32)
            far[m] = both
            fr, fi = both[:size], both[size:]
            power[...] += fr * fr + fi * fi

        modulus = jnp.maximum(jnp.sqrt(power[...]), 0.5)
        power[...] = 1.0 - measured_ref[j].astype(f32) / modulus

        @pl.loop(0, modes, unroll=True)
        def _(m):
            ratio = power[...]
            error = jnp.concatenate(
                [(far[m, :size] * ratio).astype(bf16), (far[m, size:] * ratio).astype(bf16)], axis=0
            )
            back = jnp.dot(table_a[...], error, preferred_element_type=f32).astype(bf16)
            side = jnp.concatenate([back[:size], back[size:]], axis=1)
            exit_grad = jnp.dot(side, table_b[...], preferred_element_type=f32)
            ur, ui = exit_grad[:, :size], exit_grad[:, size:]
            pr, pi = probe_ref[m, 0], probe_ref[m, 1]
            re, im = patch[0], patch[1]
            gsum[0] += pr * ur + pi * ui
            gsum[1] += pr * ui - pi * ur
            pgrad_ref[m, 0] += re * ur + im * ui
            pgrad_ref[m, 1] += re * ui - im * ur

        for s in range(2):
            total = jnp.sum(gsum[0] * slope[s, 0] + gsum[1] * slope[s, 1])
            moved_ref[s, j] = total / size

        @pl.loop(0, size // chunk)
        def _(i):
            at = pl.multiple_of(i * chunk, chunk)
            for p in range(2):
                g = gsum[p, pl.ds(at, chunk), :]
                s0, s1 = pushed(g, col, tiles), pushed(g, col + 1, tiles)
                for k in range(tiles + 1):
                    s = (1.0 - fx) * s0[k] + fx * s1[k]
                    tile = left // LANES + k
                    acc[p, tile, pl.ds(top + at, chunk), :] += (1.0 - fy) * s
                    acc[p, tile, pl.ds(top + at + 1, chunk), :] += fy * s

    @pl.loop(0, rows // span)
    def _(i):
        at = pl.multiple_of(i * span, span)
        for k in range(acc.shape[1]):
            grad_ref[:, pl.ds(at, span), pl.ds(k * LANES, LANES)] = acc[:, k, pl.ds(at, span), :]

    @pl.loop(0, size // span)
    def _(i):
        at = pl.multiple_of(i * span, span)
        for k in range(acc.shape[1]):
            below_ref[:, pl.ds(at, span), pl.ds(k * LANES, LANES)] = acc[
                :, k, pl.ds(rows + at, span), :
            ].astype(bf16)


def shards(object_tiles, probe, measured, offset_row, offset_col, subpixel, live_count):
    f32, bf16 = jnp.float32, jnp.bfloat16
    rows, _, width = object_tiles.shape
    modes, size = probe.shape[:2]
    slots = measured.shape[0]
    own = jnp.transpose(object_tiles, (1, 0, 2))
    rim = passed_along(own[:, :size], "row", -1)
    probe_planes = jnp.transpose(probe, (0, 2, 1, 3))
    cosine, sine = dft_tables(size)
    vmem = pl.BlockSpec(memory_space=pltpu.VMEM)
    smem = pl.BlockSpec(memory_space=pltpu.SMEM)
    hbm = pl.BlockSpec(memory_space=pl.ANY)
    grad, below, probe_sum, moved = pl.pallas_call(
        functools.partial(step_kernel, modes, size, rows),
        out_shape=(
            jax.ShapeDtypeStruct((2, rows, width), f32),
            jax.ShapeDtypeStruct((2, size, width), bf16),
            jax.ShapeDtypeStruct((modes, 2, size, size), f32),
            jax.ShapeDtypeStruct((2, slots), f32),
        ),
        in_specs=[smem] * 4 + [hbm] * 2 + [vmem] * 4,
        out_specs=(vmem, vmem, vmem, smem),
        scratch_shapes=[
            pltpu.VMEM((2, rows + size, width), bf16),
            pltpu.VMEM((2, size // LANES + 1, size + ROWS, LANES), f32),
            pltpu.VMEM((2, width // LANES, rows + size, LANES), f32),
            pltpu.VMEM((2 * size, 2 * size), bf16),
            pltpu.VMEM((2 * size, 2 * size), bf16),
            pltpu.VMEM((2, size, size), f32),
            pltpu.VMEM((2, 2, size, size), f32),
            pltpu.VMEM((modes, 2 * size, size), f32),
            pltpu.VMEM((size, size), f32),
            pltpu.VMEM((2, size, size), f32),
            pltpu.SemaphoreType.DMA((2,)),
        ],
        compiler_params=pltpu.CompilerParams(vmem_limit_bytes=60 << 20),
        name="step",
    )(live_count, offset_row, offset_col, subpixel, own, rim, probe_planes, measured, cosine, sine)
    landed = passed_along(below, "row", 1)
    probe_grad = jnp.transpose(summed(probe_sum, "row"), (0, 2, 1, 3))
    grad = grad.at[:, :size].add(landed.astype(f32))
    return (jnp.transpose(grad, (1, 0, 2)), probe_grad, moved)


def solution(mesh):
    in_specs = (
        P(("groups", "row"), None, None),
        P(),
        P(("groups", "row"), None, None),
        P(("groups", "row")),
        P(("groups", "row")),
        P(("groups", "row")),
        P(("groups", "row")),
    )
    out_specs = (
        P(("groups", "row"), None, None),
        P("groups", None, None, None),
        P(None, ("groups", "row")),
    )
    return jax.shard_map(shards, mesh=mesh, in_specs=in_specs, out_specs=out_specs, check_vma=False)
```

```python
import functools
import math

import jax
import jax.numpy as jnp
import numpy as np
from jax import lax
from jax.experimental import pallas as pl
from jax.experimental.pallas import tpu as pltpu
from jax.sharding import PartitionSpec as P

LANES = 128
ROWS = 16


def passed_along(x, axis, by):
    length = lax.axis_size(axis)
    pairs = [(i, i + by) for i in range(length) if 0 <= i + by < length]
    return lax.ppermute(x, axis, pairs)


def total_kernel(length, pieces, x_ref, out_ref, near, send1, send2, got0, got1, got2, full, sends, recvs):
    f32, bf16 = jnp.float32, jnp.bfloat16
    lines, width = x_ref.shape
    deep = length // 4
    me = lax.axis_index("row")
    c, b, k = me % 2, (me // 2) % 2, me // 4
    part = lines // pieces
    half, quarter = part // 2, part // 4
    leaf = quarter // deep

    def peer(stage, o):
        if stage in (0, 5):
            return {"row": me + 1 - 2 * c}
        if stage in (1, 4):
            return {"row": me + 2 - 4 * b}
        return {"row": ((k + o) % deep) * 4 + me % 4}

    barrier = pltpu.get_barrier_semaphore()
    others = [(0, 0), (1, 0)] + [(2, o) for o in range(1, deep)]
    for stage, o in others:
        pl.semaphore_signal(barrier, inc=1, device_id=peer(stage, o), device_id_type=pl.DeviceIdType.MESH)
    pl.semaphore_wait(barrier, len(others))

    base = [0, pieces, 2 * pieces, (2 + deep) * pieces, (2 + 2 * deep) * pieces, (3 + 2 * deep) * pieces]

    def rows(start, size):
        return pl.ds(pl.multiple_of(start, ROWS), size)

    def place(q, stage):
        start = q * part
        if stage == 0:
            return start
        start = start + c * half
        if stage == 1:
            return start
        start = start + b * quarter
        return start if stage == 2 else start + k * leaf

    def link(stage, q, o=0):
        at = rows(q * quarter, quarter)
        if stage == 0:
            src, dst = near.at[rows(q * half, half)], got0.at[rows(q * half, half)]
        elif stage == 1:
            src, dst = send1.at[at], got1.at[at]
        elif stage == 2:
            src = send2.at[rows(q * quarter + ((k + o) % deep) * leaf, leaf)]
            dst = got2.at[rows((q * deep + o) * leaf, leaf)]
        elif stage == 3:
            src = dst = full.at[rows(place(q, 3), leaf)]
        elif stage == 4:
            src = dst = full.at[rows(place(q, 2), quarter)]
        else:
            src = dst = full.at[rows(place(q, 1), half)]
        sem = base[stage] + (q * deep + o if stage in (2, 3) else q)
        return pltpu.make_async_remote_copy(
            src_ref=src, dst_ref=dst, send_sem=sends.at[sem], recv_sem=recvs.at[sem],
            device_id=peer(stage, o), device_id_type=pl.DeviceIdType.MESH,
        )

    started = []

    def begin(stage, q):
        for o in range(1, deep) if stage in (2, 3) else (0,):
            copy = link(stage, q, o)
            copy.start()
            started.append(copy)

    def arrive(stage, q):
        for o in range(1, deep) if stage in (2, 3) else (0,):
            link(stage, q, o).wait_recv()

    def act(stage, q):
        if stage == 0:
            near[rows(q * half, half)] = x_ref[rows(q * part + (1 - c) * half, half)].astype(bf16)
        elif stage == 1:
            arrive(0, q)
            away = q * part + c * half + (1 - b) * quarter
            send1[rows(q * quarter, quarter)] = (
                x_ref[rows(away, quarter)] + got0[rows(q * half + (1 - b) * quarter, quarter)].astype(f32)
            ).astype(bf16)
        elif stage == 2:
            arrive(1, q)
            own = (
                x_ref[rows(place(q, 2), quarter)]
                + got0[rows(q * half + b * quarter, quarter)].astype(f32)
                + got1[rows(q * quarter, quarter)].astype(f32)
            )
            send2[rows(q * quarter, quarter)] = own.astype(bf16)
        elif stage == 3:
            arrive(2, q)
            own = (
                x_ref[rows(place(q, 3), leaf)]
                + got0[rows(q * half + b * quarter + k * leaf, leaf)].astype(f32)
                + got1[rows(q * quarter + k * leaf, leaf)].astype(f32)
            )
            for o in range(1, deep):
                own = own + got2[rows((q * deep + o) * leaf, leaf)].astype(f32)
            full[rows(place(q, 3), leaf)] = own.astype(bf16)
        elif stage == 6:
            arrive(5, q)
            at = rows(q * part, part)
            out_ref[at] = full[at].astype(f32)
            return
        else:
            arrive(stage - 1, q)
        begin(stage, q)

    for q in range(pieces):
        act(0, q)
    for t in range(pieces + 6):
        for stage in range(6, 0, -1):
            q = t - stage
            if 0 <= q < pieces:
                act(stage, q)
    for copy in started:
        copy.wait_send()


def summed(x, axis):
    length = lax.axis_size(axis)
    lines = x.size // x.shape[-1]
    if length % 4 or lines % (length * ROWS):
        return lax.psum(x, axis)
    f32, bf16 = jnp.float32, jnp.bfloat16
    width = x.shape[-1]
    pieces = 4 if lines % (length * ROWS * 4) == 0 else 1
    flat = x.reshape(lines, width)
    vmem = pl.BlockSpec(memory_space=pltpu.VMEM)
    count = pieces * (4 + 2 * (length // 4))
    out = pl.pallas_call(
        functools.partial(total_kernel, length, pieces),
        out_shape=jax.ShapeDtypeStruct((lines, width), f32),
        in_specs=[vmem],
        out_specs=vmem,
        scratch_shapes=[
            pltpu.VMEM((lines // 2, width), bf16),
            pltpu.VMEM((lines // 4, width), bf16),
            pltpu.VMEM((lines // 4, width), bf16),
            pltpu.VMEM((lines // 2, width), bf16),
            pltpu.VMEM((lines // 4, width), bf16),
            pltpu.VMEM((lines // 4, width), bf16),
            pltpu.VMEM((lines, width), bf16),
            pltpu.SemaphoreType.DMA((count,)),
            pltpu.SemaphoreType.DMA((count,)),
        ],
        compiler_params=pltpu.CompilerParams(collective_id=0, has_side_effects=True, vmem_limit_bytes=32 << 20),
        name="total",
    )(flat)
    return out.reshape(x.shape)


def dft_tables(patch):
    index = np.arange(patch)
    angle = ((index[:, None] * index[None, :]) % patch).astype(np.float64) * (2.0 * math.pi / patch)
    scale = 1.0 / math.sqrt(patch)
    cosine, sine = np.cos(angle) * scale, np.sin(angle) * scale
    half = patch // 2
    tables = []
    for odd in range(2):
        c, s = cosine[:half, odd::2], sine[:half, odd::2]
        tables.append(np.block([[c, -s], [s, c]]))
        tables.append(np.block([[c.T, s.T], [-s.T, c.T]]))
    order = np.concatenate([index[0::2], index[1::2]])
    tables.append((index[:, None] == order[None, :]).astype(np.float64))
    stacked = np.stack(tables).astype(np.float32)
    return jnp.asarray(stacked).astype(jnp.bfloat16)


def pulled(x, by, tiles):
    lane = lax.broadcasted_iota(jnp.int32, x[0].shape, 1)
    back = lax.rem(LANES - by, LANES)
    parts = [pltpu.roll(x[k], back, 1) for k in range(tiles + 1)]
    keep = lane < LANES - by
    return [jnp.where(keep, parts[k], parts[k + 1]) for k in range(tiles)]


def pushed(x, by, tiles):
    lane = lax.broadcasted_iota(jnp.int32, x[0].shape, 1)
    ahead = lax.rem(by, LANES)
    parts = [pltpu.roll(x[k], ahead, 1) for k in range(tiles)]
    zero = jnp.zeros_like(parts[0])
    keep = lane >= by
    left = [zero] + parts
    right = parts + [zero]
    return [jnp.where(keep, right[k], left[k]) for k in range(tiles + 1)]


def step_kernel(
    modes, size, rows, lines,
    count_ref, top_ref, left_ref, code_ref,
    own_hbm, rim_hbm, probe_hbm, measured_ref, table_ref,
    grad_hbm, below_ref, pgrad_ref, moved_ref,
    stage, ext, acc, probe_raw, probe, pgrad, rowx, slope, patch, waves, mids, far, power, meas, gs, sems, out_sem,
):
    f32, bf16 = jnp.float32, jnp.bfloat16
    tiles = size // LANES
    half = size // 2
    slots = measured_ref.shape[0]
    step = 2 * lines
    span = 32
    cut = 24
    along, inverse_of = (0, 2), (1, 3)
    copies = [
        pltpu.make_async_copy(probe_hbm, probe_raw, sems.at[0]),
        pltpu.make_async_copy(own_hbm, stage.at[pl.ds(0, rows * step)], sems.at[1]),
        pltpu.make_async_copy(rim_hbm, stage.at[pl.ds(rows * step, size * step)], sems.at[2]),
    ]
    for copy in copies:
        copy.start()
    pgrad[...] = jnp.zeros_like(pgrad)
    gs[...] = jnp.zeros_like(gs)

    @pl.loop(0, acc.shape[0] // 256)
    def _(i):
        acc[pl.ds(pl.multiple_of(i * 256, 256), 256), :] = jnp.zeros((256, LANES), f32)

    for j in range(slots):
        moved_ref[0, j] = 0.0
        moved_ref[1, j] = 0.0
    tail = ext.shape[0] - stage.shape[0]
    ext[pl.ds(stage.shape[0], tail), :] = jnp.zeros((tail, LANES), f32)
    copies[0].wait()

    @pl.loop(0, modes * (size // span))
    def _(i):
        at = pl.multiple_of(lax.rem(i, size // span) * span, span)
        m = i // (size // span)
        for p in range(2):
            for k in range(tiles):
                probe[m, p, pl.ds(at, span), k * LANES : (k + 1) * LANES] = probe_raw[
                    pl.ds((i * span * tiles + k) * 2 + p, span, stride=2 * tiles), :
                ]

    copies[1].wait()
    copies[2].wait()

    @pl.loop(0, stage.shape[0] // 256)
    def _(i):
        at = pl.ds(pl.multiple_of(i * 256, 256), 256)
        ext[at, :] = stage[at, :].astype(f32)

    @pl.loop(0, count_ref[0])
    def _(j):
        top, left, code = top_ref[j], left_ref[j], code_ref[j]
        first = left // LANES
        col = left - first * LANES
        fy = (code // 4).astype(f32) * 0.25
        fx = (code % 4).astype(f32) * 0.25

        @pl.loop(0, rowx.shape[1] // cut)
        def _(i):
            at = pl.multiple_of(i * cut, 8)
            for p in range(2):
                w = [
                    ext[pl.ds(((top + at) * lines + first + k) * 2 + p, cut, stride=step), :]
                    for k in range(tiles + 1)
                ]
                w0, w1 = pulled(w, col, tiles), pulled(w, col + 1, tiles)
                for k in range(tiles):
                    d = w1[k] - w0[k]
                    rowx[p, pl.ds(at, cut), k * LANES : (k + 1) * LANES] = w0[k] + fx * d
                    slope[p, pl.ds(at, cut), k * LANES : (k + 1) * LANES] = d

        for p in range(2):
            for i in range(size // span):
                upper = rowx[p, i * span : (i + 1) * span, :]
                lower = rowx[p, i * span + 1 : (i + 1) * span + 1, :]
                patch[p, i * span : (i + 1) * span, :] = upper + fy * (lower - upper)

        ordered = jnp.dot(measured_ref[j], table_ref[4], preferred_element_type=f32)
        for k in range(tiles):
            meas[k] = ordered[:, k * LANES : (k + 1) * LANES]

        for m in range(modes):
            for i in range(size // span):
                at = slice(i * span, (i + 1) * span)
                pr, pi = probe[m, 0, at, :], probe[m, 1, at, :]
                re, im = patch[0, at, :], patch[1, at, :]
                for q, w in enumerate((pr * re - pi * im, pr * im + pi * re)):
                    to = slice(q * half, (q + 1) * half)
                    waves[m % 2, 0, at, to] = (w[:, :half] + w[:, half:]).astype(bf16)
                    waves[m % 2, 1, at, to] = (w[:, :half] - w[:, half:]).astype(bf16)
            for e in range(2):
                h = jnp.dot(waves[m % 2, e], table_ref[along[e]], preferred_element_type=f32)
                to = slice(e * half, (e + 1) * half)
                for q in range(2):
                    upper = h[:half, q * half : (q + 1) * half]
                    lower = h[half:, q * half : (q + 1) * half]
                    mids[m % 2, 0, q * half : (q + 1) * half, to] = (upper + lower).astype(bf16)
                    mids[m % 2, 1, q * half : (q + 1) * half, to] = (upper - lower).astype(bf16)
            for e in range(2):
                f = jnp.dot(table_ref[inverse_of[e]], mids[m % 2, e], preferred_element_type=f32)
                far[m, e] = f
                strength = f[:half] * f[:half] + f[half:] * f[half:]
                if m == 0:
                    power[e] = strength
                else:
                    power[e] += strength

        for e in range(2):
            for k in range(tiles):
                to = slice(k * LANES, (k + 1) * LANES)
                amplitude = meas[k, pl.ds(e, half, stride=2), :]
                power[e, :, to] = 1.0 - amplitude * jnp.minimum(lax.rsqrt(power[e, :, to]), 2.0)

        for m in range(modes):
            parts = []
            for e in range(2):
                ratio = power[e]
                mids[m % 2, e, 0:half, :] = (far[m, e, 0:half, :] * ratio).astype(bf16)
                mids[m % 2, e, half:size, :] = (far[m, e, half:size, :] * ratio).astype(bf16)
                parts.append(jnp.dot(table_ref[along[e]], mids[m % 2, e], preferred_element_type=f32))
            upper, lower = parts[0] + parts[1], parts[0] - parts[1]
            for e in range(2):
                for q in range(2):
                    to, at = slice(q * half, (q + 1) * half), slice(e * half, (e + 1) * half)
                    waves[m % 2, e, 0:half, to] = upper[to, at].astype(bf16)
                    waves[m % 2, e, half:size, to] = lower[to, at].astype(bf16)
            back = [
                jnp.dot(waves[m % 2, e], table_ref[inverse_of[e]], preferred_element_type=f32) for e in range(2)
            ]
            for i in range(size // span):
                at = slice(i * span, (i + 1) * span)
                there = pl.ds(8 + i * span, span)
                b0, b1 = back[0][at], back[1][at]
                for k in range(2):
                    to = slice(k * half, (k + 1) * half)
                    mixed = b0 + b1 if k == 0 else b0 - b1
                    ur, ui = mixed[:, :half], mixed[:, half:]
                    pr, pi = probe[m, 0, at, to], probe[m, 1, at, to]
                    re, im = patch[0, at, to], patch[1, at, to]
                    g0, g1 = pr * ur + pi * ui, pr * ui - pi * ur
                    if m == 0:
                        gs[0, k, there, :] = g0
                        gs[1, k, there, :] = g1
                    else:
                        gs[0, k, there, :] += g0
                        gs[1, k, there, :] += g1
                    pgrad[m, 0, at, to] += re * ur + im * ui
                    pgrad[m, 1, at, to] += re * ui - im * ur

        down, across = jnp.zeros((8, LANES), f32), jnp.zeros((8, LANES), f32)
        for i in range(size // span):
            for p in range(2):
                for k in range(tiles):
                    at, after = slice(i * span, (i + 1) * span), slice(i * span + 1, (i + 1) * span + 1)
                    to = slice(k * LANES, (k + 1) * LANES)
                    g = gs[p, k, 8 + i * span : 8 + (i + 1) * span, :]
                    dy = g * (rowx[p, after, to] - rowx[p, at, to])
                    upper = slope[p, at, to]
                    dx = g * (upper + fy * (slope[p, after, to] - upper))
                    down = down + jnp.sum(dy.reshape(span // 8, 8, LANES), 0)
                    across = across + jnp.sum(dx.reshape(span // 8, 8, LANES), 0)
        moved_ref[0, j] = jnp.sum(down) / size
        moved_ref[1, j] = jnp.sum(across) / size

        @pl.loop(0, rowx.shape[1] // cut)
        def _(i):
            at = pl.multiple_of(i * cut, 8)
            for p in range(2):
                g = []
                for k in range(tiles):
                    here = gs[p, k, pl.ds(at + 8, cut), :]
                    before = gs[p, k, pl.ds(at + 7, cut), :]
                    g.append(here + fy * (before - here))
                s0, s1 = pushed(g, col, tiles), pushed(g, col + 1, tiles)
                for k in range(tiles + 1):
                    to = pl.ds(((top + at) * lines + first + k) * 2 + p, cut, stride=step)
                    acc[to, :] += s0[k] + fx * (s1[k] - s0[k])

    out = pltpu.make_async_copy(acc.at[pl.ds(0, rows * step)], grad_hbm, out_sem.at[0])
    out.start()

    @pl.loop(0, below_ref.shape[0] // 256)
    def _(i):
        at = pl.multiple_of(i * 256, 256)
        below_ref[pl.ds(at, 256), :] = acc[pl.ds(rows * step + at, 256), :].astype(bf16)

    @pl.loop(0, modes * (size // span))
    def _(i):
        at = pl.multiple_of(lax.rem(i, size // span) * span, span)
        m = i // (size // span)
        for p in range(2):
            for k in range(tiles):
                pgrad_ref[pl.ds((i * span * tiles + k) * 2 + p, span, stride=2 * tiles), :] = pgrad[
                    m, p, pl.ds(at, span), k * LANES : (k + 1) * LANES
                ]

    out.wait()


def tiled(x):
    *lead, two, width = x.shape
    n = math.prod(lead)
    x = x.reshape(n, two, width // LANES, LANES)
    return jnp.transpose(x, (0, 2, 1, 3)).reshape(-1, LANES)


def untiled(x, lead, width):
    n = math.prod(lead)
    x = jnp.transpose(x.reshape(n, width // LANES, 2, LANES), (0, 2, 1, 3))
    return x.reshape(*lead, 2, width)


def shards(object_tiles, probe, measured, offset_row, offset_col, subpixel, live_count):
    f32, bf16 = jnp.float32, jnp.bfloat16
    rows, _, width = object_tiles.shape
    modes, size = probe.shape[:2]
    slots = measured.shape[0]
    lines = width // LANES
    own = tiled(object_tiles)
    rim = tiled(passed_along(object_tiles[:size], "row", -1))
    vmem = pl.BlockSpec(memory_space=pltpu.VMEM)
    smem = pl.BlockSpec(memory_space=pltpu.SMEM)
    hbm = pl.BlockSpec(memory_space=pl.ANY)
    high = rows + size + 8
    grad, below, probe_sum, moved = pl.pallas_call(
        functools.partial(step_kernel, modes, size, rows, lines),
        out_shape=(
            jax.ShapeDtypeStruct((rows * lines * 2, LANES), f32),
            jax.ShapeDtypeStruct((size * lines * 2, LANES), bf16),
            jax.ShapeDtypeStruct((modes * size * size * 2 // LANES, LANES), f32),
            jax.ShapeDtypeStruct((2, slots), f32),
        ),
        in_specs=[smem] * 4 + [hbm] * 3 + [vmem] * 2,
        out_specs=(hbm, vmem, vmem, smem),
        scratch_shapes=[
            pltpu.VMEM(((rows + size) * lines * 2, LANES), bf16),
            pltpu.VMEM((high * lines * 2, LANES), f32),
            pltpu.VMEM((high * lines * 2, LANES), f32),
            pltpu.VMEM((modes * size * size * 2 // LANES, LANES), f32),
            pltpu.VMEM((modes, 2, size, size), f32),
            pltpu.VMEM((modes, 2, size, size), f32),
            pltpu.VMEM((2, size + 8, size), f32),
            pltpu.VMEM((2, size + 8, size), f32),
            pltpu.VMEM((2, size, size), f32),
            pltpu.VMEM((2, 2, size, size), bf16),
            pltpu.VMEM((2, 2, size, size), bf16),
            pltpu.VMEM((modes, 2, size, size), f32),
            pltpu.VMEM((2, size // 2, size), f32),
            pltpu.VMEM((size // LANES, size, LANES), f32),
            pltpu.VMEM((2, size // LANES, size + 16, LANES), f32),
            pltpu.SemaphoreType.DMA((3,)),
            pltpu.SemaphoreType.DMA((1,)),
        ],
        compiler_params=pltpu.CompilerParams(vmem_limit_bytes=60 << 20),
        name="step",
    )(live_count, offset_row, offset_col, subpixel, own, rim, tiled(probe), measured, dft_tables(size))
    landed = passed_along(below, "row", 1)
    probe_grad = untiled(summed(probe_sum, "row"), (modes, size), size)
    grad = grad.at[: landed.shape[0]].add(landed.astype(f32))
    return (untiled(grad, (rows,), width), probe_grad, moved)


def solution(mesh):
    in_specs = (
        P(("groups", "row"), None, None),
        P(),
        P(("groups", "row"), None, None),
        P(("groups", "row")),
        P(("groups", "row")),
        P(("groups", "row")),
        P(("groups", "row")),
    )
    out_specs = (
        P(("groups", "row"), None, None),
        P("groups", None, None, None),
        P(None, ("groups", "row")),
    )
    return jax.shard_map(shards, mesh=mesh, in_specs=in_specs, out_specs=out_specs, check_vma=False)
```

```python
import functools
import math

import jax
import jax.numpy as jnp
import numpy as np
from jax import lax
from jax.experimental import pallas as pl
from jax.experimental.pallas import tpu as pltpu
from jax.sharding import PartitionSpec as P

LANES = 128
ROWS = 16


def passed_along(x, axis, by):
    length = lax.axis_size(axis)
    pairs = [(i, i + by) for i in range(length) if 0 <= i + by < length]
    return lax.ppermute(x, axis, pairs)


def total_kernel(
    length, pieces, modes, tiles, x_ref, below_hbm, out_ref, landed_hbm,
    near, send1, send2, got0, got1, got2, full, blank, sends, recvs, down_sems,
):
    f32, bf16 = jnp.float32, jnp.bfloat16
    lines, width = x_ref.shape
    deep = length // 4
    me = lax.axis_index("row")
    c, b, k = me % 2, (me // 2) % 2, me // 4
    part = lines // pieces
    half, quarter = part // 2, part // 4
    leaf = quarter // deep

    def stage_near(q):
        near[pl.ds(q * half, half)] = x_ref[
            pl.ds(pl.multiple_of(q * part + (1 - c) * half, ROWS), half)
        ].astype(bf16)

    def peer(stage, o):
        if stage in (0, 5):
            return {"row": me + 1 - 2 * c}
        if stage in (1, 4):
            return {"row": me + 2 - 4 * b}
        return {"row": ((k + o) % deep) * 4 + me % 4}

    barrier = pltpu.get_barrier_semaphore()
    others = [(0, 0), (1, 0)] + [(2, o) for o in range(1, deep)]
    for stage, o in others:
        pl.semaphore_signal(barrier, inc=1, device_id=peer(stage, o), device_id_type=pl.DeviceIdType.MESH)

    @pl.when(me > 0)
    def _():
        pl.semaphore_signal(barrier, inc=1, device_id={"row": me - 1}, device_id_type=pl.DeviceIdType.MESH)

    @pl.when(me < length - 1)
    def _():
        pl.semaphore_signal(barrier, inc=1, device_id={"row": me + 1}, device_id_type=pl.DeviceIdType.MESH)

    blank[...] = jnp.zeros_like(blank)
    for q in range(pieces):
        stage_near(q)
    pl.semaphore_wait(
        barrier, len(others) + (me > 0).astype(jnp.int32) + (me < length - 1).astype(jnp.int32)
    )
    down = pltpu.make_async_remote_copy(
        src_ref=below_hbm, dst_ref=landed_hbm, send_sem=down_sems.at[0], recv_sem=down_sems.at[1],
        device_id={"row": jnp.minimum(me + 1, length - 1)}, device_id_type=pl.DeviceIdType.MESH,
    )
    fill = pltpu.make_async_copy(blank, landed_hbm, down_sems.at[2])

    base = [0, pieces, 2 * pieces, (2 + deep) * pieces, (2 + 2 * deep) * pieces, (3 + 2 * deep) * pieces]

    def rows(start, size):
        return pl.ds(pl.multiple_of(start, ROWS), size)

    def place(q, stage):
        start = q * part
        if stage == 0:
            return start
        start = start + c * half
        if stage == 1:
            return start
        start = start + b * quarter
        return start if stage == 2 else start + k * leaf

    def link(stage, q, o=0):
        at = rows(q * quarter, quarter)
        if stage == 0:
            src, dst = near.at[rows(q * half, half)], got0.at[rows(q * half, half)]
        elif stage == 1:
            src, dst = send1.at[at], got1.at[at]
        elif stage == 2:
            src = send2.at[rows(q * quarter + ((k + o) % deep) * leaf, leaf)]
            dst = got2.at[rows((q * deep + o) * leaf, leaf)]
        elif stage == 3:
            src = dst = full.at[rows(place(q, 3), leaf)]
        elif stage == 4:
            src = dst = full.at[rows(place(q, 2), quarter)]
        else:
            src = dst = full.at[rows(place(q, 1), half)]
        sem = base[stage] + (q * deep + o if stage in (2, 3) else q)
        return pltpu.make_async_remote_copy(
            src_ref=src, dst_ref=dst, send_sem=sends.at[sem], recv_sem=recvs.at[sem],
            device_id=peer(stage, o), device_id_type=pl.DeviceIdType.MESH,
        )

    started = []

    def begin(stage, q):
        for o in range(1, deep) if stage in (2, 3) else (0,):
            copy = link(stage, q, o)
            copy.start()
            started.append(copy)

    def arrive(stage, q):
        for o in range(1, deep) if stage in (2, 3) else (0,):
            link(stage, q, o).wait_recv()

    def act(stage, q):
        if stage == 0:
            pass
        elif stage == 1:
            arrive(0, q)
            away = q * part + c * half + (1 - b) * quarter
            send1[rows(q * quarter, quarter)] = (
                x_ref[rows(away, quarter)] + got0[rows(q * half + (1 - b) * quarter, quarter)].astype(f32)
            ).astype(bf16)
        elif stage == 2:
            arrive(1, q)
            own = (
                x_ref[rows(place(q, 2), quarter)]
                + got0[rows(q * half + b * quarter, quarter)].astype(f32)
                + got1[rows(q * quarter, quarter)].astype(f32)
            )
            send2[rows(q * quarter, quarter)] = own.astype(bf16)
        elif stage == 3:
            arrive(2, q)
            own = (
                x_ref[rows(place(q, 3), leaf)]
                + got0[rows(q * half + b * quarter + k * leaf, leaf)].astype(f32)
                + got1[rows(q * quarter + k * leaf, leaf)].astype(f32)
            )
            for o in range(1, deep):
                own = own + got2[rows((q * deep + o) * leaf, leaf)].astype(f32)
            full[rows(place(q, 3), leaf)] = own.astype(bf16)
        elif stage == 6:
            arrive(5, q)
            planes = modes * 2 * tiles
            size = lines // planes
            for plane in range(planes * q // pieces, planes * (q + 1) // pieces):
                m, p, tile = plane // (2 * tiles), plane // tiles % 2, plane % tiles
                out_ref[pl.ds((m * size * tiles + tile) * 2 + p, size, stride=2 * tiles), :] = full[
                    pl.ds(plane * size, size), :
                ].astype(f32)
            return
        else:
            arrive(stage - 1, q)
        begin(stage, q)

    for q in range(pieces):
        act(0, q)
    for t in range(pieces + 6):
        for stage in range(6, 0, -1):
            q = t - stage
            if 0 <= q < pieces:
                act(stage, q)
                if stage == 1 and q == pieces - 1:

                    @pl.when(me < length - 1)
                    def _():
                        down.start()

                    @pl.when(me == 0)
                    def _():
                        fill.start()

    for copy in started:
        copy.wait_send()

    @pl.when(me < length - 1)
    def _():
        down.wait_send()

    @pl.when(me > 0)
    def _():
        down.wait_recv()

    @pl.when(me == 0)
    def _():
        fill.wait()


def summed(x, below, modes, tiles, axis):
    length = lax.axis_size(axis)
    lines, width = x.shape
    f32, bf16 = jnp.float32, jnp.bfloat16
    pieces = 2 if lines % (length * ROWS * 2) == 0 else 1
    vmem = pl.BlockSpec(memory_space=pltpu.VMEM)
    hbm = pl.BlockSpec(memory_space=pl.ANY)
    count = pieces * (4 + 2 * (length // 4))
    return pl.pallas_call(
        functools.partial(total_kernel, length, pieces, modes, tiles),
        out_shape=(
            jax.ShapeDtypeStruct((lines, width), f32),
            jax.ShapeDtypeStruct(below.shape, bf16),
        ),
        in_specs=[vmem, hbm],
        out_specs=(vmem, hbm),
        scratch_shapes=[
            pltpu.VMEM((lines // 2, width), bf16),
            pltpu.VMEM((lines // 4, width), bf16),
            pltpu.VMEM((lines // 4, width), bf16),
            pltpu.VMEM((lines // 2, width), bf16),
            pltpu.VMEM((lines // 4, width), bf16),
            pltpu.VMEM((lines // 4, width), bf16),
            pltpu.VMEM((lines, width), bf16),
            pltpu.VMEM(below.shape, bf16),
            pltpu.SemaphoreType.DMA((count,)),
            pltpu.SemaphoreType.DMA((count,)),
            pltpu.SemaphoreType.DMA((3,)),
        ],
        compiler_params=pltpu.CompilerParams(collective_id=0, has_side_effects=True, vmem_limit_bytes=32 << 20),
        name="total",
    )(x, below)


def dft_tables(patch):
    index = np.arange(patch)
    angle = ((index[:, None] * index[None, :]) % patch).astype(np.float64) * (2.0 * math.pi / patch)
    scale = 1.0 / math.sqrt(patch)
    cosine, sine = np.cos(angle) * scale, np.sin(angle) * scale
    half = patch // 2
    tables = []
    for odd in range(2):
        c, s = cosine[:half, odd::2], sine[:half, odd::2]
        tables.append(np.block([[c, -s], [s, c]]))
        tables.append(np.block([[c.T, s.T], [-s.T, c.T]]))
    order = np.concatenate([index[0::2], index[1::2]])
    tables.append((index[:, None] == order[None, :]).astype(np.float64))
    stacked = np.stack(tables).astype(np.float32)
    return jnp.asarray(stacked).astype(jnp.bfloat16)


def step_kernel(
    modes, size, rows, first_tile, low, high, keep, own_parts, rim_parts, carried, *refs
):
    f32, bf16 = jnp.float32, jnp.bfloat16
    refs = list(refs)

    def take(n):
        got, refs[:] = refs[:n], refs[n:]
        return got

    count_ref, top_ref, left_ref, code_ref = take(4)
    probe_hbm, measured_hbm, table_hbm = take(3)
    owns, rims = take(len(own_parts)), take(len(rim_parts))
    if carried:
        handed_hbm, sum_hbm, before_ref = take(3)
    grad_hbm, below_ref, pgrad_hbm, moved_ref = take(4)
    over_hbm = None if carried else take(1)[0]
    (ext, acc, probe, measured_ref, table_ref, pgrad, rowx, slope, patch, waves, mids, far, power, meas, gs,
     sems, out_sems) = refs
    tiles = size // LANES
    half = size // 2
    slots = measured_ref.shape[0]
    span = 32
    along, inverse_of = (0, 2), (1, 3)
    copies = []

    def fetch(src, dst):
        copy = pltpu.make_async_copy(src, dst, sems.at[len(copies)])
        copy.start()
        copies.append(copy)

    for sources, ranges, row, n in ((owns, own_parts, 0, rows), (rims, rim_parts, rows, size)):
        for source, (start, stop, to) in zip(sources, ranges):
            fetch(
                source.at[pl.ds(start, stop - start)],
                ext.at[pl.ds(to, stop - start), :, pl.ds(row, n), :],
            )
    fetch(probe_hbm, probe)
    fetch(measured_hbm, measured_ref)
    fetch(table_hbm, table_ref)
    overlap = 0
    if carried:
        overlap = handed_hbm.shape[0]
        fetch(handed_hbm, acc.at[pl.ds(0, overlap)])
        fetch(sum_hbm, pgrad)
    else:
        pgrad[...] = jnp.zeros_like(pgrad)
    gs[...] = jnp.zeros_like(gs)

    @pl.loop(overlap, acc.shape[0])
    def _(k):
        for p in range(2):
            acc[k, p] = jnp.zeros(acc.shape[2:], f32)

    for j in range(slots):
        for p in range(2):
            moved_ref[p, j] = before_ref[p, j] if carried else 0.0
    for copy in copies:
        copy.wait()

    def one(j):
        top, left, code = top_ref[j], left_ref[j], code_ref[j]
        first = left // LANES
        col = left - first * LANES
        first = first - first_tile
        base_row = pl.multiple_of(top // ROWS * ROWS, ROWS)
        row = top - base_row
        fy = (code // 4).astype(f32) * 0.25
        fx = (code % 4).astype(f32) * 0.25
        reach = (tiles + 1) * LANES
        tall = size + ROWS
        here = lax.broadcasted_iota(jnp.int32, (reach, size), 0)
        away = here - lax.broadcasted_iota(jnp.int32, (reach, size), 1) - col
        at_left, at_right = (away == 0).astype(f32), (away == 1).astype(f32)
        mix = ((1.0 - fx) * at_left + fx * at_right).astype(bf16)
        tilt = (at_right - at_left).astype(bf16)
        for p in range(2):
            window = jnp.concatenate(
                [ext[first + k, p, pl.ds(base_row, tall), :] for k in range(tiles + 1)], axis=1
            )
            for table, kept in ((mix, rowx), (tilt, slope)):
                cells = jnp.dot(window, table, preferred_element_type=f32)
                for k in range(tiles):
                    kept[p, k, 0:tall, :] = cells[:, k * LANES : (k + 1) * LANES]
        for p in range(2):
            for k in range(tiles):
                for i in range(size // span):
                    upper = rowx[p, k, pl.ds(row + i * span, span), :]
                    lower = rowx[p, k, pl.ds(row + i * span + 1, span), :]
                    patch[p, i * span : (i + 1) * span, k * LANES : (k + 1) * LANES] = upper + fy * (lower - upper)

        ordered = jnp.dot(measured_ref[j], table_ref[4], preferred_element_type=f32)
        for k in range(tiles):
            meas[k] = ordered[:, k * LANES : (k + 1) * LANES]

        def wave(m):
            for i in range(size // span):
                at = slice(i * span, (i + 1) * span)
                pr, pi = probe[m, 0, at, :], probe[m, 1, at, :]
                re, im = patch[0, at, :], patch[1, at, :]
                for q, w in enumerate((pr * re - pi * im, pr * im + pi * re)):
                    to = slice(q * half, (q + 1) * half)
                    waves[m, 0, at, to] = (w[:, :half] + w[:, half:]).astype(bf16)
                    waves[m, 1, at, to] = (w[:, :half] - w[:, half:]).astype(bf16)

        def along_columns(m):
            for e in range(2):
                h = jnp.dot(waves[m, e], table_ref[along[e]], preferred_element_type=f32)
                to = slice(e * half, (e + 1) * half)
                for q in range(2):
                    upper = h[:half, q * half : (q + 1) * half]
                    lower = h[half:, q * half : (q + 1) * half]
                    mids[m, 0, q * half : (q + 1) * half, to] = (upper + lower).astype(bf16)
                    mids[m, 1, q * half : (q + 1) * half, to] = (upper - lower).astype(bf16)

        def along_rows(m):
            for e in range(2):
                f = jnp.dot(table_ref[inverse_of[e]], mids[m, e], preferred_element_type=f32)
                far[m, e] = f
                strength = f[:half] * f[:half] + f[half:] * f[half:]
                if m == 0:
                    power[e] = strength
                else:
                    power[e] += strength

        def skewed(*stages):
            for t in range(modes + len(stages) - 1):
                for n in reversed(range(len(stages))):
                    if 0 <= t - n < modes:
                        stages[n](t - n)

        skewed(wave, along_columns, along_rows)

        for e in range(2):
            for k in range(tiles):
                to = slice(k * LANES, (k + 1) * LANES)
                amplitude = meas[k, pl.ds(e, half, stride=2), :]
                power[e, :, to] = 1.0 - amplitude * jnp.minimum(lax.rsqrt(power[e, :, to]), 2.0)

        def error(m):
            for e in range(2):
                ratio = power[e]
                mids[m, e, 0:half, :] = (far[m, e, 0:half, :] * ratio).astype(bf16)
                mids[m, e, half:size, :] = (far[m, e, half:size, :] * ratio).astype(bf16)

        def back_rows(m):
            parts = [jnp.dot(table_ref[along[e]], mids[m, e], preferred_element_type=f32) for e in range(2)]
            upper, lower = parts[0] + parts[1], parts[0] - parts[1]
            for e in range(2):
                for q in range(2):
                    to, at = slice(q * half, (q + 1) * half), slice(e * half, (e + 1) * half)
                    waves[m, e, 0:half, to] = upper[to, at].astype(bf16)
                    waves[m, e, half:size, to] = lower[to, at].astype(bf16)

        def back_columns(m):
            back = [jnp.dot(waves[m, e], table_ref[inverse_of[e]], preferred_element_type=f32) for e in range(2)]
            for i in range(size // span):
                at = slice(i * span, (i + 1) * span)
                there = pl.ds(8 + i * span, span)
                b0, b1 = back[0][at], back[1][at]
                for k in range(2):
                    to = slice(k * half, (k + 1) * half)
                    mixed = b0 + b1 if k == 0 else b0 - b1
                    ur, ui = mixed[:, :half], mixed[:, half:]
                    pr, pi = probe[m, 0, at, to], probe[m, 1, at, to]
                    re, im = patch[0, at, to], patch[1, at, to]
                    g0, g1 = pr * ur + pi * ui, pr * ui - pi * ur
                    if m == 0:
                        gs[0, k, there, :] = g0
                        gs[1, k, there, :] = g1
                    else:
                        gs[0, k, there, :] += g0
                        gs[1, k, there, :] += g1
                    pgrad[m, 0, k, at, :] += re * ur + im * ui
                    pgrad[m, 1, k, at, :] += re * ui - im * ur

        skewed(error, back_rows, back_columns)

        down, across = jnp.zeros((8, LANES), f32), jnp.zeros((8, LANES), f32)
        for i in range(size // span):
            for p in range(2):
                for k in range(tiles):
                    at, after = pl.ds(row + i * span, span), pl.ds(row + i * span + 1, span)
                    g = gs[p, k, 8 + i * span : 8 + (i + 1) * span, :]
                    dy = g * (rowx[p, k, after, :] - rowx[p, k, at, :])
                    upper = slope[p, k, at, :]
                    dx = g * (upper + fy * (slope[p, k, after, :] - upper))
                    down = down + jnp.sum(dy.reshape(span // 8, 8, LANES), 0)
                    across = across + jnp.sum(dx.reshape(span // 8, 8, LANES), 0)
        moved_ref[0, j] = jnp.sum(down) / size
        moved_ref[1, j] = jnp.sum(across) / size

        base = pl.multiple_of(top // 8 * 8, 8)
        lag = top - base

        there = lax.broadcasted_iota(jnp.int32, (size, reach), 1)
        gone = there - lax.broadcasted_iota(jnp.int32, (size, reach), 0) - col
        spread = ((1.0 - fx) * (gone == 0).astype(f32) + fx * (gone == 1).astype(f32)).astype(bf16)
        for p in range(2):
            g = []
            for k in range(tiles):
                here = gs[p, k, pl.ds(8 - lag, tall), :]
                before = gs[p, k, pl.ds(7 - lag, tall), :]
                g.append((here + fy * (before - here)).astype(bf16))
            wide = jnp.dot(jnp.concatenate(g, axis=1), spread, preferred_element_type=f32)
            for k in range(tiles + 1):
                acc[first + k, p, pl.ds(base, tall), :] += wide[:, k * LANES : (k + 1) * LANES]

    @pl.loop(0, count_ref[0])
    def _(j):
        tile = left_ref[j] // LANES

        @pl.when((tile >= low) & (tile < high))
        def _():
            one(j)

    outs = [
        pltpu.make_async_copy(acc.at[pl.ds(0, keep), :, pl.ds(0, rows), :], grad_hbm, out_sems.at[0]),
        pltpu.make_async_copy(pgrad, pgrad_hbm, out_sems.at[1]),
    ]
    if not carried:
        outs.append(pltpu.make_async_copy(acc.at[pl.ds(keep, over_hbm.shape[0])], over_hbm, out_sems.at[2]))
    for out in outs:
        out.start()

    @pl.loop(0, keep)
    def _(k):
        for p in range(2):
            below_ref[k, p] = acc[k, p, rows : rows + size, :].astype(bf16)

    for out in outs:
        out.wait()


def step(modes, size, rows, slots, first_tile, low, high, keep, count, own, rim, carried, common):
    f32, bf16 = jnp.float32, jnp.bfloat16
    tiles = size // LANES
    deep = rows + size + 8
    vmem = pl.BlockSpec(memory_space=pltpu.VMEM)
    smem = pl.BlockSpec(memory_space=pltpu.SMEM)
    hbm = pl.BlockSpec(memory_space=pl.ANY)
    planes = (modes, 2, tiles, size, LANES)
    out_shape = [
        jax.ShapeDtypeStruct((keep, 2, rows, LANES), f32),
        jax.ShapeDtypeStruct((keep, 2, size, LANES), bf16),
        jax.ShapeDtypeStruct(planes, f32),
        jax.ShapeDtypeStruct((2, slots), f32),
    ]
    out_specs = [hbm, vmem, hbm, smem]
    if not carried:
        out_shape.append(jax.ShapeDtypeStruct((count - keep, 2, deep, LANES), f32))
        out_specs.append(hbm)
    own_arrays, own_parts = zip(*own)
    rim_arrays, rim_parts = zip(*rim)
    return pl.pallas_call(
        functools.partial(
            step_kernel, modes, size, rows, first_tile, low, high, keep, own_parts, rim_parts, bool(carried)
        ),
        out_shape=tuple(out_shape),
        in_specs=[smem] * 4 + [hbm] * (3 + len(own) + len(rim)) + ([hbm, hbm, smem] if carried else []),
        out_specs=tuple(out_specs),
        scratch_shapes=[
            pltpu.VMEM((count, 2, rows + size, LANES), bf16),
            pltpu.VMEM((count, 2, deep, LANES), f32),
            pltpu.VMEM((modes, 2, size, size), f32),
            pltpu.VMEM((slots, size, size), bf16),
            pltpu.VMEM((5, size, size), bf16),
            pltpu.VMEM(planes, f32),
            pltpu.VMEM((2, tiles, size + 32, LANES), f32),
            pltpu.VMEM((2, tiles, size + 32, LANES), f32),
            pltpu.VMEM((2, size, size), f32),
            pltpu.VMEM((modes, 2, size, size), bf16),
            pltpu.VMEM((modes, 2, size, size), bf16),
            pltpu.VMEM((modes, 2, size, size), f32),
            pltpu.VMEM((2, size // 2, size), f32),
            pltpu.VMEM((tiles, size, LANES), f32),
            pltpu.VMEM((2, tiles, size + 32, LANES), f32),
            pltpu.SemaphoreType.DMA((12,)),
            pltpu.SemaphoreType.DMA((3,)),
        ],
        compiler_params=pltpu.CompilerParams(vmem_limit_bytes=48 << 20),
        cost_estimate=pl.CostEstimate(flops=3 << 30, bytes_accessed=16 << 20, transcendentals=0),
        name="step_b" if carried else "step_a",
    )(*common, *own_arrays, *rim_arrays, *carried)


def sort_kernel(lines, x_ref, near_ref, rest_ref, temp):
    n = near_ref.shape[2]
    line = 2 * lines
    for y in range(n):
        temp[y * (line + 1) : y * (line + 1) + line, :] = x_ref[y * line : (y + 1) * line, :].astype(jnp.float32)
    for k in range(lines):
        for p in range(2):
            plane = temp[pl.ds(2 * k + p, n, stride=line + 1), :].astype(jnp.bfloat16)
            if k < near_ref.shape[0]:
                near_ref[k, p] = plane
            else:
                rest_ref[k - near_ref.shape[0], p] = plane


def sorted_planes(x, rows, lines, near):
    n = 64
    return pl.pallas_call(
        functools.partial(sort_kernel, lines),
        grid=(rows // n,),
        out_shape=tuple(
            jax.ShapeDtypeStruct((t, 2, rows, LANES), jnp.bfloat16) for t in (near, lines - near)
        ),
        in_specs=[pl.BlockSpec((n * lines * 2, LANES), lambda i: (i, 0))],
        out_specs=tuple(
            pl.BlockSpec((t, 2, n, LANES), lambda i: (0, 0, i, 0)) for t in (near, lines - near)
        ),
        scratch_shapes=[pltpu.VMEM((n * (lines * 2 + 1) + 7, LANES), jnp.float32)],
        cost_estimate=pl.CostEstimate(flops=1 << 20, bytes_accessed=4 << 20, transcendentals=0),
        name="sort",
    )(x)


def probe_kernel(tiles, x_ref, out_ref):
    size = out_ref.shape[2]
    for p in range(2):
        for k in range(tiles):
            out_ref[0, p, :, k * LANES : (k + 1) * LANES] = x_ref[pl.ds(2 * k + p, size, stride=2 * tiles), :]


def probe_planes(x, modes, size):
    tiles = size // LANES
    return pl.pallas_call(
        functools.partial(probe_kernel, tiles),
        grid=(modes,),
        out_shape=jax.ShapeDtypeStruct((modes, 2, size, size), jnp.float32),
        in_specs=[pl.BlockSpec((size * tiles * 2, LANES), lambda m: (m, 0))],
        out_specs=pl.BlockSpec((1, 2, size, size), lambda m: (m, 0, 0, 0)),
        cost_estimate=pl.CostEstimate(flops=1 << 20, bytes_accessed=4 << 20, transcendentals=0),
        name="probes",
    )(x)


def merge_kernel(lines, *refs):
    *parts, out_ref, temp = refs
    n = parts[0].shape[2]
    line = 2 * lines
    base = 0
    for grad, landed in (parts[:2], parts[2:]):
        for k in range(grad.shape[0]):
            for p in range(2):
                temp[pl.ds(2 * (base + k) + p, n, stride=line + 1), :] = (
                    grad[k, p] + landed[k, p].astype(jnp.float32)
                )
        base += grad.shape[0]
    for y in range(n):
        out_ref[y * line : (y + 1) * line, :] = temp[y * (line + 1) : y * (line + 1) + line, :]


def merged(pairs, rows, lines):
    n = 64
    specs, arrays = [], []
    for grad, landed in pairs:
        if landed.shape[2] < rows:
            landed = jnp.pad(landed, ((0, 0), (0, 0), (0, rows - landed.shape[2]), (0, 0)))
        for x in (grad, landed):
            arrays.append(x)
            specs.append(pl.BlockSpec((x.shape[0], 2, n, LANES), lambda i: (0, 0, i, 0)))
    return pl.pallas_call(
        functools.partial(merge_kernel, lines),
        grid=(rows // n,),
        out_shape=jax.ShapeDtypeStruct((rows * lines * 2, LANES), jnp.float32),
        in_specs=specs,
        out_specs=pl.BlockSpec((n * lines * 2, LANES), lambda i: (i, 0)),
        scratch_shapes=[pltpu.VMEM((n * (lines * 2 + 1) + 7, LANES), jnp.float32)],
        name="merge",
    )(*arrays)


def tiled(x):
    *lead, two, width = x.shape
    n = math.prod(lead)
    x = x.reshape(n, two, width // LANES, LANES)
    return jnp.transpose(x, (0, 2, 1, 3)).reshape(-1, LANES)


def untiled(x, lead, width):
    n = math.prod(lead)
    x = jnp.transpose(x.reshape(n, width // LANES, 2, LANES), (0, 2, 1, 3))
    return x.reshape(*lead, 2, width)


def shards(object_tiles, probe, measured, offset_row, offset_col, subpixel, live_count):
    rows, _, width = object_tiles.shape
    modes, size = probe.shape[:2]
    slots = measured.shape[0]
    lines, tiles = width // LANES, size // LANES
    mid = lines // 2
    near = mid + tiles
    own_a, own_b = sorted_planes(tiled(object_tiles), rows, lines, near)
    rim_a = passed_along(own_a[:, :, :size], "row", -1)
    rim_b = passed_along(own_b[:, :, :size], "row", -1)
    planes = probe_planes(tiled(probe), modes, size)
    common = (live_count, offset_row, offset_col, subpixel, planes, measured, dft_tables(size))
    whole = (0, near, 0)
    grad_a, below_a, sum_a, moved_a, over = step(
        modes, size, rows, slots, 0, 0, mid, mid, near, [(own_a, whole)], [(rim_a, whole)], (), common
    )
    landed_a = passed_along(below_a, "row", 1)
    kept, rest = (mid, near, 0), (0, lines - near, tiles)
    grad_b, below_b, sums, moved = step(
        modes, size, rows, slots, mid, mid, lines, lines - mid, lines - mid,
        [(own_a, kept), (own_b, rest)], [(rim_a, kept), (rim_b, rest)], (over, sum_a, moved_a), common,
    )
    probe_grad, landed_b = summed(sums.reshape(-1, LANES), below_b, modes, tiles, "row")
    grad = merged([(grad_a, landed_a), (grad_b, landed_b)], rows, lines)
    return (untiled(grad, (rows,), width), untiled(probe_grad, (modes, size), size), moved)


def solution(mesh):
    in_specs = (
        P(("groups", "row"), None, None),
        P(),
        P(("groups", "row"), None, None),
        P(("groups", "row")),
        P(("groups", "row")),
        P(("groups", "row")),
        P(("groups", "row")),
    )
    out_specs = (
        P(("groups", "row"), None, None),
        P("groups", None, None, None),
        P(None, ("groups", "row")),
    )
    return jax.shard_map(shards, mesh=mesh, in_specs=in_specs, out_specs=out_specs, check_vma=False)
```

```python
import functools
import math

import jax
import jax.numpy as jnp
import numpy as np
from jax import lax
from jax.experimental import pallas as pl
from jax.experimental.pallas import tpu as pltpu
from jax.sharding import PartitionSpec as P

LANES = 128
ROWS = 16


def passed_along(x, axis, by):
    length = lax.axis_size(axis)
    pairs = [(i, i + by) for i in range(length) if 0 <= i + by < length]
    return lax.ppermute(x, axis, pairs)


def total_kernel(
    length, pieces, modes, tiles, x_ref, below_hbm, out_ref, landed_hbm,
    near, send1, send2, got0, got1, got2, full, blank, sends, recvs, down_sems,
):
    f32, bf16 = jnp.float32, jnp.bfloat16
    lines, width = x_ref.shape
    deep = length // 4
    me = lax.axis_index("row")
    c, b, k = me % 2, (me // 2) % 2, me // 4
    part = lines // pieces
    half, quarter = part // 2, part // 4
    leaf = quarter // deep

    def stage_near(q):
        near[pl.ds(q * half, half)] = x_ref[
            pl.ds(pl.multiple_of(q * part + (1 - c) * half, ROWS), half)
        ].astype(bf16)

    def peer(stage, o):
        if stage in (0, 5):
            return {"row": me + 1 - 2 * c}
        if stage in (1, 4):
            return {"row": me + 2 - 4 * b}
        return {"row": ((k + o) % deep) * 4 + me % 4}

    barrier = pltpu.get_barrier_semaphore()
    others = [(0, 0), (1, 0)] + [(2, o) for o in range(1, deep)]
    for stage, o in others:
        pl.semaphore_signal(barrier, inc=1, device_id=peer(stage, o), device_id_type=pl.DeviceIdType.MESH)

    @pl.when(me > 0)
    def _():
        pl.semaphore_signal(barrier, inc=1, device_id={"row": me - 1}, device_id_type=pl.DeviceIdType.MESH)

    @pl.when(me < length - 1)
    def _():
        pl.semaphore_signal(barrier, inc=1, device_id={"row": me + 1}, device_id_type=pl.DeviceIdType.MESH)

    blank[...] = jnp.zeros_like(blank)
    for q in range(pieces):
        stage_near(q)
    pl.semaphore_wait(
        barrier, len(others) + (me > 0).astype(jnp.int32) + (me < length - 1).astype(jnp.int32)
    )
    down = pltpu.make_async_remote_copy(
        src_ref=below_hbm, dst_ref=landed_hbm, send_sem=down_sems.at[0], recv_sem=down_sems.at[1],
        device_id={"row": jnp.minimum(me + 1, length - 1)}, device_id_type=pl.DeviceIdType.MESH,
    )
    fill = pltpu.make_async_copy(blank, landed_hbm, down_sems.at[2])

    base = [0, pieces, 2 * pieces, (2 + deep) * pieces, (2 + 2 * deep) * pieces, (3 + 2 * deep) * pieces]

    def rows(start, size):
        return pl.ds(pl.multiple_of(start, ROWS), size)

    def place(q, stage):
        start = q * part
        if stage == 0:
            return start
        start = start + c * half
        if stage == 1:
            return start
        start = start + b * quarter
        return start if stage == 2 else start + k * leaf

    def link(stage, q, o=0):
        at = rows(q * quarter, quarter)
        if stage == 0:
            src, dst = near.at[rows(q * half, half)], got0.at[rows(q * half, half)]
        elif stage == 1:
            src, dst = send1.at[at], got1.at[at]
        elif stage == 2:
            src = send2.at[rows(q * quarter + ((k + o) % deep) * leaf, leaf)]
            dst = got2.at[rows((q * deep + o) * leaf, leaf)]
        elif stage == 3:
            src = dst = full.at[rows(place(q, 3), leaf)]
        elif stage == 4:
            src = dst = full.at[rows(place(q, 2), quarter)]
        else:
            src = dst = full.at[rows(place(q, 1), half)]
        sem = base[stage] + (q * deep + o if stage in (2, 3) else q)
        return pltpu.make_async_remote_copy(
            src_ref=src, dst_ref=dst, send_sem=sends.at[sem], recv_sem=recvs.at[sem],
            device_id=peer(stage, o), device_id_type=pl.DeviceIdType.MESH,
        )

    started = []

    def begin(stage, q):
        for o in range(1, deep) if stage in (2, 3) else (0,):
            copy = link(stage, q, o)
            copy.start()
            started.append(copy)

    def arrive(stage, q):
        for o in range(1, deep) if stage in (2, 3) else (0,):
            link(stage, q, o).wait_recv()

    def act(stage, q):
        if stage == 0:
            pass
        elif stage == 1:
            arrive(0, q)
            away = q * part + c * half + (1 - b) * quarter
            send1[rows(q * quarter, quarter)] = (
                x_ref[rows(away, quarter)] + got0[rows(q * half + (1 - b) * quarter, quarter)].astype(f32)
            ).astype(bf16)
        elif stage == 2:
            arrive(1, q)
            own = (
                x_ref[rows(place(q, 2), quarter)]
                + got0[rows(q * half + b * quarter, quarter)].astype(f32)
                + got1[rows(q * quarter, quarter)].astype(f32)
            )
            send2[rows(q * quarter, quarter)] = own.astype(bf16)
        elif stage == 3:
            arrive(2, q)
            own = (
                x_ref[rows(place(q, 3), leaf)]
                + got0[rows(q * half + b * quarter + k * leaf, leaf)].astype(f32)
                + got1[rows(q * quarter + k * leaf, leaf)].astype(f32)
            )
            for o in range(1, deep):
                own = own + got2[rows((q * deep + o) * leaf, leaf)].astype(f32)
            full[rows(place(q, 3), leaf)] = own.astype(bf16)
        elif stage == 6:
            arrive(5, q)
            planes = modes * 2 * tiles
            size = lines // planes
            for plane in range(planes * q // pieces, planes * (q + 1) // pieces):
                m, p, tile = plane // (2 * tiles), plane // tiles % 2, plane % tiles
                out_ref[pl.ds((m * size * tiles + tile) * 2 + p, size, stride=2 * tiles), :] = full[
                    pl.ds(plane * size, size), :
                ].astype(f32)
            return
        else:
            arrive(stage - 1, q)
        begin(stage, q)

    for q in range(pieces):
        act(0, q)
    for t in range(pieces + 6):
        for stage in range(6, 0, -1):
            q = t - stage
            if 0 <= q < pieces:
                act(stage, q)
                if stage == 1 and q == pieces - 1:

                    @pl.when(me < length - 1)
                    def _():
                        down.start()

                    @pl.when(me == 0)
                    def _():
                        fill.start()

    for copy in started:
        copy.wait_send()

    @pl.when(me < length - 1)
    def _():
        down.wait_send()

    @pl.when(me > 0)
    def _():
        down.wait_recv()

    @pl.when(me == 0)
    def _():
        fill.wait()


def summed(x, below, modes, tiles, axis):
    length = lax.axis_size(axis)
    lines, width = x.shape
    f32, bf16 = jnp.float32, jnp.bfloat16
    pieces = 2 if lines % (length * ROWS * 2) == 0 else 1
    vmem = pl.BlockSpec(memory_space=pltpu.VMEM)
    hbm = pl.BlockSpec(memory_space=pl.ANY)
    count = pieces * (4 + 2 * (length // 4))
    return pl.pallas_call(
        functools.partial(total_kernel, length, pieces, modes, tiles),
        out_shape=(
            jax.ShapeDtypeStruct((lines, width), f32),
            jax.ShapeDtypeStruct(below.shape, bf16),
        ),
        in_specs=[vmem, hbm],
        out_specs=(vmem, hbm),
        scratch_shapes=[
            pltpu.VMEM((lines // 2, width), bf16),
            pltpu.VMEM((lines // 4, width), bf16),
            pltpu.VMEM((lines // 4, width), bf16),
            pltpu.VMEM((lines // 2, width), bf16),
            pltpu.VMEM((lines // 4, width), bf16),
            pltpu.VMEM((lines // 4, width), bf16),
            pltpu.VMEM((lines, width), bf16),
            pltpu.VMEM(below.shape, bf16),
            pltpu.SemaphoreType.DMA((count,)),
            pltpu.SemaphoreType.DMA((count,)),
            pltpu.SemaphoreType.DMA((3,)),
        ],
        compiler_params=pltpu.CompilerParams(collective_id=0, has_side_effects=True, vmem_limit_bytes=32 << 20),
        name="total",
    )(x, below)


def dft_tables(patch):
    index = np.arange(patch)
    angle = ((index[:, None] * index[None, :]) % patch).astype(np.float64) * (2.0 * math.pi / patch)
    scale = 1.0 / math.sqrt(patch)
    cosine, sine = np.cos(angle) * scale, np.sin(angle) * scale
    half = patch // 2
    tables = []
    for odd in range(2):
        c, s = cosine[:half, odd::2], sine[:half, odd::2]
        tables.append(np.block([[c, -s], [s, c]]))
        tables.append(np.block([[c.T, s.T], [-s.T, c.T]]))
    order = np.concatenate([index[0::2], index[1::2]])
    tables.append((index[:, None] == order[None, :]).astype(np.float64))
    stacked = np.stack(tables).astype(np.float32)
    return jnp.asarray(stacked).astype(jnp.bfloat16)


def step_kernel(
    modes, size, rows, first_tile, low, high, keep, own_parts, rim_parts, carried, *refs
):
    f32, bf16 = jnp.float32, jnp.bfloat16
    refs = list(refs)

    def take(n):
        got, refs[:] = refs[:n], refs[n:]
        return got

    count_ref, top_ref, left_ref, code_ref = take(4)
    probe_hbm, measured_hbm, table_hbm = take(3)
    owns, rims = take(len(own_parts)), take(len(rim_parts))
    if carried:
        handed_hbm, sum_hbm, before_ref = take(3)
    grad_hbm, below_ref, pgrad_hbm, moved_ref = take(4)
    over_hbm = None if carried else take(1)[0]
    (ext, acc, probe, measured_ref, table_ref, pgrad, rowx, slope, patch, waves, mids, far, power, ratios, meas, gs,
     sems, out_sems) = refs
    tiles = size // LANES
    half = size // 2
    slots = measured_ref.shape[0]
    span = 32
    along, inverse_of = (0, 2), (1, 3)
    copies = []

    def fetch(src, dst):
        copy = pltpu.make_async_copy(src, dst, sems.at[len(copies)])
        copy.start()
        copies.append(copy)

    for sources, ranges, row, n in ((owns, own_parts, 0, rows), (rims, rim_parts, rows, size)):
        for source, (start, stop, to) in zip(sources, ranges):
            fetch(
                source.at[pl.ds(start, stop - start)],
                ext.at[pl.ds(to, stop - start), :, pl.ds(row, n), :],
            )
    fetch(probe_hbm, probe)
    fetch(measured_hbm, measured_ref)
    fetch(table_hbm, table_ref)
    overlap = 0
    if carried:
        overlap = handed_hbm.shape[0]
        fetch(handed_hbm, acc.at[pl.ds(0, overlap)])
        fetch(sum_hbm, pgrad)
    else:
        pgrad[...] = jnp.zeros_like(pgrad)
    gs[...] = jnp.zeros_like(gs)

    @pl.loop(overlap, acc.shape[0])
    def _(k):
        for p in range(2):
            acc[k, p] = jnp.zeros(acc.shape[2:], f32)

    for j in range(slots):
        for p in range(2):
            moved_ref[p, j] = before_ref[p, j] if carried else 0.0
    for copy in copies:
        copy.wait()

    def one(j):
        top, left, code = top_ref[j], left_ref[j], code_ref[j]
        first = left // LANES
        col = left - first * LANES
        first = first - first_tile
        base_row = pl.multiple_of(top // ROWS * ROWS, ROWS)
        row = top - base_row
        fy = (code // 4).astype(f32) * 0.25
        fx = (code % 4).astype(f32) * 0.25
        reach = (tiles + 1) * LANES
        tall = size + ROWS
        here = lax.broadcasted_iota(jnp.int32, (reach, size), 0)
        away = here - lax.broadcasted_iota(jnp.int32, (reach, size), 1) - col
        at_left, at_right = (away == 0).astype(f32), (away == 1).astype(f32)
        mix = ((1.0 - fx) * at_left + fx * at_right).astype(bf16)
        tilt = (at_right - at_left).astype(bf16)
        for p in range(2):
            window = jnp.concatenate(
                [ext[first + k, p, pl.ds(base_row, tall), :] for k in range(tiles + 1)], axis=1
            )
            for table, kept in ((mix, rowx), (tilt, slope)):
                cells = jnp.dot(window, table, preferred_element_type=f32)
                for k in range(tiles):
                    kept[p, k, 0:tall, :] = cells[:, k * LANES : (k + 1) * LANES]
        for p in range(2):
            for k in range(tiles):
                for i in range(size // span):
                    upper = rowx[p, k, pl.ds(row + i * span, span), :]
                    lower = rowx[p, k, pl.ds(row + i * span + 1, span), :]
                    patch[p, i * span : (i + 1) * span, k * LANES : (k + 1) * LANES] = upper + fy * (lower - upper)

        ordered = jnp.dot(measured_ref[j], table_ref[4], preferred_element_type=f32)
        for k in range(tiles):
            meas[k] = ordered[:, k * LANES : (k + 1) * LANES]

        share = size // modes
        short = share // 2

        def wave(c):
            for h in range(2):
                at = slice(h * half + c * short, h * half + (c + 1) * short)
                re, im = patch[0, at, :], patch[1, at, :]
                for m in range(modes):
                    here = slice(m * share + h * short, m * share + (h + 1) * short)
                    pr, pi = probe[m, 0, at, :], probe[m, 1, at, :]
                    for q, w in enumerate((pr * re - pi * im, pr * im + pi * re)):
                        to = slice(q * half, (q + 1) * half)
                        waves[0, c, here, to] = (w[:, :half] + w[:, half:]).astype(bf16)
                        waves[1, c, here, to] = (w[:, :half] - w[:, half:]).astype(bf16)

        def along_columns(c):
            for e in range(2):
                h = jnp.dot(waves[e, c], table_ref[along[e]], preferred_element_type=f32)
                to = slice(e * half, (e + 1) * half)
                for m in range(modes):
                    for q in range(2):
                        upper = h[m * share : m * share + short, q * half : (q + 1) * half]
                        lower = h[m * share + short : (m + 1) * share, q * half : (q + 1) * half]
                        at = slice(q * half + c * short, q * half + (c + 1) * short)
                        mids[m, 0, at, to] = (upper + lower).astype(bf16)
                        mids[m, 1, at, to] = (upper - lower).astype(bf16)

        def along_rows(m):
            for e in range(2):
                f = jnp.dot(table_ref[inverse_of[e]], mids[m, e], preferred_element_type=f32)
                far[m, e] = f.astype(far.dtype)
                strength = f[:half] * f[:half] + f[half:] * f[half:]
                if m == 0:
                    power[e] = strength
                else:
                    power[e] += strength

        def skewed(*stages):
            for t in range(modes + len(stages) - 1):
                for n in reversed(range(len(stages))):
                    if 0 <= t - n < modes:
                        stages[n](t - n)

        skewed(wave, along_columns)
        skewed(along_rows)

        for e in range(2):
            for k in range(tiles):
                to = slice(k * LANES, (k + 1) * LANES)
                amplitude = meas[k, pl.ds(e, half, stride=2), :]
                ratio = 1.0 - amplitude * jnp.minimum(lax.rsqrt(power[e, :, to]), 2.0)
                ratios[e, :, to] = ratio.astype(bf16)

        def error(m):
            for e in range(2):
                ratio = ratios[e]
                mids[m, e, 0:half, :] = far[m, e, 0:half, :] * ratio
                mids[m, e, half:size, :] = far[m, e, half:size, :] * ratio

        def back_rows(m):
            parts = [jnp.dot(table_ref[along[e]], mids[m, e], preferred_element_type=f32) for e in range(2)]
            for h, both in enumerate((parts[0] + parts[1], parts[0] - parts[1])):
                for e in range(2):
                    for q in range(2):
                        to, at = slice(q * half, (q + 1) * half), slice(e * half, (e + 1) * half)
                        for n in range(half // share):
                            waves[e, h * (half // share) + n, m * share : (m + 1) * share, to] = both[
                                q * half + n * share : q * half + (n + 1) * share, at
                            ].astype(bf16)

        def back_columns(c):
            back = [jnp.dot(waves[e, c], table_ref[inverse_of[e]], preferred_element_type=f32) for e in range(2)]
            for i in range(share // span):
                start = c * share + i * span
                at = slice(start, start + span)
                for k in range(2):
                    to = slice(k * half, (k + 1) * half)
                    re, im = patch[0, at, to], patch[1, at, to]
                    sums = [0.0, 0.0]
                    for m in range(modes):
                        here = slice(m * share + i * span, m * share + (i + 1) * span)
                        b0, b1 = back[0][here], back[1][here]
                        mixed = b0 + b1 if k == 0 else b0 - b1
                        ur, ui = mixed[:, :half], mixed[:, half:]
                        pr, pi = probe[m, 0, at, to], probe[m, 1, at, to]
                        sums[0] = sums[0] + (pr * ur + pi * ui)
                        sums[1] = sums[1] + (pr * ui - pi * ur)
                        pgrad[m, 0, k, at, :] += re * ur + im * ui
                        pgrad[m, 1, k, at, :] += re * ui - im * ur
                    for p in range(2):
                        gs[p, k, 8 + start : 8 + start + span, :] = sums[p]

        skewed(error, back_rows)
        skewed(back_columns)

        down, across = jnp.zeros((8, LANES), f32), jnp.zeros((8, LANES), f32)
        for i in range(size // span):
            for p in range(2):
                for k in range(tiles):
                    at, after = pl.ds(row + i * span, span), pl.ds(row + i * span + 1, span)
                    g = gs[p, k, 8 + i * span : 8 + (i + 1) * span, :]
                    dy = g * (rowx[p, k, after, :] - rowx[p, k, at, :])
                    upper = slope[p, k, at, :]
                    dx = g * (upper + fy * (slope[p, k, after, :] - upper))
                    down = down + jnp.sum(dy.reshape(span // 8, 8, LANES), 0)
                    across = across + jnp.sum(dx.reshape(span // 8, 8, LANES), 0)
        moved_ref[0, j] = jnp.sum(down) / size
        moved_ref[1, j] = jnp.sum(across) / size

        base = pl.multiple_of(top // 8 * 8, 8)
        lag = top - base

        there = lax.broadcasted_iota(jnp.int32, (size, reach), 1)
        gone = there - lax.broadcasted_iota(jnp.int32, (size, reach), 0) - col
        spread = ((1.0 - fx) * (gone == 0).astype(f32) + fx * (gone == 1).astype(f32)).astype(bf16)
        for p in range(2):
            g = []
            for k in range(tiles):
                here = gs[p, k, pl.ds(8 - lag, tall), :]
                before = gs[p, k, pl.ds(7 - lag, tall), :]
                g.append((here + fy * (before - here)).astype(bf16))
            wide = jnp.dot(jnp.concatenate(g, axis=1), spread, preferred_element_type=f32)
            for k in range(tiles + 1):
                acc[first + k, p, pl.ds(base, tall), :] += wide[:, k * LANES : (k + 1) * LANES]

    @pl.loop(0, count_ref[0])
    def _(j):
        tile = left_ref[j] // LANES

        @pl.when((tile >= low) & (tile < high))
        def _():
            one(j)

    outs = [
        pltpu.make_async_copy(acc.at[pl.ds(0, keep), :, pl.ds(0, rows), :], grad_hbm, out_sems.at[0]),
        pltpu.make_async_copy(pgrad, pgrad_hbm, out_sems.at[1]),
    ]
    if not carried:
        outs.append(pltpu.make_async_copy(acc.at[pl.ds(keep, over_hbm.shape[0])], over_hbm, out_sems.at[2]))
    for out in outs:
        out.start()

    @pl.loop(0, keep)
    def _(k):
        for p in range(2):
            below_ref[k, p] = acc[k, p, rows : rows + size, :].astype(bf16)

    for out in outs:
        out.wait()


def step(modes, size, rows, slots, first_tile, low, high, keep, count, own, rim, carried, common):
    f32, bf16 = jnp.float32, jnp.bfloat16
    tiles = size // LANES
    deep = rows + size + 8
    vmem = pl.BlockSpec(memory_space=pltpu.VMEM)
    smem = pl.BlockSpec(memory_space=pltpu.SMEM)
    hbm = pl.BlockSpec(memory_space=pl.ANY)
    planes = (modes, 2, tiles, size, LANES)
    out_shape = [
        jax.ShapeDtypeStruct((keep, 2, rows, LANES), f32),
        jax.ShapeDtypeStruct((keep, 2, size, LANES), bf16),
        jax.ShapeDtypeStruct(planes, f32),
        jax.ShapeDtypeStruct((2, slots), f32),
    ]
    out_specs = [hbm, vmem, hbm, smem]
    if not carried:
        out_shape.append(jax.ShapeDtypeStruct((count - keep, 2, deep, LANES), f32))
        out_specs.append(hbm)
    own_arrays, own_parts = zip(*own)
    rim_arrays, rim_parts = zip(*rim)
    return pl.pallas_call(
        functools.partial(
            step_kernel, modes, size, rows, first_tile, low, high, keep, own_parts, rim_parts, bool(carried)
        ),
        out_shape=tuple(out_shape),
        in_specs=[smem] * 4 + [hbm] * (3 + len(own) + len(rim)) + ([hbm, hbm, smem] if carried else []),
        out_specs=tuple(out_specs),
        scratch_shapes=[
            pltpu.VMEM((count, 2, rows + size, LANES), bf16),
            pltpu.VMEM((count, 2, deep, LANES), f32),
            pltpu.VMEM((modes, 2, size, size), f32),
            pltpu.VMEM((slots, size, size), bf16),
            pltpu.VMEM((5, size, size), bf16),
            pltpu.VMEM(planes, f32),
            pltpu.VMEM((2, tiles, size + 32, LANES), f32),
            pltpu.VMEM((2, tiles, size + 32, LANES), f32),
            pltpu.VMEM((2, size, size), f32),
            pltpu.VMEM((2, modes, size, size), bf16),
            pltpu.VMEM((modes, 2, size, size), bf16),
            pltpu.VMEM((modes, 2, size, size), bf16),
            pltpu.VMEM((2, size // 2, size), f32),
            pltpu.VMEM((2, size // 2, size), bf16),
            pltpu.VMEM((tiles, size, LANES), f32),
            pltpu.VMEM((2, tiles, size + 32, LANES), f32),
            pltpu.SemaphoreType.DMA((12,)),
            pltpu.SemaphoreType.DMA((3,)),
        ],
        compiler_params=pltpu.CompilerParams(vmem_limit_bytes=48 << 20),
        cost_estimate=pl.CostEstimate(flops=3 << 30, bytes_accessed=16 << 20, transcendentals=0),
        name="step_b" if carried else "step_a",
    )(*common, *own_arrays, *rim_arrays, *carried)


def sort_kernel(lines, x_ref, near_ref, rest_ref, temp):
    n = near_ref.shape[2]
    line = 2 * lines
    for y in range(n):
        temp[y * (line + 1) : y * (line + 1) + line, :] = x_ref[y * line : (y + 1) * line, :].astype(jnp.float32)
    for k in range(lines):
        for p in range(2):
            plane = temp[pl.ds(2 * k + p, n, stride=line + 1), :].astype(jnp.bfloat16)
            if k < near_ref.shape[0]:
                near_ref[k, p] = plane
            else:
                rest_ref[k - near_ref.shape[0], p] = plane


def sorted_planes(x, rows, lines, near):
    n = 64
    return pl.pallas_call(
        functools.partial(sort_kernel, lines),
        grid=(rows // n,),
        out_shape=tuple(
            jax.ShapeDtypeStruct((t, 2, rows, LANES), jnp.bfloat16) for t in (near, lines - near)
        ),
        in_specs=[pl.BlockSpec((n * lines * 2, LANES), lambda i: (i, 0))],
        out_specs=tuple(
            pl.BlockSpec((t, 2, n, LANES), lambda i: (0, 0, i, 0)) for t in (near, lines - near)
        ),
        scratch_shapes=[pltpu.VMEM((n * (lines * 2 + 1) + 7, LANES), jnp.float32)],
        cost_estimate=pl.CostEstimate(flops=1 << 20, bytes_accessed=4 << 20, transcendentals=0),
        name="sort",
    )(x)


def probe_kernel(tiles, x_ref, out_ref):
    size = out_ref.shape[2]
    for p in range(2):
        for k in range(tiles):
            out_ref[0, p, :, k * LANES : (k + 1) * LANES] = x_ref[pl.ds(2 * k + p, size, stride=2 * tiles), :]


def probe_planes(x, modes, size):
    tiles = size // LANES
    return pl.pallas_call(
        functools.partial(probe_kernel, tiles),
        grid=(modes,),
        out_shape=jax.ShapeDtypeStruct((modes, 2, size, size), jnp.float32),
        in_specs=[pl.BlockSpec((size * tiles * 2, LANES), lambda m: (m, 0))],
        out_specs=pl.BlockSpec((1, 2, size, size), lambda m: (m, 0, 0, 0)),
        cost_estimate=pl.CostEstimate(flops=1 << 20, bytes_accessed=4 << 20, transcendentals=0),
        name="probes",
    )(x)


def merge_kernel(lines, *refs):
    *parts, out_ref, temp = refs
    n = parts[0].shape[2]
    line = 2 * lines
    base = 0
    for grad, landed in (parts[:2], parts[2:]):
        for k in range(grad.shape[0]):
            for p in range(2):
                temp[pl.ds(2 * (base + k) + p, n, stride=line + 1), :] = (
                    grad[k, p] + landed[k, p].astype(jnp.float32)
                )
        base += grad.shape[0]
    for y in range(n):
        out_ref[y * line : (y + 1) * line, :] = temp[y * (line + 1) : y * (line + 1) + line, :]


def merged(pairs, rows, lines):
    n = 64
    specs, arrays = [], []
    for grad, landed in pairs:
        if landed.shape[2] < rows:
            landed = jnp.pad(landed, ((0, 0), (0, 0), (0, rows - landed.shape[2]), (0, 0)))
        for x in (grad, landed):
            arrays.append(x)
            specs.append(pl.BlockSpec((x.shape[0], 2, n, LANES), lambda i: (0, 0, i, 0)))
    return pl.pallas_call(
        functools.partial(merge_kernel, lines),
        grid=(rows // n,),
        out_shape=jax.ShapeDtypeStruct((rows * lines * 2, LANES), jnp.float32),
        in_specs=specs,
        out_specs=pl.BlockSpec((n * lines * 2, LANES), lambda i: (i, 0)),
        scratch_shapes=[pltpu.VMEM((n * (lines * 2 + 1) + 7, LANES), jnp.float32)],
        name="merge",
    )(*arrays)


def tiled(x):
    *lead, two, width = x.shape
    n = math.prod(lead)
    x = x.reshape(n, two, width // LANES, LANES)
    return jnp.transpose(x, (0, 2, 1, 3)).reshape(-1, LANES)


def untiled(x, lead, width):
    n = math.prod(lead)
    x = jnp.transpose(x.reshape(n, width // LANES, 2, LANES), (0, 2, 1, 3))
    return x.reshape(*lead, 2, width)


def shards(object_tiles, probe, measured, offset_row, offset_col, subpixel, live_count):
    rows, _, width = object_tiles.shape
    modes, size = probe.shape[:2]
    slots = measured.shape[0]
    lines, tiles = width // LANES, size // LANES
    mid = lines // 2
    near = mid + tiles
    own_a, own_b = sorted_planes(tiled(object_tiles), rows, lines, near)
    rim_a = passed_along(own_a[:, :, :size], "row", -1)
    rim_b = passed_along(own_b[:, :, :size], "row", -1)
    planes = probe_planes(tiled(probe), modes, size)
    common = (live_count, offset_row, offset_col, subpixel, planes, measured, dft_tables(size))
    whole = (0, near, 0)
    grad_a, below_a, sum_a, moved_a, over = step(
        modes, size, rows, slots, 0, 0, mid, mid, near, [(own_a, whole)], [(rim_a, whole)], (), common
    )
    landed_a = passed_along(below_a, "row", 1)
    kept, rest = (mid, near, 0), (0, lines - near, tiles)
    grad_b, below_b, sums, moved = step(
        modes, size, rows, slots, mid, mid, lines, lines - mid, lines - mid,
        [(own_a, kept), (own_b, rest)], [(rim_a, kept), (rim_b, rest)], (over, sum_a, moved_a), common,
    )
    probe_grad, landed_b = summed(sums.reshape(-1, LANES), below_b, modes, tiles, "row")
    grad = merged([(grad_a, landed_a), (grad_b, landed_b)], rows, lines)
    return (untiled(grad, (rows,), width), untiled(probe_grad, (modes, size), size), moved)


def solution(mesh):
    in_specs = (
        P(("groups", "row"), None, None),
        P(),
        P(("groups", "row"), None, None),
        P(("groups", "row")),
        P(("groups", "row")),
        P(("groups", "row")),
        P(("groups", "row")),
    )
    out_specs = (
        P(("groups", "row"), None, None),
        P("groups", None, None, None),
        P(None, ("groups", "row")),
    )
    return jax.shard_map(shards, mesh=mesh, in_specs=in_specs, out_specs=out_specs, check_vma=False)
```

```python
import functools
import math

import jax
import jax.numpy as jnp
import numpy as np
from jax import lax
from jax.experimental import pallas as pl
from jax.experimental.pallas import tpu as pltpu
from jax.sharding import PartitionSpec as P

LANES = 128
ROWS = 16


def passed_along(x, axis, by):
    length = lax.axis_size(axis)
    pairs = [(i, i + by) for i in range(length) if 0 <= i + by < length]
    return lax.ppermute(x, axis, pairs)


def total_kernel(
    length, pieces, modes, tiles, x_ref, grad_a, grad_b, landed_a, below_ref, out_ref, grad_ref,
    near, send1, send2, got0, got1, got2, full, part_a, part_b, came_a, came_b, temp, sends, recvs, down_sems, local_sems,
):
    f32, bf16 = jnp.float32, jnp.bfloat16
    lines, width = x_ref.shape
    deep = length // 4
    me = lax.axis_index("row")
    c, b, k = me % 2, (me // 2) % 2, me // 4
    part = lines // pieces
    half, quarter = part // 2, part // 4
    leaf = quarter // deep

    def stage_near(q):
        near[pl.ds(q * half, half)] = x_ref[
            pl.ds(pl.multiple_of(q * part + (1 - c) * half, ROWS), half)
        ].astype(bf16)

    def peer(stage, o):
        if stage in (0, 5):
            return {"row": me + 1 - 2 * c}
        if stage in (1, 4):
            return {"row": me + 2 - 4 * b}
        return {"row": ((k + o) % deep) * 4 + me % 4}

    barrier = pltpu.get_barrier_semaphore()
    others = [(0, 0), (1, 0)] + [(2, o) for o in range(1, deep)]
    for stage, o in others:
        pl.semaphore_signal(barrier, inc=1, device_id=peer(stage, o), device_id_type=pl.DeviceIdType.MESH)

    @pl.when(me > 0)
    def _():
        pl.semaphore_signal(barrier, inc=1, device_id={"row": me - 1}, device_id_type=pl.DeviceIdType.MESH)

    @pl.when(me < length - 1)
    def _():
        pl.semaphore_signal(barrier, inc=1, device_id={"row": me + 1}, device_id_type=pl.DeviceIdType.MESH)

    fetches = [
        pltpu.make_async_copy(src, dst, local_sems.at[n])
        for n, (src, dst) in enumerate(((grad_a, part_a), (landed_a, came_a), (grad_b, part_b)))
    ]
    for fetch in fetches:
        fetch.start()
    for q in range(pieces):
        stage_near(q)

    @pl.when(me == 0)
    def _():
        came_b[...] = jnp.zeros_like(came_b)

    pl.semaphore_wait(
        barrier, len(others) + (me > 0).astype(jnp.int32) + (me < length - 1).astype(jnp.int32)
    )
    early = 5 * below_ref.shape[0] // 8
    downs = []
    for n, at in enumerate((pl.ds(0, early), pl.ds(early, below_ref.shape[0] - early))):
        downs.append(pltpu.make_async_remote_copy(
            src_ref=below_ref.at[at], dst_ref=came_b.at[at],
            send_sem=down_sems.at[n], recv_sem=down_sems.at[2 + n],
            device_id={"row": jnp.minimum(me + 1, length - 1)}, device_id_type=pl.DeviceIdType.MESH,
        ))

    def send_down(n):
        @pl.when(me < length - 1)
        def _():
            downs[n].start()

    rows = part_a.shape[2]
    line = 2 * (part_a.shape[0] + part_b.shape[0])
    block = 32

    def merge(part, came, base, first, last):
        many = part.shape[0]

        @pl.loop(first, last)
        def _(i):
            at = pl.multiple_of(i * block, block)
            for t in range(many):
                for p in range(2):
                    value = part[t, p, pl.ds(at, block), :]
                    value = value + came[t, p, pl.ds(at, block), :].astype(f32)
                    temp[pl.ds(2 * t + p, block, stride=2 * many + 1), :] = value
            for y in range(block):
                grad_ref[pl.ds(pl.multiple_of((at + y) * line + 2 * base, 8), 2 * many), :] = temp[
                    y * (2 * many + 1) : y * (2 * many + 1) + 2 * many, :
                ]

    base = [0, pieces, 2 * pieces, (2 + deep) * pieces, (2 + 2 * deep) * pieces, (3 + 2 * deep) * pieces]

    def span_of(start, size):
        return pl.ds(pl.multiple_of(start, ROWS), size)

    def place(q, stage):
        start = q * part
        if stage == 0:
            return start
        start = start + c * half
        if stage == 1:
            return start
        start = start + b * quarter
        return start if stage == 2 else start + k * leaf

    def link(stage, q, o=0):
        at = span_of(q * quarter, quarter)
        if stage == 0:
            src, dst = near.at[span_of(q * half, half)], got0.at[span_of(q * half, half)]
        elif stage == 1:
            src, dst = send1.at[at], got1.at[at]
        elif stage == 2:
            src = send2.at[span_of(q * quarter + ((k + o) % deep) * leaf, leaf)]
            dst = got2.at[span_of((q * deep + o) * leaf, leaf)]
        elif stage == 3:
            src = dst = full.at[span_of(place(q, 3), leaf)]
        elif stage == 4:
            src = dst = full.at[span_of(place(q, 2), quarter)]
        else:
            src = dst = full.at[span_of(place(q, 1), half)]
        sem = base[stage] + (q * deep + o if stage in (2, 3) else q)
        return pltpu.make_async_remote_copy(
            src_ref=src, dst_ref=dst, send_sem=sends.at[sem], recv_sem=recvs.at[sem],
            device_id=peer(stage, o), device_id_type=pl.DeviceIdType.MESH,
        )

    started = []

    def begin(stage, q):
        for o in range(1, deep) if stage in (2, 3) else (0,):
            copy = link(stage, q, o)
            copy.start()
            started.append(copy)

    def arrive(stage, q):
        for o in range(1, deep) if stage in (2, 3) else (0,):
            link(stage, q, o).wait_recv()

    def act(stage, q):
        if stage == 0:
            pass
        elif stage == 1:
            arrive(0, q)
            away = q * part + c * half + (1 - b) * quarter
            send1[span_of(q * quarter, quarter)] = (
                x_ref[span_of(away, quarter)] + got0[span_of(q * half + (1 - b) * quarter, quarter)].astype(f32)
            ).astype(bf16)
        elif stage == 2:
            arrive(1, q)
            own = (
                x_ref[span_of(place(q, 2), quarter)]
                + got0[span_of(q * half + b * quarter, quarter)].astype(f32)
                + got1[span_of(q * quarter, quarter)].astype(f32)
            )
            send2[span_of(q * quarter, quarter)] = own.astype(bf16)
        elif stage == 3:
            arrive(2, q)
            own = (
                x_ref[span_of(place(q, 3), leaf)]
                + got0[span_of(q * half + b * quarter + k * leaf, leaf)].astype(f32)
                + got1[span_of(q * quarter + k * leaf, leaf)].astype(f32)
            )
            for o in range(1, deep):
                own = own + got2[span_of((q * deep + o) * leaf, leaf)].astype(f32)
            full[span_of(place(q, 3), leaf)] = own.astype(bf16)
        elif stage == 6:
            arrive(5, q)
            planes = modes * 2 * tiles
            size = lines // planes
            for plane in range(planes * q // pieces, planes * (q + 1) // pieces):
                m, p, tile = plane // (2 * tiles), plane // tiles % 2, plane % tiles
                out_ref[pl.ds((m * size * tiles + tile) * 2 + p, size, stride=2 * tiles), :] = full[
                    pl.ds(plane * size, size), :
                ].astype(f32)
            return
        else:
            arrive(stage - 1, q)
        begin(stage, q)

    for q in range(pieces):
        act(0, q)
    chunks = rows // block
    done = 0
    for t in range(pieces + 6):
        for stage in range(6, 0, -1):
            q = t - stage
            if 0 <= q < pieces:
                act(stage, q)
                if stage == 1 and q == pieces - 1:
                    send_down(0)
                    fetches[0].wait()
                    fetches[1].wait()
                if stage == 4 and q == pieces - 1:
                    send_down(1)
        if t >= pieces and done < chunks:
            more = min(chunks, done + (chunks + 3) // 4)
            merge(part_a, came_a, 0, done, more)
            done = more
    if done < chunks:
        merge(part_a, came_a, 0, done, chunks)
    for copy in started:
        copy.wait_send()
    fetches[2].wait()

    for n in range(2):

        @pl.when(me < length - 1)
        def _():
            downs[n].wait_send()

        @pl.when(me > 0)
        def _():
            downs[n].wait_recv()

    merge(part_b, came_b, part_a.shape[0], 0, chunks)


def summed(x, grads, landed, below, modes, tiles, axis):
    length = lax.axis_size(axis)
    lines, width = x.shape
    f32, bf16 = jnp.float32, jnp.bfloat16
    pieces = 2 if lines % (length * ROWS * 2) == 0 else 1
    vmem = pl.BlockSpec(memory_space=pltpu.VMEM)
    hbm = pl.BlockSpec(memory_space=pl.ANY)
    count = pieces * (4 + 2 * (length // 4))
    rows = grads[0].shape[2]
    if below.shape[2] < rows:
        room = ((0, 0), (0, 0), (0, rows - below.shape[2]), (0, 0))
        landed, below = jnp.pad(landed, room), jnp.pad(below, room)
    total = 2 * rows * (grads[0].shape[0] + grads[1].shape[0])
    return pl.pallas_call(
        functools.partial(total_kernel, length, pieces, modes, tiles),
        out_shape=(
            jax.ShapeDtypeStruct((lines, width), f32),
            jax.ShapeDtypeStruct((total, width), f32),
        ),
        in_specs=[vmem, hbm, hbm, hbm, vmem],
        out_specs=(vmem, vmem),
        scratch_shapes=[
            pltpu.VMEM((lines // 2, width), bf16),
            pltpu.VMEM((lines // 4, width), bf16),
            pltpu.VMEM((lines // 4, width), bf16),
            pltpu.VMEM((lines // 2, width), bf16),
            pltpu.VMEM((lines // 4, width), bf16),
            pltpu.VMEM((lines // 4, width), bf16),
            pltpu.VMEM((lines, width), bf16),
            pltpu.VMEM(grads[0].shape, f32),
            pltpu.VMEM(grads[1].shape, f32),
            pltpu.VMEM(landed.shape, bf16),
            pltpu.VMEM(below.shape, bf16),
            pltpu.VMEM((32 * (2 * max(g.shape[0] for g in grads) + 1) + 7, width), f32),
            pltpu.SemaphoreType.DMA((count,)),
            pltpu.SemaphoreType.DMA((count,)),
            pltpu.SemaphoreType.DMA((4,)),
            pltpu.SemaphoreType.DMA((3,)),
        ],
        compiler_params=pltpu.CompilerParams(collective_id=0, has_side_effects=True, vmem_limit_bytes=40 << 20),
        name="total",
    )(x, *grads, landed, below)


def dft_tables(patch):
    index = np.arange(patch)
    angle = ((index[:, None] * index[None, :]) % patch).astype(np.float64) * (2.0 * math.pi / patch)
    scale = 1.0 / math.sqrt(patch)
    cosine, sine = np.cos(angle) * scale, np.sin(angle) * scale
    half = patch // 2
    tables = []
    for odd in range(2):
        c, s = cosine[:half, odd::2], sine[:half, odd::2]
        tables.append(np.block([[c, -s], [s, c]]))
        tables.append(np.block([[c.T, s.T], [-s.T, c.T]]))
    order = np.concatenate([index[0::2], index[1::2]])
    tables.append((index[:, None] == order[None, :]).astype(np.float64))
    stacked = np.stack(tables).astype(np.float32)
    return jnp.asarray(stacked).astype(jnp.bfloat16)


def step_kernel(
    modes, size, rows, first_tile, low, high, keep, own_parts, rim_parts, carried, *refs
):
    f32, bf16 = jnp.float32, jnp.bfloat16
    refs = list(refs)

    def take(n):
        got, refs[:] = refs[:n], refs[n:]
        return got

    count_ref, top_ref, left_ref, code_ref = take(4)
    probe_hbm, measured_hbm, table_hbm = take(3)
    owns, rims = take(len(own_parts)), take(len(rim_parts))
    if carried:
        handed_hbm, sum_hbm, before_ref = take(3)
    grad_hbm, below_ref, pgrad_hbm, moved_ref = take(4)
    over_hbm = None if carried else take(1)[0]
    (ext, acc, probe, measured_ref, table_ref, pgrad, rowx, slope, patch, waves, mids, far, power, ratios, meas, gs,
     sems, out_sems) = refs
    tiles = size // LANES
    half = size // 2
    slots = measured_ref.shape[0]
    span = 32
    along, inverse_of = (0, 2), (1, 3)
    copies = []

    def fetch(src, dst):
        copy = pltpu.make_async_copy(src, dst, sems.at[len(copies)])
        copy.start()
        copies.append(copy)

    for sources, ranges, row, n in ((owns, own_parts, 0, rows), (rims, rim_parts, rows, size)):
        for source, (start, stop, to) in zip(sources, ranges):
            fetch(
                source.at[pl.ds(start, stop - start)],
                ext.at[pl.ds(to, stop - start), :, pl.ds(row, n), :],
            )
    fetch(probe_hbm, probe)
    fetch(measured_hbm, measured_ref)
    fetch(table_hbm, table_ref)
    overlap = 0
    if carried:
        overlap = handed_hbm.shape[0]
        fetch(handed_hbm, acc.at[pl.ds(0, overlap)])
        fetch(sum_hbm, pgrad)
    else:
        pgrad[...] = jnp.zeros_like(pgrad)
    gs[...] = jnp.zeros_like(gs)

    @pl.loop(overlap, acc.shape[0])
    def _(k):
        for p in range(2):
            acc[k, p] = jnp.zeros(acc.shape[2:], f32)

    for j in range(slots):
        for p in range(2):
            moved_ref[p, j] = before_ref[p, j] if carried else 0.0
    for copy in copies:
        copy.wait()

    def one(j):
        top, left, code = top_ref[j], left_ref[j], code_ref[j]
        first = left // LANES
        col = left - first * LANES
        first = first - first_tile
        base_row = pl.multiple_of(top // ROWS * ROWS, ROWS)
        row = top - base_row
        fy = (code // 4).astype(f32) * 0.25
        fx = (code % 4).astype(f32) * 0.25
        reach = (tiles + 1) * LANES
        tall = size + ROWS
        here = lax.broadcasted_iota(jnp.int32, (reach, size), 0)
        away = here - lax.broadcasted_iota(jnp.int32, (reach, size), 1) - col
        at_left, at_right = (away == 0).astype(f32), (away == 1).astype(f32)
        mix = ((1.0 - fx) * at_left + fx * at_right).astype(bf16)
        tilt = (at_right - at_left).astype(bf16)
        for p in range(2):
            window = jnp.concatenate(
                [ext[first + k, p, pl.ds(base_row, tall), :] for k in range(tiles + 1)], axis=1
            )
            for table, kept in ((mix, rowx), (tilt, slope)):
                cells = jnp.dot(window, table, preferred_element_type=f32)
                for k in range(tiles):
                    kept[p, k, 0:tall, :] = cells[:, k * LANES : (k + 1) * LANES]
        for p in range(2):
            for k in range(tiles):
                for i in range(size // span):
                    upper = rowx[p, k, pl.ds(row + i * span, span), :]
                    lower = rowx[p, k, pl.ds(row + i * span + 1, span), :]
                    patch[p, i * span : (i + 1) * span, k * LANES : (k + 1) * LANES] = upper + fy * (lower - upper)

        ordered = jnp.dot(measured_ref[j], table_ref[4], preferred_element_type=f32)
        for k in range(tiles):
            meas[k] = ordered[:, k * LANES : (k + 1) * LANES]

        share = size // modes
        short = share // 2

        def wave(c):
            for h in range(2):
                at = slice(h * half + c * short, h * half + (c + 1) * short)
                re, im = patch[0, at, :], patch[1, at, :]
                for m in range(modes):
                    here = slice(m * share + h * short, m * share + (h + 1) * short)
                    pr, pi = probe[m, 0, at, :], probe[m, 1, at, :]
                    for q, w in enumerate((pr * re - pi * im, pr * im + pi * re)):
                        to = slice(q * half, (q + 1) * half)
                        waves[0, c, here, to] = (w[:, :half] + w[:, half:]).astype(bf16)
                        waves[1, c, here, to] = (w[:, :half] - w[:, half:]).astype(bf16)

        def along_columns(c):
            for e in range(2):
                h = jnp.dot(waves[e, c], table_ref[along[e]], preferred_element_type=f32)
                to = slice(e * half, (e + 1) * half)
                for m in range(modes):
                    for q in range(2):
                        upper = h[m * share : m * share + short, q * half : (q + 1) * half]
                        lower = h[m * share + short : (m + 1) * share, q * half : (q + 1) * half]
                        at = slice(q * half + c * short, q * half + (c + 1) * short)
                        mids[m, 0, at, to] = (upper + lower).astype(bf16)
                        mids[m, 1, at, to] = (upper - lower).astype(bf16)

        def along_rows(m):
            for e in range(2):
                f = jnp.dot(table_ref[inverse_of[e]], mids[m, e], preferred_element_type=f32)
                far[m, e] = f.astype(far.dtype)
                strength = f[:half] * f[:half] + f[half:] * f[half:]
                if m == 0:
                    power[e] = strength
                else:
                    power[e] += strength

        def skewed(*stages):
            for t in range(modes + len(stages) - 1):
                for n in reversed(range(len(stages))):
                    if 0 <= t - n < modes:
                        stages[n](t - n)

        skewed(wave, along_columns)
        skewed(along_rows)

        for e in range(2):
            for k in range(tiles):
                to = slice(k * LANES, (k + 1) * LANES)
                amplitude = meas[k, pl.ds(e, half, stride=2), :]
                ratio = 1.0 - amplitude * jnp.minimum(lax.rsqrt(power[e, :, to]), 2.0)
                ratios[e, :, to] = ratio.astype(bf16)

        def error(m):
            for e in range(2):
                ratio = ratios[e]
                mids[m, e, 0:half, :] = far[m, e, 0:half, :] * ratio
                mids[m, e, half:size, :] = far[m, e, half:size, :] * ratio

        def back_rows(m):
            parts = [jnp.dot(table_ref[along[e]], mids[m, e], preferred_element_type=f32) for e in range(2)]
            for h, both in enumerate((parts[0] + parts[1], parts[0] - parts[1])):
                for e in range(2):
                    for q in range(2):
                        to, at = slice(q * half, (q + 1) * half), slice(e * half, (e + 1) * half)
                        for n in range(half // share):
                            waves[e, h * (half // share) + n, m * share : (m + 1) * share, to] = both[
                                q * half + n * share : q * half + (n + 1) * share, at
                            ].astype(bf16)

        def back_columns(c):
            back = [jnp.dot(waves[e, c], table_ref[inverse_of[e]], preferred_element_type=f32) for e in range(2)]
            for i in range(share // span):
                start = c * share + i * span
                at = slice(start, start + span)
                for k in range(2):
                    to = slice(k * half, (k + 1) * half)
                    re, im = patch[0, at, to], patch[1, at, to]
                    sums = [0.0, 0.0]
                    for m in range(modes):
                        here = slice(m * share + i * span, m * share + (i + 1) * span)
                        b0, b1 = back[0][here], back[1][here]
                        mixed = b0 + b1 if k == 0 else b0 - b1
                        ur, ui = mixed[:, :half], mixed[:, half:]
                        pr, pi = probe[m, 0, at, to], probe[m, 1, at, to]
                        sums[0] = sums[0] + (pr * ur + pi * ui)
                        sums[1] = sums[1] + (pr * ui - pi * ur)
                        pgrad[m, 0, k, at, :] += re * ur + im * ui
                        pgrad[m, 1, k, at, :] += re * ui - im * ur
                    for p in range(2):
                        gs[p, k, 8 + start : 8 + start + span, :] = sums[p]

        skewed(error, back_rows)
        skewed(back_columns)

        down, across = jnp.zeros((8, LANES), f32), jnp.zeros((8, LANES), f32)
        for i in range(size // span):
            for p in range(2):
                for k in range(tiles):
                    at, after = pl.ds(row + i * span, span), pl.ds(row + i * span + 1, span)
                    g = gs[p, k, 8 + i * span : 8 + (i + 1) * span, :]
                    dy = g * (rowx[p, k, after, :] - rowx[p, k, at, :])
                    upper = slope[p, k, at, :]
                    dx = g * (upper + fy * (slope[p, k, after, :] - upper))
                    down = down + jnp.sum(dy.reshape(span // 8, 8, LANES), 0)
                    across = across + jnp.sum(dx.reshape(span // 8, 8, LANES), 0)
        moved_ref[0, j] = jnp.sum(down) / size
        moved_ref[1, j] = jnp.sum(across) / size

        base = pl.multiple_of(top // 8 * 8, 8)
        lag = top - base

        there = lax.broadcasted_iota(jnp.int32, (size, reach), 1)
        gone = there - lax.broadcasted_iota(jnp.int32, (size, reach), 0) - col
        spread = ((1.0 - fx) * (gone == 0).astype(f32) + fx * (gone == 1).astype(f32)).astype(bf16)
        for p in range(2):
            g = []
            for k in range(tiles):
                here = gs[p, k, pl.ds(8 - lag, tall), :]
                before = gs[p, k, pl.ds(7 - lag, tall), :]
                g.append((here + fy * (before - here)).astype(bf16))
            wide = jnp.dot(jnp.concatenate(g, axis=1), spread, preferred_element_type=f32)
            for k in range(tiles + 1):
                acc[first + k, p, pl.ds(base, tall), :] += wide[:, k * LANES : (k + 1) * LANES]

    @pl.loop(0, count_ref[0])
    def _(j):
        tile = left_ref[j] // LANES

        @pl.when((tile >= low) & (tile < high))
        def _():
            one(j)

    outs = [
        pltpu.make_async_copy(acc.at[pl.ds(0, keep), :, pl.ds(0, rows), :], grad_hbm, out_sems.at[0]),
        pltpu.make_async_copy(pgrad, pgrad_hbm, out_sems.at[1]),
    ]
    if not carried:
        outs.append(pltpu.make_async_copy(acc.at[pl.ds(keep, over_hbm.shape[0])], over_hbm, out_sems.at[2]))
    for out in outs:
        out.start()

    @pl.loop(0, keep)
    def _(k):
        for p in range(2):
            below_ref[k, p] = acc[k, p, rows : rows + size, :].astype(bf16)

    for out in outs:
        out.wait()


def step(modes, size, rows, slots, first_tile, low, high, keep, count, own, rim, carried, common):
    f32, bf16 = jnp.float32, jnp.bfloat16
    tiles = size // LANES
    deep = rows + size + 8
    vmem = pl.BlockSpec(memory_space=pltpu.VMEM)
    smem = pl.BlockSpec(memory_space=pltpu.SMEM)
    hbm = pl.BlockSpec(memory_space=pl.ANY)
    planes = (modes, 2, tiles, size, LANES)
    out_shape = [
        jax.ShapeDtypeStruct((keep, 2, rows, LANES), f32),
        jax.ShapeDtypeStruct((keep, 2, size, LANES), bf16),
        jax.ShapeDtypeStruct(planes, f32),
        jax.ShapeDtypeStruct((2, slots), f32),
    ]
    out_specs = [hbm, vmem, hbm, smem]
    if not carried:
        out_shape.append(jax.ShapeDtypeStruct((count - keep, 2, deep, LANES), f32))
        out_specs.append(hbm)
    own_arrays, own_parts = zip(*own)
    rim_arrays, rim_parts = zip(*rim)
    return pl.pallas_call(
        functools.partial(
            step_kernel, modes, size, rows, first_tile, low, high, keep, own_parts, rim_parts, bool(carried)
        ),
        out_shape=tuple(out_shape),
        in_specs=[smem] * 4 + [hbm] * (3 + len(own) + len(rim)) + ([hbm, hbm, smem] if carried else []),
        out_specs=tuple(out_specs),
        scratch_shapes=[
            pltpu.VMEM((count, 2, rows + size, LANES), bf16),
            pltpu.VMEM((count, 2, deep, LANES), f32),
            pltpu.VMEM((modes, 2, size, size), f32),
            pltpu.VMEM((slots, size, size), bf16),
            pltpu.VMEM((5, size, size), bf16),
            pltpu.VMEM(planes, f32),
            pltpu.VMEM((2, tiles, size + 32, LANES), f32),
            pltpu.VMEM((2, tiles, size + 32, LANES), f32),
            pltpu.VMEM((2, size, size), f32),
            pltpu.VMEM((2, modes, size, size), bf16),
            pltpu.VMEM((modes, 2, size, size), bf16),
            pltpu.VMEM((modes, 2, size, size), bf16),
            pltpu.VMEM((2, size // 2, size), f32),
            pltpu.VMEM((2, size // 2, size), bf16),
            pltpu.VMEM((tiles, size, LANES), f32),
            pltpu.VMEM((2, tiles, size + 32, LANES), f32),
            pltpu.SemaphoreType.DMA((12,)),
            pltpu.SemaphoreType.DMA((3,)),
        ],
        compiler_params=pltpu.CompilerParams(vmem_limit_bytes=48 << 20),
        cost_estimate=pl.CostEstimate(flops=3 << 30, bytes_accessed=16 << 20, transcendentals=0),
        name="step_b" if carried else "step_a",
    )(*common, *own_arrays, *rim_arrays, *carried)


def sort_kernel(lines, x_ref, near_ref, rest_ref, temp):
    n = near_ref.shape[2]
    line = 2 * lines
    for y in range(n):
        temp[y * (line + 1) : y * (line + 1) + line, :] = x_ref[y * line : (y + 1) * line, :].astype(jnp.float32)
    for k in range(lines):
        for p in range(2):
            plane = temp[pl.ds(2 * k + p, n, stride=line + 1), :].astype(jnp.bfloat16)
            if k < near_ref.shape[0]:
                near_ref[k, p] = plane
            else:
                rest_ref[k - near_ref.shape[0], p] = plane


def sorted_planes(x, rows, lines, near):
    n = 64
    return pl.pallas_call(
        functools.partial(sort_kernel, lines),
        grid=(rows // n,),
        out_shape=tuple(
            jax.ShapeDtypeStruct((t, 2, rows, LANES), jnp.bfloat16) for t in (near, lines - near)
        ),
        in_specs=[pl.BlockSpec((n * lines * 2, LANES), lambda i: (i, 0))],
        out_specs=tuple(
            pl.BlockSpec((t, 2, n, LANES), lambda i: (0, 0, i, 0)) for t in (near, lines - near)
        ),
        scratch_shapes=[pltpu.VMEM((n * (lines * 2 + 1) + 7, LANES), jnp.float32)],
        cost_estimate=pl.CostEstimate(flops=1 << 20, bytes_accessed=4 << 20, transcendentals=0),
        name="sort",
    )(x)


def probe_kernel(tiles, x_ref, out_ref):
    size = out_ref.shape[2]
    for p in range(2):
        for k in range(tiles):
            out_ref[0, p, :, k * LANES : (k + 1) * LANES] = x_ref[pl.ds(2 * k + p, size, stride=2 * tiles), :]


def probe_planes(x, modes, size):
    tiles = size // LANES
    return pl.pallas_call(
        functools.partial(probe_kernel, tiles),
        grid=(modes,),
        out_shape=jax.ShapeDtypeStruct((modes, 2, size, size), jnp.float32),
        in_specs=[pl.BlockSpec((size * tiles * 2, LANES), lambda m: (m, 0))],
        out_specs=pl.BlockSpec((1, 2, size, size), lambda m: (m, 0, 0, 0)),
        cost_estimate=pl.CostEstimate(flops=1 << 20, bytes_accessed=4 << 20, transcendentals=0),
        name="probes",
    )(x)


def tiled(x):
    *lead, two, width = x.shape
    n = math.prod(lead)
    x = x.reshape(n, two, width // LANES, LANES)
    return jnp.transpose(x, (0, 2, 1, 3)).reshape(-1, LANES)


def untiled(x, lead, width):
    n = math.prod(lead)
    x = jnp.transpose(x.reshape(n, width // LANES, 2, LANES), (0, 2, 1, 3))
    return x.reshape(*lead, 2, width)


def shards(object_tiles, probe, measured, offset_row, offset_col, subpixel, live_count):
    rows, _, width = object_tiles.shape
    modes, size = probe.shape[:2]
    slots = measured.shape[0]
    lines, tiles = width // LANES, size // LANES
    mid = lines // 2
    near = mid + tiles
    own_a, own_b = sorted_planes(tiled(object_tiles), rows, lines, near)
    rim_a = passed_along(own_a[:, :, :size], "row", -1)
    rim_b = passed_along(own_b[:, :, :size], "row", -1)
    planes = probe_planes(tiled(probe), modes, size)
    common = (live_count, offset_row, offset_col, subpixel, planes, measured, dft_tables(size))
    whole = (0, near, 0)
    grad_a, below_a, sum_a, moved_a, over = step(
        modes, size, rows, slots, 0, 0, mid, mid, near, [(own_a, whole)], [(rim_a, whole)], (), common
    )
    landed_a = passed_along(below_a, "row", 1)
    kept, rest = (mid, near, 0), (0, lines - near, tiles)
    grad_b, below_b, sums, moved = step(
        modes, size, rows, slots, mid, mid, lines, lines - mid, lines - mid,
        [(own_a, kept), (own_b, rest)], [(rim_a, kept), (rim_b, rest)], (over, sum_a, moved_a), common,
    )
    probe_grad, grad = summed(
        sums.reshape(-1, LANES), (grad_a, grad_b), landed_a, below_b, modes, tiles, "row"
    )
    return (untiled(grad, (rows,), width), untiled(probe_grad, (modes, size), size), moved)


def solution(mesh):
    in_specs = (
        P(("groups", "row"), None, None),
        P(),
        P(("groups", "row"), None, None),
        P(("groups", "row")),
        P(("groups", "row")),
        P(("groups", "row")),
        P(("groups", "row")),
    )
    out_specs = (
        P(("groups", "row"), None, None),
        P("groups", None, None, None),
        P(None, ("groups", "row")),
    )
    return jax.shard_map(shards, mesh=mesh, in_specs=in_specs, out_specs=out_specs, check_vma=False)
```

```python
import functools
import math

import jax
import jax.numpy as jnp
import numpy as np
from jax import lax
from jax.experimental import pallas as pl
from jax.experimental.pallas import tpu as pltpu
from jax.sharding import PartitionSpec as P

LANES = 128
ROWS = 16


def passed_along(x, axis, by, odd=False):
    length = lax.axis_size(axis)
    pairs = [(i, i + by) for i in range(odd, length, 1 + odd) if 0 <= i + by < length]
    return lax.ppermute(x, axis, pairs)


def total_kernel(
    length, pieces, modes, tiles, x_ref, grad_a, grad_b, landed_a, above_ref, below_ref, out_ref, grad_ref, landed_ref,
    near, send1, send2, got0, got1, got2, full, part_a, part_b, came_a, came_b, temp, sends, recvs, down_sems, local_sems,
):
    f32, bf16 = jnp.float32, jnp.bfloat16
    lines, width = x_ref.shape
    deep = length // 4
    me = lax.axis_index("row")
    c, b, k = me % 2, (me // 2) % 2, me // 4
    part = lines // pieces
    half, quarter = part // 2, part // 4
    leaf = quarter // deep

    def stage_near(q):
        near[pl.ds(q * half, half)] = x_ref[
            pl.ds(pl.multiple_of(q * part + (1 - c) * half, ROWS), half)
        ].astype(bf16)

    def peer(stage, o):
        if stage in (0, 5):
            return {"row": me + 1 - 2 * c}
        if stage in (1, 4):
            return {"row": me + 2 - 4 * b}
        return {"row": ((k + o) % deep) * 4 + me % 4}

    barrier = pltpu.get_barrier_semaphore()
    others = [(0, 0), (1, 0)] + [(2, o) for o in range(1, deep)]
    for stage, o in others:
        pl.semaphore_signal(barrier, inc=1, device_id=peer(stage, o), device_id_type=pl.DeviceIdType.MESH)

    @pl.when(me > 0)
    def _():
        pl.semaphore_signal(barrier, inc=1, device_id={"row": me - 1}, device_id_type=pl.DeviceIdType.MESH)

    @pl.when(me < length - 1)
    def _():
        pl.semaphore_signal(barrier, inc=1, device_id={"row": me + 1}, device_id_type=pl.DeviceIdType.MESH)

    fetches = [
        pltpu.make_async_copy(src, dst, local_sems.at[n])
        for n, (src, dst) in enumerate(((grad_a, part_a), (grad_b, part_b), (landed_a, came_a)))
    ]
    for fetch in fetches[:2]:
        fetch.start()

    @pl.when(c == 0)
    def _():
        fetches[2].start()

    for q in range(pieces):
        stage_near(q)

    @pl.when(me == 0)
    def _():
        came_b[...] = jnp.zeros_like(came_b)

    pl.semaphore_wait(
        barrier, len(others) + (me > 0).astype(jnp.int32) + (me < length - 1).astype(jnp.int32)
    )
    early = 5 * below_ref.shape[0] // 8
    downs = []
    for n, (src, dst, first, last) in enumerate((
        (below_ref, came_b, 0, early),
        (below_ref, came_b, early, below_ref.shape[0]),
        (above_ref, came_a, 0, above_ref.shape[0]),
    )):
        at = pl.ds(first, last - first)
        downs.append(pltpu.make_async_remote_copy(
            src_ref=src.at[at], dst_ref=dst.at[at],
            send_sem=down_sems.at[n], recv_sem=down_sems.at[3 + n],
            device_id={"row": jnp.minimum(me + 1, length - 1)}, device_id_type=pl.DeviceIdType.MESH,
        ))

    def send_down(n):
        @pl.when((c == 0) if n == 2 else (me < length - 1))
        def _():
            downs[n].start()

    rows = part_a.shape[2]
    line = 2 * (part_a.shape[0] + part_b.shape[0])
    block = 32

    def lay_out(part, out, first):
        many = part.shape[0]

        @pl.loop(0, rows // block)
        def _(i):
            at = pl.multiple_of(i * block, block)
            for t in range(many):
                for p in range(2):
                    temp[pl.ds(2 * t + p, block, stride=2 * many + 1), :] = part[t, p, pl.ds(at, block), :].astype(f32)
            for y in range(block):
                out[pl.ds(pl.multiple_of((at + y) * line + 2 * first, ROWS), 2 * many), :] = temp[
                    y * (2 * many + 1) : y * (2 * many + 1) + 2 * many, :
                ].astype(out.dtype)

    base = [0, pieces, 2 * pieces, (2 + deep) * pieces, (2 + 2 * deep) * pieces, (3 + 2 * deep) * pieces]

    def span_of(start, size):
        return pl.ds(pl.multiple_of(start, ROWS), size)

    def place(q, stage):
        start = q * part
        if stage == 0:
            return start
        start = start + c * half
        if stage == 1:
            return start
        start = start + b * quarter
        return start if stage == 2 else start + k * leaf

    def link(stage, q, o=0):
        at = span_of(q * quarter, quarter)
        if stage == 0:
            src, dst = near.at[span_of(q * half, half)], got0.at[span_of(q * half, half)]
        elif stage == 1:
            src, dst = send1.at[at], got1.at[at]
        elif stage == 2:
            src = send2.at[span_of(q * quarter + ((k + o) % deep) * leaf, leaf)]
            dst = got2.at[span_of((q * deep + o) * leaf, leaf)]
        elif stage == 3:
            src = dst = full.at[span_of(place(q, 3), leaf)]
        elif stage == 4:
            src = dst = full.at[span_of(place(q, 2), quarter)]
        else:
            src = dst = full.at[span_of(place(q, 1), half)]
        sem = base[stage] + (q * deep + o if stage in (2, 3) else q)
        return pltpu.make_async_remote_copy(
            src_ref=src, dst_ref=dst, send_sem=sends.at[sem], recv_sem=recvs.at[sem],
            device_id=peer(stage, o), device_id_type=pl.DeviceIdType.MESH,
        )

    started = []

    def begin(stage, q):
        for o in range(1, deep) if stage in (2, 3) else (0,):
            copy = link(stage, q, o)
            copy.start()
            started.append(copy)

    def arrive(stage, q):
        for o in range(1, deep) if stage in (2, 3) else (0,):
            link(stage, q, o).wait_recv()

    def act(stage, q):
        if stage == 0:
            pass
        elif stage == 1:
            arrive(0, q)
            away = q * part + c * half + (1 - b) * quarter
            send1[span_of(q * quarter, quarter)] = (
                x_ref[span_of(away, quarter)] + got0[span_of(q * half + (1 - b) * quarter, quarter)].astype(f32)
            ).astype(bf16)
        elif stage == 2:
            arrive(1, q)
            own = (
                x_ref[span_of(place(q, 2), quarter)]
                + got0[span_of(q * half + b * quarter, quarter)].astype(f32)
                + got1[span_of(q * quarter, quarter)].astype(f32)
            )
            send2[span_of(q * quarter, quarter)] = own.astype(bf16)
        elif stage == 3:
            arrive(2, q)
            own = (
                x_ref[span_of(place(q, 3), leaf)]
                + got0[span_of(q * half + b * quarter + k * leaf, leaf)].astype(f32)
                + got1[span_of(q * quarter + k * leaf, leaf)].astype(f32)
            )
            for o in range(1, deep):
                own = own + got2[span_of((q * deep + o) * leaf, leaf)].astype(f32)
            full[span_of(place(q, 3), leaf)] = own.astype(bf16)
        elif stage == 6:
            arrive(5, q)
            planes = modes * 2 * tiles
            size = lines // planes
            for plane in range(planes * q // pieces, planes * (q + 1) // pieces):
                m, p, tile = plane // (2 * tiles), plane // tiles % 2, plane % tiles
                out_ref[pl.ds((m * size * tiles + tile) * 2 + p, size, stride=2 * tiles), :] = full[
                    pl.ds(plane * size, size), :
                ].astype(f32)
            return
        else:
            arrive(stage - 1, q)
        begin(stage, q)

    for q in range(pieces):
        act(0, q)
    for t in range(pieces + 6):
        for stage in range(6, 0, -1):
            q = t - stage
            if 0 <= q < pieces:
                act(stage, q)
                if stage == 1 and q == pieces - 1:
                    send_down(2)
                    send_down(0)
                if stage == 4 and q == pieces - 1:
                    send_down(1)
        if t == pieces:
            fetches[0].wait()
            lay_out(part_a, grad_ref, 0)
        if t == pieces + 1:
            fetches[1].wait()
            lay_out(part_b, grad_ref, part_a.shape[0])
        if t == pieces + 2:

            @pl.when(c == 0)
            def _():
                fetches[2].wait()

            @pl.when(c == 1)
            def _():
                downs[2].wait_recv()

            lay_out(came_a, landed_ref, 0)
    for copy in started:
        copy.wait_send()

    @pl.when(c == 0)
    def _():
        downs[2].wait_send()

    for n in range(2):

        @pl.when(me < length - 1)
        def _():
            downs[n].wait_send()

        @pl.when(me > 0)
        def _():
            downs[n].wait_recv()

    lay_out(came_b, landed_ref, part_a.shape[0])


def summed(x, grads, landed, above, below, modes, tiles, axis):
    length = lax.axis_size(axis)
    lines, width = x.shape
    f32, bf16 = jnp.float32, jnp.bfloat16
    pieces = 2 if lines % (length * ROWS * 2) == 0 else 1
    vmem = pl.BlockSpec(memory_space=pltpu.VMEM)
    hbm = pl.BlockSpec(memory_space=pl.ANY)
    count = pieces * (4 + 2 * (length // 4))
    rows = grads[0].shape[2]
    if below.shape[2] < rows:
        room = ((0, 0), (0, 0), (0, rows - below.shape[2]), (0, 0))
        landed, above, below = (jnp.pad(y, room) for y in (landed, above, below))
    total = 2 * rows * (grads[0].shape[0] + grads[1].shape[0])
    return pl.pallas_call(
        functools.partial(total_kernel, length, pieces, modes, tiles),
        out_shape=(
            jax.ShapeDtypeStruct((lines, width), f32),
            jax.ShapeDtypeStruct((total, width), f32),
            jax.ShapeDtypeStruct((total, width), bf16),
        ),
        in_specs=[vmem, hbm, hbm, hbm, vmem, vmem],
        out_specs=(vmem, vmem, vmem),
        scratch_shapes=[
            pltpu.VMEM((lines // 2, width), bf16),
            pltpu.VMEM((lines // 4, width), bf16),
            pltpu.VMEM((lines // 4, width), bf16),
            pltpu.VMEM((lines // 2, width), bf16),
            pltpu.VMEM((lines // 4, width), bf16),
            pltpu.VMEM((lines // 4, width), bf16),
            pltpu.VMEM((lines, width), bf16),
            pltpu.VMEM(grads[0].shape, f32),
            pltpu.VMEM(grads[1].shape, f32),
            pltpu.VMEM(landed.shape, bf16),
            pltpu.VMEM(below.shape, bf16),
            pltpu.VMEM((32 * (2 * max(g.shape[0] for g in grads) + 1) + 7, width), f32),
            pltpu.SemaphoreType.DMA((count,)),
            pltpu.SemaphoreType.DMA((count,)),
            pltpu.SemaphoreType.DMA((6,)),
            pltpu.SemaphoreType.DMA((3,)),
        ],
        compiler_params=pltpu.CompilerParams(collective_id=0, has_side_effects=True, vmem_limit_bytes=28 << 20),
        name="total",
    )(x, *grads, landed, above, below)


def dft_tables(patch):
    index = np.arange(patch)
    angle = ((index[:, None] * index[None, :]) % patch).astype(np.float64) * (2.0 * math.pi / patch)
    scale = 1.0 / math.sqrt(patch)
    cosine, sine = np.cos(angle) * scale, np.sin(angle) * scale
    half = patch // 2
    tables = []
    for odd in range(2):
        c, s = cosine[:half, odd::2], sine[:half, odd::2]
        tables.append(np.block([[c, -s], [s, c]]))
        tables.append(np.block([[c.T, s.T], [-s.T, c.T]]))
    order = np.concatenate([index[0::2], index[1::2]])
    tables.append((index[:, None] == order[None, :]).astype(np.float64))
    stacked = np.stack(tables).astype(np.float32)
    return jnp.asarray(stacked).astype(jnp.bfloat16)


def step_kernel(
    modes, size, rows, first_tile, low, high, keep, own_parts, rim_parts, carried, *refs
):
    f32, bf16 = jnp.float32, jnp.bfloat16
    refs = list(refs)

    def take(n):
        got, refs[:] = refs[:n], refs[n:]
        return got

    count_ref, top_ref, left_ref, code_ref = take(4)
    probe_hbm, measured_hbm, table_hbm = take(3)
    owns, rims = take(len(own_parts)), take(len(rim_parts))
    if carried:
        handed_hbm, sum_hbm, before_ref = take(3)
    grad_hbm, below_ref, pgrad, moved_ref = take(4)
    over_hbm = None if carried else take(1)[0]
    (ext, acc, probe, measured_ref, table_ref, rowx, slope, patch, waves, mids, far, power, ratios, meas, gs,
     sems, out_sems) = refs
    tiles = size // LANES
    half = size // 2
    slots = measured_ref.shape[0]
    span = 32
    along, inverse_of = (0, 2), (1, 3)
    copies = []

    def fetch(src, dst):
        copy = pltpu.make_async_copy(src, dst, sems.at[len(copies)])
        copy.start()
        copies.append(copy)

    for sources, ranges, row, n in ((owns, own_parts, 0, rows), (rims, rim_parts, rows, size)):
        for source, (start, stop, to) in zip(sources, ranges):
            fetch(
                source.at[pl.ds(start, stop - start)],
                ext.at[pl.ds(to, stop - start), :, pl.ds(row, n), :],
            )
    fetch(probe_hbm, probe)
    fetch(measured_hbm, measured_ref)
    fetch(table_hbm, table_ref)
    overlap = 0
    if carried:
        overlap = handed_hbm.shape[0]
        fetch(handed_hbm, acc.at[pl.ds(0, overlap)])
        fetch(sum_hbm, pgrad)
    else:
        pgrad[...] = jnp.zeros_like(pgrad)
    gs[...] = jnp.zeros_like(gs)

    @pl.loop(overlap, acc.shape[0])
    def _(k):
        for p in range(2):
            acc[k, p] = jnp.zeros(acc.shape[2:], f32)

    for j in range(slots):
        for p in range(2):
            moved_ref[p, j] = before_ref[p, j] if carried else 0.0
    for copy in copies:
        copy.wait()

    def one(j):
        top, left, code = top_ref[j], left_ref[j], code_ref[j]
        first = left // LANES
        col = left - first * LANES
        first = first - first_tile
        base_row = pl.multiple_of(top // ROWS * ROWS, ROWS)
        row = top - base_row
        fy = (code // 4).astype(f32) * 0.25
        fx = (code % 4).astype(f32) * 0.25
        reach = (tiles + 1) * LANES
        tall = size + ROWS
        here = lax.broadcasted_iota(jnp.int32, (reach, size), 0)
        away = here - lax.broadcasted_iota(jnp.int32, (reach, size), 1) - col
        at_left, at_right = (away == 0).astype(f32), (away == 1).astype(f32)
        mix = ((1.0 - fx) * at_left + fx * at_right).astype(bf16)
        tilt = (at_right - at_left).astype(bf16)
        for p in range(2):
            window = jnp.concatenate(
                [ext[first + k, p, pl.ds(base_row, tall), :] for k in range(tiles + 1)], axis=1
            )
            for table, kept in ((mix, rowx), (tilt, slope)):
                cells = jnp.dot(window, table, preferred_element_type=f32)
                for k in range(tiles):
                    kept[p, k, 0:tall, :] = cells[:, k * LANES : (k + 1) * LANES]
        for p in range(2):
            for k in range(tiles):
                for i in range(size // span):
                    upper = rowx[p, k, pl.ds(row + i * span, span), :]
                    lower = rowx[p, k, pl.ds(row + i * span + 1, span), :]
                    patch[p, i * span : (i + 1) * span, k * LANES : (k + 1) * LANES] = upper + fy * (lower - upper)

        ordered = jnp.dot(measured_ref[j], table_ref[4], preferred_element_type=f32)
        for k in range(tiles):
            meas[k] = ordered[:, k * LANES : (k + 1) * LANES]

        share = size // modes
        short = share // 2

        def wave(c):
            for h in range(2):
                at = slice(h * half + c * short, h * half + (c + 1) * short)
                re, im = patch[0, at, :], patch[1, at, :]
                for m in range(modes):
                    here = slice(m * share + h * short, m * share + (h + 1) * short)
                    pr, pi = probe[m, 0, at, :], probe[m, 1, at, :]
                    for q, w in enumerate((pr * re - pi * im, pr * im + pi * re)):
                        to = slice(q * half, (q + 1) * half)
                        waves[0, c, here, to] = (w[:, :half] + w[:, half:]).astype(bf16)
                        waves[1, c, here, to] = (w[:, :half] - w[:, half:]).astype(bf16)

        def along_columns(c):
            for e in range(2):
                h = jnp.dot(waves[e, c], table_ref[along[e]], preferred_element_type=f32)
                to = slice(e * half, (e + 1) * half)
                for m in range(modes):
                    for q in range(2):
                        upper = h[m * share : m * share + short, q * half : (q + 1) * half]
                        lower = h[m * share + short : (m + 1) * share, q * half : (q + 1) * half]
                        at = slice(q * half + c * short, q * half + (c + 1) * short)
                        mids[m, 0, at, to] = (upper + lower).astype(bf16)
                        mids[m, 1, at, to] = (upper - lower).astype(bf16)

        def along_rows(m):
            for e in range(2):
                f = jnp.dot(table_ref[inverse_of[e]], mids[m, e], preferred_element_type=f32)
                far[m, e] = f.astype(far.dtype)
                strength = f[:half] * f[:half] + f[half:] * f[half:]
                if m == 0:
                    power[e] = strength
                else:
                    power[e] += strength

        def skewed(*stages):
            for t in range(modes + len(stages) - 1):
                for n in reversed(range(len(stages))):
                    if 0 <= t - n < modes:
                        stages[n](t - n)

        skewed(wave, along_columns)
        skewed(along_rows)

        for e in range(2):
            for k in range(tiles):
                to = slice(k * LANES, (k + 1) * LANES)
                amplitude = meas[k, pl.ds(e, half, stride=2), :]
                ratio = 1.0 - amplitude * jnp.minimum(lax.rsqrt(power[e, :, to]), 2.0)
                ratios[e, :, to] = ratio.astype(bf16)

        def error(m):
            for e in range(2):
                ratio = ratios[e]
                mids[m, e, 0:half, :] = far[m, e, 0:half, :] * ratio
                mids[m, e, half:size, :] = far[m, e, half:size, :] * ratio

        def back_rows(m):
            parts = [jnp.dot(table_ref[along[e]], mids[m, e], preferred_element_type=f32) for e in range(2)]
            for h, both in enumerate((parts[0] + parts[1], parts[0] - parts[1])):
                for e in range(2):
                    for q in range(2):
                        to, at = slice(q * half, (q + 1) * half), slice(e * half, (e + 1) * half)
                        for n in range(half // share):
                            waves[e, h * (half // share) + n, m * share : (m + 1) * share, to] = both[
                                q * half + n * share : q * half + (n + 1) * share, at
                            ].astype(bf16)

        def back_columns(c):
            back = [jnp.dot(waves[e, c], table_ref[inverse_of[e]], preferred_element_type=f32) for e in range(2)]
            for i in range(share // span):
                start = c * share + i * span
                at = slice(start, start + span)
                for k in range(2):
                    to = slice(k * half, (k + 1) * half)
                    re, im = patch[0, at, to], patch[1, at, to]
                    sums = [0.0, 0.0]
                    for m in range(modes):
                        here = slice(m * share + i * span, m * share + (i + 1) * span)
                        b0, b1 = back[0][here], back[1][here]
                        mixed = b0 + b1 if k == 0 else b0 - b1
                        ur, ui = mixed[:, :half], mixed[:, half:]
                        pr, pi = probe[m, 0, at, to], probe[m, 1, at, to]
                        sums[0] = sums[0] + (pr * ur + pi * ui)
                        sums[1] = sums[1] + (pr * ui - pi * ur)
                        pgrad[m, 0, k, at, :] += re * ur + im * ui
                        pgrad[m, 1, k, at, :] += re * ui - im * ur
                    for p in range(2):
                        gs[p, k, 8 + start : 8 + start + span, :] = sums[p]

        skewed(error, back_rows)
        skewed(back_columns)

        down, across = jnp.zeros((8, LANES), f32), jnp.zeros((8, LANES), f32)
        for i in range(size // span):
            for p in range(2):
                for k in range(tiles):
                    at, after = pl.ds(row + i * span, span), pl.ds(row + i * span + 1, span)
                    g = gs[p, k, 8 + i * span : 8 + (i + 1) * span, :]
                    dy = g * (rowx[p, k, after, :] - rowx[p, k, at, :])
                    upper = slope[p, k, at, :]
                    dx = g * (upper + fy * (slope[p, k, after, :] - upper))
                    down = down + jnp.sum(dy.reshape(span // 8, 8, LANES), 0)
                    across = across + jnp.sum(dx.reshape(span // 8, 8, LANES), 0)
        moved_ref[0, j] = jnp.sum(down) / size
        moved_ref[1, j] = jnp.sum(across) / size

        base = pl.multiple_of(top // 8 * 8, 8)
        lag = top - base

        there = lax.broadcasted_iota(jnp.int32, (size, reach), 1)
        gone = there - lax.broadcasted_iota(jnp.int32, (size, reach), 0) - col
        spread = ((1.0 - fx) * (gone == 0).astype(f32) + fx * (gone == 1).astype(f32)).astype(bf16)
        for p in range(2):
            g = []
            for k in range(tiles):
                here = gs[p, k, pl.ds(8 - lag, tall), :]
                before = gs[p, k, pl.ds(7 - lag, tall), :]
                g.append((here + fy * (before - here)).astype(bf16))
            wide = jnp.dot(jnp.concatenate(g, axis=1), spread, preferred_element_type=f32)
            for k in range(tiles + 1):
                acc[first + k, p, pl.ds(base, tall), :] += wide[:, k * LANES : (k + 1) * LANES]

    @pl.loop(0, count_ref[0])
    def _(j):
        tile = left_ref[j] // LANES

        @pl.when((tile >= low) & (tile < high))
        def _():
            one(j)

    outs = [
        pltpu.make_async_copy(acc.at[pl.ds(0, keep), :, pl.ds(0, rows), :], grad_hbm, out_sems.at[0]),
    ]
    if not carried:
        outs.append(pltpu.make_async_copy(acc.at[pl.ds(keep, over_hbm.shape[0])], over_hbm, out_sems.at[2]))
    for out in outs:
        out.start()

    @pl.loop(0, keep)
    def _(k):
        for p in range(2):
            below_ref[k, p] = acc[k, p, rows : rows + size, :].astype(bf16)

    for out in outs:
        out.wait()


def step(modes, size, rows, slots, first_tile, low, high, keep, count, own, rim, carried, common):
    f32, bf16 = jnp.float32, jnp.bfloat16
    tiles = size // LANES
    deep = rows + size + 8
    vmem = pl.BlockSpec(memory_space=pltpu.VMEM)
    smem = pl.BlockSpec(memory_space=pltpu.SMEM)
    hbm = pl.BlockSpec(memory_space=pl.ANY)
    planes = (modes, 2, tiles, size, LANES)
    out_shape = [
        jax.ShapeDtypeStruct((keep, 2, rows, LANES), f32),
        jax.ShapeDtypeStruct((keep, 2, size, LANES), bf16),
        jax.ShapeDtypeStruct(planes, f32),
        jax.ShapeDtypeStruct((2, slots), f32),
    ]
    out_specs = [hbm, vmem, vmem, smem]
    if not carried:
        out_shape.append(jax.ShapeDtypeStruct((count - keep, 2, deep, LANES), f32))
        out_specs.append(hbm)
    own_arrays, own_parts = zip(*own)
    rim_arrays, rim_parts = zip(*rim)
    return pl.pallas_call(
        functools.partial(
            step_kernel, modes, size, rows, first_tile, low, high, keep, own_parts, rim_parts, bool(carried)
        ),
        out_shape=tuple(out_shape),
        in_specs=[smem] * 4 + [hbm] * (3 + len(own) + len(rim)) + ([hbm, hbm, smem] if carried else []),
        out_specs=tuple(out_specs),
        scratch_shapes=[
            pltpu.VMEM((count, 2, rows + size, LANES), bf16),
            pltpu.VMEM((count, 2, deep, LANES), f32),
            pltpu.VMEM((modes, 2, size, size), f32),
            pltpu.VMEM((slots, size, size), bf16),
            pltpu.VMEM((5, size, size), bf16),
            pltpu.VMEM((2, tiles, size + 32, LANES), f32),
            pltpu.VMEM((2, tiles, size + 32, LANES), f32),
            pltpu.VMEM((2, size, size), f32),
            pltpu.VMEM((2, modes, size, size), bf16),
            pltpu.VMEM((modes, 2, size, size), bf16),
            pltpu.VMEM((modes, 2, size, size), bf16),
            pltpu.VMEM((2, size // 2, size), f32),
            pltpu.VMEM((2, size // 2, size), bf16),
            pltpu.VMEM((tiles, size, LANES), f32),
            pltpu.VMEM((2, tiles, size + 32, LANES), f32),
            pltpu.SemaphoreType.DMA((12,)),
            pltpu.SemaphoreType.DMA((3,)),
        ],
        compiler_params=pltpu.CompilerParams(vmem_limit_bytes=30 << 20),
        cost_estimate=pl.CostEstimate(flops=3 << 30, bytes_accessed=16 << 20, transcendentals=0),
        name="step_b" if carried else "step_a",
    )(*common, *own_arrays, *rim_arrays, *carried)


def sort_kernel(lines, x_ref, near_ref, rest_ref, temp):
    n = near_ref.shape[2]
    line = 2 * lines
    for y in range(n):
        temp[y * (line + 1) : y * (line + 1) + line, :] = x_ref[y * line : (y + 1) * line, :].astype(jnp.float32)
    for k in range(lines):
        for p in range(2):
            plane = temp[pl.ds(2 * k + p, n, stride=line + 1), :].astype(jnp.bfloat16)
            if k < near_ref.shape[0]:
                near_ref[k, p] = plane
            else:
                rest_ref[k - near_ref.shape[0], p] = plane


def sorted_planes(x, rows, lines, near):
    n = 64
    return pl.pallas_call(
        functools.partial(sort_kernel, lines),
        grid=(rows // n,),
        out_shape=tuple(
            jax.ShapeDtypeStruct((t, 2, rows, LANES), jnp.bfloat16) for t in (near, lines - near)
        ),
        in_specs=[pl.BlockSpec((n * lines * 2, LANES), lambda i: (i, 0))],
        out_specs=tuple(
            pl.BlockSpec((t, 2, n, LANES), lambda i: (0, 0, i, 0)) for t in (near, lines - near)
        ),
        scratch_shapes=[pltpu.VMEM((n * (lines * 2 + 1) + 7, LANES), jnp.float32)],
        cost_estimate=pl.CostEstimate(flops=1 << 20, bytes_accessed=4 << 20, transcendentals=0),
        name="sort",
    )(x)


def probe_kernel(tiles, x_ref, out_ref):
    size = out_ref.shape[2]
    for p in range(2):
        for k in range(tiles):
            out_ref[0, p, :, k * LANES : (k + 1) * LANES] = x_ref[pl.ds(2 * k + p, size, stride=2 * tiles), :]


def probe_planes(x, modes, size):
    tiles = size // LANES
    return pl.pallas_call(
        functools.partial(probe_kernel, tiles),
        grid=(modes,),
        out_shape=jax.ShapeDtypeStruct((modes, 2, size, size), jnp.float32),
        in_specs=[pl.BlockSpec((size * tiles * 2, LANES), lambda m: (m, 0))],
        out_specs=pl.BlockSpec((1, 2, size, size), lambda m: (m, 0, 0, 0)),
        cost_estimate=pl.CostEstimate(flops=1 << 20, bytes_accessed=4 << 20, transcendentals=0),
        name="probes",
    )(x)


def tiled(x):
    *lead, two, width = x.shape
    n = math.prod(lead)
    x = x.reshape(n, two, width // LANES, LANES)
    return jnp.transpose(x, (0, 2, 1, 3)).reshape(-1, LANES)


def untiled(x, lead, width):
    n = math.prod(lead)
    x = jnp.transpose(x.reshape(n, width // LANES, 2, LANES), (0, 2, 1, 3))
    return x.reshape(*lead, 2, width)


def shards(object_tiles, probe, measured, offset_row, offset_col, subpixel, live_count):
    rows, _, width = object_tiles.shape
    modes, size = probe.shape[:2]
    slots = measured.shape[0]
    lines, tiles = width // LANES, size // LANES
    mid = lines // 2
    near = mid + tiles
    own_a, own_b = sorted_planes(tiled(object_tiles), rows, lines, near)
    rim_a = passed_along(own_a[:, :, :size], "row", -1)
    rim_b = passed_along(own_b[:, :, :size], "row", -1)
    planes = probe_planes(tiled(probe), modes, size)
    common = (live_count, offset_row, offset_col, subpixel, planes, measured, dft_tables(size))
    whole = (0, near, 0)
    grad_a, below_a, sum_a, moved_a, over = step(
        modes, size, rows, slots, 0, 0, mid, mid, near, [(own_a, whole)], [(rim_a, whole)], (), common
    )
    landed_a = passed_along(below_a, "row", 1, odd=True)
    kept, rest = (mid, near, 0), (0, lines - near, tiles)
    grad_b, below_b, sums, moved = step(
        modes, size, rows, slots, mid, mid, lines, lines - mid, lines - mid,
        [(own_a, kept), (own_b, rest)], [(rim_a, kept), (rim_b, rest)], (over, sum_a, moved_a), common,
    )
    probe_grad, grad, landed = summed(
        sums.reshape(-1, LANES), (grad_a, grad_b), landed_a, below_a, below_b, modes, tiles, "row"
    )
    grad = grad + landed.astype(jnp.float32)
    return (untiled(grad, (rows,), width), untiled(probe_grad, (modes, size), size), moved)


def solution(mesh):
    in_specs = (
        P(("groups", "row"), None, None),
        P(),
        P(("groups", "row"), None, None),
        P(("groups", "row")),
        P(("groups", "row")),
        P(("groups", "row")),
        P(("groups", "row")),
    )
    out_specs = (
        P(("groups", "row"), None, None),
        P("groups", None, None, None),
        P(None, ("groups", "row")),
    )
    return jax.shard_map(shards, mesh=mesh, in_specs=in_specs, out_specs=out_specs, check_vma=False)
```

```python
import functools
import math

import jax
import jax.numpy as jnp
import numpy as np
from jax import lax
from jax.experimental import pallas as pl
from jax.experimental.pallas import tpu as pltpu
from jax.sharding import PartitionSpec as P

LANES = 128
ROWS = 16


def passed_along(x, axis, by, odd=False):
    length = lax.axis_size(axis)
    pairs = [(i, i + by) for i in range(odd, length, 1 + odd) if 0 <= i + by < length]
    return lax.ppermute(x, axis, pairs)


def total_kernel(
    length, pieces, modes, tiles, x_ref, part_a, part_b, above_ref, below_ref, out_ref, grad_ref, came_a, came_b,
    near, send1, send2, got0, got1, got2, full, flat, temp, sends, recvs, down_sems,
):
    f32, bf16 = jnp.float32, jnp.bfloat16
    lines, width = x_ref.shape
    deep = length // 4
    me = lax.axis_index("row")
    c, b, k = me % 2, (me // 2) % 2, me // 4
    part = lines // pieces
    half, quarter = part // 2, part // 4
    leaf = quarter // deep

    def stage_near(q):
        near[pl.ds(q * half, half)] = x_ref[
            pl.ds(pl.multiple_of(q * part + (1 - c) * half, ROWS), half)
        ].astype(bf16)

    def peer(stage, o):
        if stage in (0, 5):
            return {"row": me + 1 - 2 * c}
        if stage in (1, 4):
            return {"row": me + 2 - 4 * b}
        return {"row": ((k + o) % deep) * 4 + me % 4}

    barrier = pltpu.get_barrier_semaphore()
    others = [(0, 0), (1, 0)] + [(2, o) for o in range(1, deep)]
    for stage, o in others:
        pl.semaphore_signal(barrier, inc=1, device_id=peer(stage, o), device_id_type=pl.DeviceIdType.MESH)

    @pl.when(me > 0)
    def _():
        pl.semaphore_signal(barrier, inc=1, device_id={"row": me - 1}, device_id_type=pl.DeviceIdType.MESH)

    @pl.when(me < length - 1)
    def _():
        pl.semaphore_signal(barrier, inc=1, device_id={"row": me + 1}, device_id_type=pl.DeviceIdType.MESH)

    for q in range(pieces):
        stage_near(q)

    @pl.when(c == 0)
    def _():
        came_a[...] = jnp.zeros_like(came_a)

    @pl.when(me == 0)
    def _():
        came_b[...] = jnp.zeros_like(came_b)

    pl.semaphore_wait(
        barrier, len(others) + (me > 0).astype(jnp.int32) + (me < length - 1).astype(jnp.int32)
    )
    early = flat.shape[0] // 8 * 5
    downs = []
    for n, (src, dst, first, last) in enumerate((
        (flat, came_b, 0, early),
        (flat, came_b, early, flat.shape[0]),
        (above_ref, came_a, 0, above_ref.shape[0]),
    )):
        at = pl.ds(first, last - first)
        downs.append(pltpu.make_async_remote_copy(
            src_ref=src.at[at], dst_ref=dst.at[at],
            send_sem=down_sems.at[n], recv_sem=down_sems.at[3 + n],
            device_id={"row": jnp.minimum(me + 1, length - 1)}, device_id_type=pl.DeviceIdType.MESH,
        ))

    def send_down(n):
        @pl.when((c == 0) if n == 2 else (me < length - 1))
        def _():
            downs[n].start()

    whole = 2 * (part_a.shape[0] + part_b.shape[0])
    block = 32

    def lay_out(part, out, first, line):
        many = part.shape[0]

        @pl.loop(0, part.shape[2] // block)
        def _(i):
            at = pl.multiple_of(i * block, block)
            for t in range(many):
                for p in range(2):
                    temp[pl.ds(2 * t + p, block, stride=2 * many + 1), :] = part[t, p, pl.ds(at, block), :].astype(f32)
            for y in range(block):
                out[pl.ds(pl.multiple_of((at + y) * line + 2 * first, ROWS), 2 * many), :] = temp[
                    y * (2 * many + 1) : y * (2 * many + 1) + 2 * many, :
                ].astype(out.dtype)

    base = [0, pieces, 2 * pieces, (2 + deep) * pieces, (2 + 2 * deep) * pieces, (3 + 2 * deep) * pieces]

    def span_of(start, size):
        return pl.ds(pl.multiple_of(start, ROWS), size)

    def place(q, stage):
        start = q * part
        if stage == 0:
            return start
        start = start + c * half
        if stage == 1:
            return start
        start = start + b * quarter
        return start if stage == 2 else start + k * leaf

    def link(stage, q, o=0):
        at = span_of(q * quarter, quarter)
        if stage == 0:
            src, dst = near.at[span_of(q * half, half)], got0.at[span_of(q * half, half)]
        elif stage == 1:
            src, dst = send1.at[at], got1.at[at]
        elif stage == 2:
            src = send2.at[span_of(q * quarter + ((k + o) % deep) * leaf, leaf)]
            dst = got2.at[span_of((q * deep + o) * leaf, leaf)]
        elif stage == 3:
            src = dst = full.at[span_of(place(q, 3), leaf)]
        elif stage == 4:
            src = dst = full.at[span_of(place(q, 2), quarter)]
        else:
            src = dst = full.at[span_of(place(q, 1), half)]
        sem = base[stage] + (q * deep + o if stage in (2, 3) else q)
        return pltpu.make_async_remote_copy(
            src_ref=src, dst_ref=dst, send_sem=sends.at[sem], recv_sem=recvs.at[sem],
            device_id=peer(stage, o), device_id_type=pl.DeviceIdType.MESH,
        )

    started = []

    def begin(stage, q):
        for o in range(1, deep) if stage in (2, 3) else (0,):
            copy = link(stage, q, o)
            copy.start()
            started.append(copy)

    def arrive(stage, q):
        for o in range(1, deep) if stage in (2, 3) else (0,):
            link(stage, q, o).wait_recv()

    def act(stage, q):
        if stage == 0:
            pass
        elif stage == 1:
            arrive(0, q)
            away = q * part + c * half + (1 - b) * quarter
            send1[span_of(q * quarter, quarter)] = (
                x_ref[span_of(away, quarter)] + got0[span_of(q * half + (1 - b) * quarter, quarter)].astype(f32)
            ).astype(bf16)
        elif stage == 2:
            arrive(1, q)
            own = (
                x_ref[span_of(place(q, 2), quarter)]
                + got0[span_of(q * half + b * quarter, quarter)].astype(f32)
                + got1[span_of(q * quarter, quarter)].astype(f32)
            )
            send2[span_of(q * quarter, quarter)] = own.astype(bf16)
        elif stage == 3:
            arrive(2, q)
            own = (
                x_ref[span_of(place(q, 3), leaf)]
                + got0[span_of(q * half + b * quarter + k * leaf, leaf)].astype(f32)
                + got1[span_of(q * quarter + k * leaf, leaf)].astype(f32)
            )
            for o in range(1, deep):
                own = own + got2[span_of((q * deep + o) * leaf, leaf)].astype(f32)
            full[span_of(place(q, 3), leaf)] = own.astype(bf16)
        elif stage == 6:
            arrive(5, q)
            planes = modes * 2 * tiles
            size = lines // planes
            for plane in range(planes * q // pieces, planes * (q + 1) // pieces):
                m, p, tile = plane // (2 * tiles), plane // tiles % 2, plane % tiles
                out_ref[pl.ds((m * size * tiles + tile) * 2 + p, size, stride=2 * tiles), :] = full[
                    pl.ds(plane * size, size), :
                ].astype(f32)
            return
        else:
            arrive(stage - 1, q)
        begin(stage, q)

    for q in range(pieces):
        act(0, q)
    for stage in range(1, 7):
        for q in range(pieces):
            act(stage, q)
        if stage == 1:
            send_down(2)
            lay_out(below_ref, flat, 0, 2 * below_ref.shape[0])
            send_down(0)
        elif stage == 2:
            lay_out(part_a, grad_ref, 0, whole)
        elif stage == 3:
            lay_out(part_b, grad_ref, part_a.shape[0], whole)
        elif stage == 4:
            send_down(1)
    for copy in started:
        copy.wait_send()

    @pl.when(c == 0)
    def _():
        downs[2].wait_send()

    @pl.when(c == 1)
    def _():
        downs[2].wait_recv()

    for n in range(2):

        @pl.when(me < length - 1)
        def _():
            downs[n].wait_send()

        @pl.when(me > 0)
        def _():
            downs[n].wait_recv()


def summed(x, grads, above, below, modes, tiles, axis):
    length = lax.axis_size(axis)
    lines, width = x.shape
    f32, bf16 = jnp.float32, jnp.bfloat16
    pieces = next(n for n in (4, 2, 1) if n == 1 or lines % (length * ROWS * n) == 0)
    vmem = pl.BlockSpec(memory_space=pltpu.VMEM)
    count = pieces * (4 + 2 * (length // 4))
    total = 2 * grads[0].shape[2] * (grads[0].shape[0] + grads[1].shape[0])
    flat = (2 * below.shape[2] * below.shape[0], width)
    return pl.pallas_call(
        functools.partial(total_kernel, length, pieces, modes, tiles),
        out_shape=(
            jax.ShapeDtypeStruct((lines, width), f32),
            jax.ShapeDtypeStruct((total, width), f32),
            jax.ShapeDtypeStruct(above.shape, bf16),
            jax.ShapeDtypeStruct(flat, bf16),
        ),
        in_specs=[vmem] * 5,
        out_specs=(vmem,) * 4,
        scratch_shapes=[
            pltpu.VMEM((lines // 2, width), bf16),
            pltpu.VMEM((lines // 4, width), bf16),
            pltpu.VMEM((lines // 4, width), bf16),
            pltpu.VMEM((lines // 2, width), bf16),
            pltpu.VMEM((lines // 4, width), bf16),
            pltpu.VMEM((lines // 4, width), bf16),
            pltpu.VMEM((lines, width), bf16),
            pltpu.VMEM(flat, bf16),
            pltpu.VMEM((32 * (2 * max(g.shape[0] for g in grads) + 1) + 7, width), f32),
            pltpu.SemaphoreType.DMA((count,)),
            pltpu.SemaphoreType.DMA((count,)),
            pltpu.SemaphoreType.DMA((6,)),
        ],
        compiler_params=pltpu.CompilerParams(collective_id=0, has_side_effects=True, vmem_limit_bytes=28 << 20),
        name="total",
    )(x, *grads, above, below)


def dft_tables(patch):
    index = np.arange(patch)
    angle = ((index[:, None] * index[None, :]) % patch).astype(np.float64) * (2.0 * math.pi / patch)
    scale = 1.0 / math.sqrt(patch)
    cosine, sine = np.cos(angle) * scale, np.sin(angle) * scale
    half = patch // 2
    tables = []
    for odd in range(2):
        c, s = cosine[:half, odd::2], sine[:half, odd::2]
        tables.append(np.block([[c, -s], [s, c]]))
        tables.append(np.block([[c.T, s.T], [-s.T, c.T]]))
    order = np.concatenate([index[0::2], index[1::2]])
    tables.append((index[:, None] == order[None, :]).astype(np.float64))
    stacked = np.stack(tables).astype(np.float32)
    return jnp.asarray(stacked).astype(jnp.bfloat16)


def step_kernel(
    modes, size, rows, first_tile, low, high, keep, own_parts, rim_parts, carried, *refs
):
    f32, bf16 = jnp.float32, jnp.bfloat16
    refs = list(refs)

    def take(n):
        got, refs[:] = refs[:n], refs[n:]
        return got

    count_ref, top_ref, left_ref, code_ref = take(4)
    probe_hbm, measured_hbm, table_hbm = take(3)
    owns, rims = take(len(own_parts)), take(len(rim_parts))
    if carried:
        handed_hbm, sum_hbm, before_ref = take(3)
    grad_hbm, below_ref, pgrad, moved_ref = take(4)
    over_hbm = None if carried else take(1)[0]
    (ext, acc, probe, measured_ref, table_ref, rowx, slope, patch, waves, mids, far, power, ratios, meas, gs,
     temp, sems, out_sems) = refs
    tiles = size // LANES
    half = size // 2
    slots = measured_ref.shape[0]
    span = 32
    along, inverse_of = (0, 2), (1, 3)
    copies = []

    def fetch(src, dst):
        copy = pltpu.make_async_copy(src, dst, sems.at[len(copies)])
        copy.start()
        copies.append(copy)

    for sources, ranges, row, n in ((owns, own_parts, 0, rows), (rims, rim_parts, rows, size)):
        for source, (start, stop, to) in zip(sources, ranges):
            fetch(
                source.at[pl.ds(start, stop - start)],
                ext.at[pl.ds(to, stop - start), :, pl.ds(row, n), :],
            )
    fetch(probe_hbm, probe)
    fetch(measured_hbm, measured_ref)
    fetch(table_hbm, table_ref)
    overlap = 0
    if carried:
        overlap = handed_hbm.shape[0]
        fetch(handed_hbm, acc.at[pl.ds(0, overlap)])
        fetch(sum_hbm, pgrad)
    else:
        pgrad[...] = jnp.zeros_like(pgrad)
    gs[...] = jnp.zeros_like(gs)

    @pl.loop(overlap, acc.shape[0])
    def _(k):
        for p in range(2):
            acc[k, p] = jnp.zeros(acc.shape[2:], f32)

    for j in range(slots):
        for p in range(2):
            moved_ref[p, j] = before_ref[p, j] if carried else 0.0
    for copy in copies:
        copy.wait()

    def one(j):
        top, left, code = top_ref[j], left_ref[j], code_ref[j]
        first = left // LANES
        col = left - first * LANES
        first = first - first_tile
        base_row = pl.multiple_of(top // ROWS * ROWS, ROWS)
        row = top - base_row
        fy = (code // 4).astype(f32) * 0.25
        fx = (code % 4).astype(f32) * 0.25
        reach = (tiles + 1) * LANES
        tall = size + ROWS
        here = lax.broadcasted_iota(jnp.int32, (reach, size), 0)
        away = here - lax.broadcasted_iota(jnp.int32, (reach, size), 1) - col
        at_left, at_right = (away == 0).astype(f32), (away == 1).astype(f32)
        mix = ((1.0 - fx) * at_left + fx * at_right).astype(bf16)
        tilt = (at_right - at_left).astype(bf16)
        for p in range(2):
            window = jnp.concatenate(
                [ext[first + k, p, pl.ds(base_row, tall), :] for k in range(tiles + 1)], axis=1
            )
            for table, kept in ((mix, rowx), (tilt, slope)):
                cells = jnp.dot(window, table, preferred_element_type=f32)
                for k in range(tiles):
                    kept[p, k, 0:tall, :] = cells[:, k * LANES : (k + 1) * LANES]
        for p in range(2):
            for k in range(tiles):
                for i in range(size // span):
                    upper = rowx[p, k, pl.ds(row + i * span, span), :]
                    lower = rowx[p, k, pl.ds(row + i * span + 1, span), :]
                    patch[p, i * span : (i + 1) * span, k * LANES : (k + 1) * LANES] = upper + fy * (lower - upper)

        ordered = jnp.dot(measured_ref[j], table_ref[4], preferred_element_type=f32)
        for k in range(tiles):
            meas[k] = ordered[:, k * LANES : (k + 1) * LANES]

        share = size // modes
        short = share // 2

        def wave(c):
            for h in range(2):
                at = slice(h * half + c * short, h * half + (c + 1) * short)
                re, im = patch[0, at, :], patch[1, at, :]
                for m in range(modes):
                    here = slice(m * share + h * short, m * share + (h + 1) * short)
                    pr, pi = probe[m, 0, at, :], probe[m, 1, at, :]
                    for q, w in enumerate((pr * re - pi * im, pr * im + pi * re)):
                        to = slice(q * half, (q + 1) * half)
                        waves[0, c, here, to] = (w[:, :half] + w[:, half:]).astype(bf16)
                        waves[1, c, here, to] = (w[:, :half] - w[:, half:]).astype(bf16)

        def along_columns(c):
            for e in range(2):
                h = jnp.dot(waves[e, c], table_ref[along[e]], preferred_element_type=f32)
                to = slice(e * half, (e + 1) * half)
                for m in range(modes):
                    for q in range(2):
                        upper = h[m * share : m * share + short, q * half : (q + 1) * half]
                        lower = h[m * share + short : (m + 1) * share, q * half : (q + 1) * half]
                        at = slice(q * half + c * short, q * half + (c + 1) * short)
                        mids[m, 0, at, to] = (upper + lower).astype(bf16)
                        mids[m, 1, at, to] = (upper - lower).astype(bf16)

        def along_rows(m):
            for e in range(2):
                f = jnp.dot(table_ref[inverse_of[e]], mids[m, e], preferred_element_type=f32)
                far[m, e] = f.astype(far.dtype)
                strength = f[:half] * f[:half] + f[half:] * f[half:]
                if m == 0:
                    power[e] = strength
                else:
                    power[e] += strength

        def skewed(*stages):
            for t in range(modes + len(stages) - 1):
                for n in reversed(range(len(stages))):
                    if 0 <= t - n < modes:
                        stages[n](t - n)

        skewed(wave, along_columns)
        skewed(along_rows)

        for e in range(2):
            for k in range(tiles):
                to = slice(k * LANES, (k + 1) * LANES)
                amplitude = meas[k, pl.ds(e, half, stride=2), :]
                ratio = 1.0 - amplitude * jnp.minimum(lax.rsqrt(power[e, :, to]), 2.0)
                ratios[e, :, to] = ratio.astype(bf16)

        def error(m):
            for e in range(2):
                ratio = ratios[e]
                mids[m, e, 0:half, :] = far[m, e, 0:half, :] * ratio
                mids[m, e, half:size, :] = far[m, e, half:size, :] * ratio

        def back_rows(m):
            parts = [jnp.dot(table_ref[along[e]], mids[m, e], preferred_element_type=f32) for e in range(2)]
            for h, both in enumerate((parts[0] + parts[1], parts[0] - parts[1])):
                for e in range(2):
                    for q in range(2):
                        to, at = slice(q * half, (q + 1) * half), slice(e * half, (e + 1) * half)
                        for n in range(half // share):
                            waves[e, h * (half // share) + n, m * share : (m + 1) * share, to] = both[
                                q * half + n * share : q * half + (n + 1) * share, at
                            ].astype(bf16)

        def back_columns(c):
            back = [jnp.dot(waves[e, c], table_ref[inverse_of[e]], preferred_element_type=f32) for e in range(2)]
            for i in range(share // span):
                start = c * share + i * span
                at = slice(start, start + span)
                for k in range(2):
                    to = slice(k * half, (k + 1) * half)
                    re, im = patch[0, at, to], patch[1, at, to]
                    sums = [0.0, 0.0]
                    for m in range(modes):
                        here = slice(m * share + i * span, m * share + (i + 1) * span)
                        b0, b1 = back[0][here], back[1][here]
                        mixed = b0 + b1 if k == 0 else b0 - b1
                        ur, ui = mixed[:, :half], mixed[:, half:]
                        pr, pi = probe[m, 0, at, to], probe[m, 1, at, to]
                        sums[0] = sums[0] + (pr * ur + pi * ui)
                        sums[1] = sums[1] + (pr * ui - pi * ur)
                        pgrad[m, 0, k, at, :] += re * ur + im * ui
                        pgrad[m, 1, k, at, :] += re * ui - im * ur
                    for p in range(2):
                        gs[p, k, 8 + start : 8 + start + span, :] = sums[p]

        skewed(error, back_rows)
        skewed(back_columns)

        down, across = jnp.zeros((8, LANES), f32), jnp.zeros((8, LANES), f32)
        for i in range(size // span):
            for p in range(2):
                for k in range(tiles):
                    at, after = pl.ds(row + i * span, span), pl.ds(row + i * span + 1, span)
                    g = gs[p, k, 8 + i * span : 8 + (i + 1) * span, :]
                    dy = g * (rowx[p, k, after, :] - rowx[p, k, at, :])
                    upper = slope[p, k, at, :]
                    dx = g * (upper + fy * (slope[p, k, after, :] - upper))
                    down = down + jnp.sum(dy.reshape(span // 8, 8, LANES), 0)
                    across = across + jnp.sum(dx.reshape(span // 8, 8, LANES), 0)
        moved_ref[0, j] = jnp.sum(down) / size
        moved_ref[1, j] = jnp.sum(across) / size

        base = pl.multiple_of(top // 8 * 8, 8)
        lag = top - base

        there = lax.broadcasted_iota(jnp.int32, (size, reach), 1)
        gone = there - lax.broadcasted_iota(jnp.int32, (size, reach), 0) - col
        spread = ((1.0 - fx) * (gone == 0).astype(f32) + fx * (gone == 1).astype(f32)).astype(bf16)
        for p in range(2):
            g = []
            for k in range(tiles):
                here = gs[p, k, pl.ds(8 - lag, tall), :]
                before = gs[p, k, pl.ds(7 - lag, tall), :]
                g.append((here + fy * (before - here)).astype(bf16))
            wide = jnp.dot(jnp.concatenate(g, axis=1), spread, preferred_element_type=f32)
            for k in range(tiles + 1):
                acc[first + k, p, pl.ds(base, tall), :] += wide[:, k * LANES : (k + 1) * LANES]

    @pl.loop(0, count_ref[0])
    def _(j):
        tile = left_ref[j] // LANES

        @pl.when((tile >= low) & (tile < high))
        def _():
            one(j)

    outs = [
        pltpu.make_async_copy(acc.at[pl.ds(0, keep), :, pl.ds(0, rows), :], grad_hbm, out_sems.at[0]),
    ]
    if not carried:
        outs.append(pltpu.make_async_copy(acc.at[pl.ds(keep, over_hbm.shape[0])], over_hbm, out_sems.at[2]))
    for out in outs:
        out.start()

    if carried:

        @pl.loop(0, keep)
        def _(k):
            for p in range(2):
                below_ref[k, p] = acc[k, p, rows : rows + size, :].astype(bf16)

    else:

        @pl.loop(0, size // span)
        def _(i):
            at = pl.multiple_of(i * span, span)
            for k in range(keep):
                for p in range(2):
                    temp[pl.ds(2 * k + p, span, stride=2 * keep + 1), :] = acc[k, p, pl.ds(rows + at, span), :]
            for y in range(span):
                below_ref[pl.ds(pl.multiple_of((at + y) * 2 * keep, ROWS), 2 * keep), :] = temp[
                    y * (2 * keep + 1) : y * (2 * keep + 1) + 2 * keep, :
                ].astype(bf16)

    for out in outs:
        out.wait()


def step(modes, size, rows, slots, first_tile, low, high, keep, count, own, rim, carried, common):
    f32, bf16 = jnp.float32, jnp.bfloat16
    tiles = size // LANES
    deep = rows + size + 8
    vmem = pl.BlockSpec(memory_space=pltpu.VMEM)
    smem = pl.BlockSpec(memory_space=pltpu.SMEM)
    hbm = pl.BlockSpec(memory_space=pl.ANY)
    planes = (modes, 2, tiles, size, LANES)
    out_shape = [
        jax.ShapeDtypeStruct((keep, 2, rows, LANES), f32),
        jax.ShapeDtypeStruct((keep, 2, size, LANES) if carried else (2 * keep * size, LANES), bf16),
        jax.ShapeDtypeStruct(planes, f32),
        jax.ShapeDtypeStruct((2, slots), f32),
    ]
    out_specs = [hbm, vmem, vmem, smem]
    if not carried:
        out_shape.append(jax.ShapeDtypeStruct((count - keep, 2, deep, LANES), f32))
        out_specs.append(hbm)
    own_arrays, own_parts = zip(*own)
    rim_arrays, rim_parts = zip(*rim)
    return pl.pallas_call(
        functools.partial(
            step_kernel, modes, size, rows, first_tile, low, high, keep, own_parts, rim_parts, bool(carried)
        ),
        out_shape=tuple(out_shape),
        in_specs=[smem] * 4 + [hbm] * (3 + len(own) + len(rim)) + ([hbm, hbm, smem] if carried else []),
        out_specs=tuple(out_specs),
        scratch_shapes=[
            pltpu.VMEM((count, 2, rows + size, LANES), bf16),
            pltpu.VMEM((count, 2, deep, LANES), f32),
            pltpu.VMEM((modes, 2, size, size), f32),
            pltpu.VMEM((slots, size, size), bf16),
            pltpu.VMEM((5, size, size), bf16),
            pltpu.VMEM((2, tiles, size + 32, LANES), f32),
            pltpu.VMEM((2, tiles, size + 32, LANES), f32),
            pltpu.VMEM((2, size, size), f32),
            pltpu.VMEM((2, modes, size, size), bf16),
            pltpu.VMEM((modes, 2, size, size), bf16),
            pltpu.VMEM((modes, 2, size, size), bf16),
            pltpu.VMEM((2, size // 2, size), f32),
            pltpu.VMEM((2, size // 2, size), bf16),
            pltpu.VMEM((tiles, size, LANES), f32),
            pltpu.VMEM((2, tiles, size + 32, LANES), f32),
            pltpu.VMEM((32 * (2 * keep + 1) + 7, LANES), f32),
            pltpu.SemaphoreType.DMA((12,)),
            pltpu.SemaphoreType.DMA((3,)),
        ],
        compiler_params=pltpu.CompilerParams(vmem_limit_bytes=30 << 20),
        cost_estimate=pl.CostEstimate(flops=3 << 30, bytes_accessed=16 << 20, transcendentals=0),
        name="step_b" if carried else "step_a",
    )(*common, *own_arrays, *rim_arrays, *carried)


def sort_kernel(lines, first, x_ref, out_ref, temp):
    n = out_ref.shape[2]
    line = 2 * lines
    for y in range(n):
        temp[y * (line + 1) : y * (line + 1) + line, :] = x_ref[y * line : (y + 1) * line, :].astype(jnp.float32)
    for k in range(out_ref.shape[0]):
        for p in range(2):
            out_ref[k, p] = temp[pl.ds(2 * (first + k) + p, n, stride=line + 1), :].astype(jnp.bfloat16)


def sorted_planes(x, rows, lines, first, last):
    n = 64
    return pl.pallas_call(
        functools.partial(sort_kernel, lines, first),
        grid=(rows // n,),
        out_shape=jax.ShapeDtypeStruct((last - first, 2, rows, LANES), jnp.bfloat16),
        in_specs=[pl.BlockSpec((n * lines * 2, LANES), lambda i: (i, 0))],
        out_specs=pl.BlockSpec((last - first, 2, n, LANES), lambda i: (0, 0, i, 0)),
        scratch_shapes=[pltpu.VMEM((n * (lines * 2 + 1) + 7, LANES), jnp.float32)],
        cost_estimate=pl.CostEstimate(flops=1 << 20, bytes_accessed=4 << 20, transcendentals=0),
        name="sort",
    )(x)


def probe_kernel(tiles, x_ref, table_ref, out_ref, table_out):
    modes, _, size, _ = out_ref.shape
    span = 32
    table_out[...] = table_ref[...]

    @pl.loop(0, modes * (size // span))
    def _(i):
        at = pl.multiple_of(lax.rem(i, size // span) * span, span)
        m = i // (size // span)
        for p in range(2):
            for k in range(tiles):
                out_ref[m, p, pl.ds(at, span), k * LANES : (k + 1) * LANES] = x_ref[
                    pl.ds((i * span * tiles + k) * 2 + p, span, stride=2 * tiles), :
                ]


def probe_planes(x, tables, modes, size):
    vmem = pl.BlockSpec(memory_space=pltpu.VMEM)
    return pl.pallas_call(
        functools.partial(probe_kernel, size // LANES),
        out_shape=(
            jax.ShapeDtypeStruct((modes, 2, size, size), jnp.float32),
            jax.ShapeDtypeStruct(tables.shape, tables.dtype),
        ),
        in_specs=[vmem, vmem],
        out_specs=(vmem, vmem),
        compiler_params=pltpu.CompilerParams(vmem_limit_bytes=16 << 20),
        cost_estimate=pl.CostEstimate(flops=1 << 20, bytes_accessed=8 << 20, transcendentals=0),
        name="probes",
    )(x, tables)


def tiled(x):
    *lead, two, width = x.shape
    n = math.prod(lead)
    x = x.reshape(n, two, width // LANES, LANES)
    return jnp.transpose(x, (0, 2, 1, 3)).reshape(-1, LANES)


def untiled(x, lead, width):
    n = math.prod(lead)
    x = jnp.transpose(x.reshape(n, width // LANES, 2, LANES), (0, 2, 1, 3))
    return x.reshape(*lead, 2, width)


def shards(object_tiles, probe, measured, offset_row, offset_col, subpixel, live_count):
    rows, _, width = object_tiles.shape
    modes, size = probe.shape[:2]
    slots = measured.shape[0]
    lines, tiles = width // LANES, size // LANES
    mid = lines // 2
    near = mid + tiles
    own = tiled(object_tiles)
    own_a = sorted_planes(own, rows, lines, 0, near)
    own_b = sorted_planes(own, rows, lines, near, lines)
    rim_a = passed_along(own_a[:, :, :size], "row", -1)
    rim_b = passed_along(own_b[:, :, :size], "row", -1)
    planes, tables = probe_planes(tiled(probe), dft_tables(size), modes, size)
    common = (live_count, offset_row, offset_col, subpixel, planes, measured, tables)
    whole = (0, near, 0)
    grad_a, below_a, sum_a, moved_a, over = step(
        modes, size, rows, slots, 0, 0, mid, mid, near, [(own_a, whole)], [(rim_a, whole)], (), common
    )
    landed_a = passed_along(below_a, "row", 1, odd=True)
    kept, rest = (mid, near, 0), (0, lines - near, tiles)
    grad_b, below_b, sums, moved = step(
        modes, size, rows, slots, mid, mid, lines, lines - mid, lines - mid,
        [(own_a, kept), (own_b, rest)], [(rim_a, kept), (rim_b, rest)], (over, sum_a, moved_a), common,
    )
    probe_grad, grad, core_a, landed_b = summed(
        sums.reshape(-1, LANES), (grad_a, grad_b), below_a, below_b, modes, tiles, "row"
    )
    landed = jnp.concatenate(
        [(landed_a + core_a).reshape(size, 2 * mid, LANES), landed_b.reshape(size, 2 * (lines - mid), LANES)], axis=1
    ).astype(jnp.float32)
    grad = grad.reshape(rows, 2 * lines, LANES).at[:size].add(landed).reshape(-1, LANES)
    return (untiled(grad, (rows,), width), untiled(probe_grad, (modes, size), size), moved)


def solution(mesh):
    in_specs = (
        P(("groups", "row"), None, None),
        P(),
        P(("groups", "row"), None, None),
        P(("groups", "row")),
        P(("groups", "row")),
        P(("groups", "row")),
        P(("groups", "row")),
    )
    out_specs = (
        P(("groups", "row"), None, None),
        P("groups", None, None, None),
        P(None, ("groups", "row")),
    )
    return jax.shard_map(shards, mesh=mesh, in_specs=in_specs, out_specs=out_specs, check_vma=False)
```

```python
import functools
import math

import jax
import jax.numpy as jnp
import numpy as np
from jax import lax
from jax.experimental import pallas as pl
from jax.experimental.pallas import tpu as pltpu
from jax.sharding import PartitionSpec as P

LANES = 128
ROWS = 16


def passed_along(x, axis, by, odd=False):
    length = lax.axis_size(axis)
    pairs = [(i, i + by) for i in range(odd, length, 1 + odd) if 0 <= i + by < length]
    return lax.ppermute(x, axis, pairs)


def total_kernel(
    length, pieces, modes, tiles, x_ref, part_a, part_b, above_ref, below_ref, out_ref, grad_ref, came_a, came_b,
    near, send1, send2, got0, got1, got2, full, flat, temp, sends, recvs, down_sems,
):
    f32, bf16 = jnp.float32, jnp.bfloat16
    lines, width = x_ref.shape
    deep = length // 4
    me = lax.axis_index("row")
    c, b, k = me % 2, (me // 2) % 2, me // 4
    part = lines // pieces
    half, quarter = part // 2, part // 4
    leaf = quarter // deep

    def stage_near(q):
        near[pl.ds(q * half, half)] = x_ref[
            pl.ds(pl.multiple_of(q * part + (1 - c) * half, ROWS), half)
        ].astype(bf16)

    def peer(stage, o):
        if stage in (0, 5):
            return {"row": me + 1 - 2 * c}
        if stage in (1, 4):
            return {"row": me + 2 - 4 * b}
        return {"row": ((k + o) % deep) * 4 + me % 4}

    barrier = pltpu.get_barrier_semaphore()
    others = [(0, 0), (1, 0)] + [(2, o) for o in range(1, deep)]
    for stage, o in others:
        pl.semaphore_signal(barrier, inc=1, device_id=peer(stage, o), device_id_type=pl.DeviceIdType.MESH)

    @pl.when(me > 0)
    def _():
        pl.semaphore_signal(barrier, inc=1, device_id={"row": me - 1}, device_id_type=pl.DeviceIdType.MESH)

    @pl.when(me < length - 1)
    def _():
        pl.semaphore_signal(barrier, inc=1, device_id={"row": me + 1}, device_id_type=pl.DeviceIdType.MESH)

    for q in range(pieces):
        stage_near(q)

    @pl.when(c == 0)
    def _():
        came_a[...] = jnp.zeros_like(came_a)

    @pl.when(me == 0)
    def _():
        came_b[...] = jnp.zeros_like(came_b)

    pl.semaphore_wait(
        barrier, len(others) + (me > 0).astype(jnp.int32) + (me < length - 1).astype(jnp.int32)
    )
    early = flat.shape[0] // 8 * 5
    downs = []
    for n, (src, dst, first, last) in enumerate((
        (flat, came_b, 0, early),
        (flat, came_b, early, flat.shape[0]),
        (above_ref, came_a, 0, above_ref.shape[0]),
    )):
        at = pl.ds(first, last - first)
        downs.append(pltpu.make_async_remote_copy(
            src_ref=src.at[at], dst_ref=dst.at[at],
            send_sem=down_sems.at[n], recv_sem=down_sems.at[3 + n],
            device_id={"row": jnp.minimum(me + 1, length - 1)}, device_id_type=pl.DeviceIdType.MESH,
        ))

    def send_down(n):
        @pl.when((c == 0) if n == 2 else (me < length - 1))
        def _():
            downs[n].start()

    whole = 2 * (part_a.shape[0] + part_b.shape[0])
    block = 32

    def lay_out(part, out, first, line):
        many = part.shape[0]

        @pl.loop(0, part.shape[2] // block)
        def _(i):
            at = pl.multiple_of(i * block, block)
            for t in range(many):
                for p in range(2):
                    temp[pl.ds(2 * t + p, block, stride=2 * many + 1), :] = part[t, p, pl.ds(at, block), :].astype(f32)
            for y in range(block):
                out[pl.ds(pl.multiple_of((at + y) * line + 2 * first, ROWS), 2 * many), :] = temp[
                    y * (2 * many + 1) : y * (2 * many + 1) + 2 * many, :
                ].astype(out.dtype)

    base = [0, pieces, 2 * pieces, (2 + deep) * pieces, (2 + 2 * deep) * pieces, (3 + 2 * deep) * pieces]

    def span_of(start, size):
        return pl.ds(pl.multiple_of(start, ROWS), size)

    def place(q, stage):
        start = q * part
        if stage == 0:
            return start
        start = start + c * half
        if stage == 1:
            return start
        start = start + b * quarter
        return start if stage == 2 else start + k * leaf

    def link(stage, q, o=0):
        at = span_of(q * quarter, quarter)
        if stage == 0:
            src, dst = near.at[span_of(q * half, half)], got0.at[span_of(q * half, half)]
        elif stage == 1:
            src, dst = send1.at[at], got1.at[at]
        elif stage == 2:
            src = send2.at[span_of(q * quarter + ((k + o) % deep) * leaf, leaf)]
            dst = got2.at[span_of((q * deep + o) * leaf, leaf)]
        elif stage == 3:
            src = dst = full.at[span_of(place(q, 3), leaf)]
        elif stage == 4:
            src = dst = full.at[span_of(place(q, 2), quarter)]
        else:
            src = dst = full.at[span_of(place(q, 1), half)]
        sem = base[stage] + (q * deep + o if stage in (2, 3) else q)
        return pltpu.make_async_remote_copy(
            src_ref=src, dst_ref=dst, send_sem=sends.at[sem], recv_sem=recvs.at[sem],
            device_id=peer(stage, o), device_id_type=pl.DeviceIdType.MESH,
        )

    started = []

    def begin(stage, q):
        for o in range(1, deep) if stage in (2, 3) else (0,):
            copy = link(stage, q, o)
            copy.start()
            started.append(copy)

    def arrive(stage, q):
        for o in range(1, deep) if stage in (2, 3) else (0,):
            link(stage, q, o).wait_recv()

    def act(stage, q):
        if stage == 0:
            pass
        elif stage == 1:
            arrive(0, q)
            away = q * part + c * half + (1 - b) * quarter
            send1[span_of(q * quarter, quarter)] = (
                x_ref[span_of(away, quarter)] + got0[span_of(q * half + (1 - b) * quarter, quarter)].astype(f32)
            ).astype(bf16)
        elif stage == 2:
            arrive(1, q)
            own = (
                x_ref[span_of(place(q, 2), quarter)]
                + got0[span_of(q * half + b * quarter, quarter)].astype(f32)
                + got1[span_of(q * quarter, quarter)].astype(f32)
            )
            send2[span_of(q * quarter, quarter)] = own.astype(bf16)
        elif stage == 3:
            arrive(2, q)
            own = (
                x_ref[span_of(place(q, 3), leaf)]
                + got0[span_of(q * half + b * quarter + k * leaf, leaf)].astype(f32)
                + got1[span_of(q * quarter + k * leaf, leaf)].astype(f32)
            )
            for o in range(1, deep):
                own = own + got2[span_of((q * deep + o) * leaf, leaf)].astype(f32)
            full[span_of(place(q, 3), leaf)] = own.astype(bf16)
        elif stage == 6:
            arrive(5, q)
            planes = modes * 2 * tiles
            size = lines // planes
            for plane in range(planes * q // pieces, planes * (q + 1) // pieces):
                m, p, tile = plane // (2 * tiles), plane // tiles % 2, plane % tiles
                out_ref[pl.ds((m * size * tiles + tile) * 2 + p, size, stride=2 * tiles), :] = full[
                    pl.ds(plane * size, size), :
                ].astype(f32)
            return
        else:
            arrive(stage - 1, q)
        begin(stage, q)

    for q in range(pieces):
        act(0, q)
    for stage in range(1, 7):
        for q in range(pieces):
            act(stage, q)
        if stage == 1:
            send_down(2)
            lay_out(below_ref, flat, 0, 2 * below_ref.shape[0])
            send_down(0)
        elif stage == 2:
            lay_out(part_a, grad_ref, 0, whole)
        elif stage == 3:
            lay_out(part_b, grad_ref, part_a.shape[0], whole)
        elif stage == 4:
            send_down(1)
    for copy in started:
        copy.wait_send()

    @pl.when(c == 0)
    def _():
        downs[2].wait_send()

    @pl.when(c == 1)
    def _():
        downs[2].wait_recv()

    for n in range(2):

        @pl.when(me < length - 1)
        def _():
            downs[n].wait_send()

        @pl.when(me > 0)
        def _():
            downs[n].wait_recv()


def summed(x, grads, above, below, modes, tiles, axis):
    length = lax.axis_size(axis)
    lines, width = x.shape
    f32, bf16 = jnp.float32, jnp.bfloat16
    pieces = next(n for n in (4, 2, 1) if n == 1 or lines % (length * ROWS * n) == 0)
    vmem = pl.BlockSpec(memory_space=pltpu.VMEM)
    count = pieces * (4 + 2 * (length // 4))
    total = 2 * grads[0].shape[2] * (grads[0].shape[0] + grads[1].shape[0])
    flat = (2 * below.shape[2] * below.shape[0], width)
    return pl.pallas_call(
        functools.partial(total_kernel, length, pieces, modes, tiles),
        out_shape=(
            jax.ShapeDtypeStruct((lines, width), f32),
            jax.ShapeDtypeStruct((total, width), f32),
            jax.ShapeDtypeStruct(above.shape, bf16),
            jax.ShapeDtypeStruct(flat, bf16),
        ),
        in_specs=[vmem] * 5,
        out_specs=(vmem,) * 4,
        scratch_shapes=[
            pltpu.VMEM((lines // 2, width), bf16),
            pltpu.VMEM((lines // 4, width), bf16),
            pltpu.VMEM((lines // 4, width), bf16),
            pltpu.VMEM((lines // 2, width), bf16),
            pltpu.VMEM((lines // 4, width), bf16),
            pltpu.VMEM((lines // 4, width), bf16),
            pltpu.VMEM((lines, width), bf16),
            pltpu.VMEM(flat, bf16),
            pltpu.VMEM((32 * (2 * max(g.shape[0] for g in grads) + 1) + 7, width), f32),
            pltpu.SemaphoreType.DMA((count,)),
            pltpu.SemaphoreType.DMA((count,)),
            pltpu.SemaphoreType.DMA((6,)),
        ],
        compiler_params=pltpu.CompilerParams(collective_id=0, has_side_effects=True, vmem_limit_bytes=28 << 20),
        name="total",
    )(x, *grads, above, below)


def dft_tables(patch):
    index = np.arange(patch)
    angle = ((index[:, None] * index[None, :]) % patch).astype(np.float64) * (2.0 * math.pi / patch)
    scale = 1.0 / math.sqrt(patch)
    cosine, sine = np.cos(angle) * scale, np.sin(angle) * scale
    half = patch // 2
    tables = []
    for odd in range(2):
        c, s = cosine[:half, odd::2], sine[:half, odd::2]
        tables.append(np.block([[c, -s], [s, c]]))
        tables.append(np.block([[c.T, s.T], [-s.T, c.T]]))
    order = np.concatenate([index[0::2], index[1::2]])
    tables.append((index[:, None] == order[None, :]).astype(np.float64))
    stacked = np.stack(tables).astype(np.float32)
    return jnp.asarray(stacked).astype(jnp.bfloat16)


def step_kernel(
    modes, size, rows, first_tile, low, high, keep, own_parts, rim_parts, carried, *refs
):
    f32, bf16 = jnp.float32, jnp.bfloat16
    refs = list(refs)

    def take(n):
        got, refs[:] = refs[:n], refs[n:]
        return got

    count_ref, top_ref, left_ref, code_ref = take(4)
    probe_hbm, measured_hbm, table_hbm = take(3)
    owns, rims = take(len(own_parts)), take(len(rim_parts))
    if carried:
        handed_hbm, sum_hbm, before_ref = take(3)
    grad_hbm, below_ref, pgrad, moved_ref = take(4)
    over_hbm = None if carried else take(1)[0]
    (ext, acc, probe, measured_ref, table_ref, rowx, slope, patch, waves, mids, far, ratios, gs,
     temp, sems, out_sems) = refs
    tiles = size // LANES
    half = size // 2
    slots = measured_ref.shape[0]
    span = 32
    along, inverse_of = (0, 2), (1, 3)
    copies = []

    def fetch(src, dst):
        copy = pltpu.make_async_copy(src, dst, sems.at[len(copies)])
        copy.start()
        copies.append(copy)

    for sources, ranges, row, n in ((owns, own_parts, 0, rows), (rims, rim_parts, rows, size)):
        for source, (start, stop, to) in zip(sources, ranges):
            fetch(
                source.at[pl.ds(start, stop - start)],
                ext.at[pl.ds(to, stop - start), :, pl.ds(row, n), :],
            )
    fetch(probe_hbm, probe)
    fetch(measured_hbm, measured_ref)
    fetch(table_hbm, table_ref)
    overlap = 0
    if carried:
        overlap = handed_hbm.shape[0]
        fetch(handed_hbm, acc.at[pl.ds(0, overlap)])
        fetch(sum_hbm, pgrad)
    else:
        pgrad[...] = jnp.zeros_like(pgrad)
    gs[...] = jnp.zeros_like(gs)

    @pl.loop(overlap, acc.shape[0])
    def _(k):
        for p in range(2):
            acc[k, p] = jnp.zeros(acc.shape[2:], f32)

    for j in range(slots):
        for p in range(2):
            moved_ref[p, j] = before_ref[p, j] if carried else 0.0
    for copy in copies:
        copy.wait()

    def one(j):
        top, left, code = top_ref[j], left_ref[j], code_ref[j]
        first = left // LANES
        col = left - first * LANES
        first = first - first_tile
        base_row = pl.multiple_of(top // ROWS * ROWS, ROWS)
        row = top - base_row
        fy = (code // 4).astype(f32) * 0.25
        fx = (code % 4).astype(f32) * 0.25
        reach = (tiles + 1) * LANES
        tall = size + ROWS
        here = lax.broadcasted_iota(jnp.int32, (reach, size), 0)
        away = here - lax.broadcasted_iota(jnp.int32, (reach, size), 1) - col
        at_left, at_right = (away == 0).astype(f32), (away == 1).astype(f32)
        mix = ((1.0 - fx) * at_left + fx * at_right).astype(bf16)
        tilt = (at_right - at_left).astype(bf16)
        for p in range(2):
            window = jnp.concatenate(
                [ext[first + k, p, pl.ds(base_row, tall), :] for k in range(tiles + 1)], axis=1
            )
            for table, kept in ((mix, rowx), (tilt, slope)):
                cells = jnp.dot(window, table, preferred_element_type=f32)
                for k in range(tiles):
                    kept[p, k, 0:tall, :] = cells[:, k * LANES : (k + 1) * LANES]
        for p in range(2):
            for k in range(tiles):
                for i in range(size // span):
                    upper = rowx[p, k, pl.ds(row + i * span, span), :]
                    lower = rowx[p, k, pl.ds(row + i * span + 1, span), :]
                    patch[p, i * span : (i + 1) * span, k * LANES : (k + 1) * LANES] = upper + fy * (lower - upper)


        share = size // modes
        short = share // 2

        def wave(c):
            for h in range(2):
                at = slice(h * half + c * short, h * half + (c + 1) * short)
                re, im = patch[0, at, :], patch[1, at, :]
                for m in range(modes):
                    here = slice(m * share + h * short, m * share + (h + 1) * short)
                    pr, pi = probe[m, 0, at, :], probe[m, 1, at, :]
                    for q, w in enumerate((pr * re - pi * im, pr * im + pi * re)):
                        to = slice(q * half, (q + 1) * half)
                        waves[0, c, here, to] = (w[:, :half] + w[:, half:]).astype(bf16)
                        waves[1, c, here, to] = (w[:, :half] - w[:, half:]).astype(bf16)

        def along_columns(c):
            for e in range(2):
                h = jnp.dot(waves[e, c], table_ref[along[e]], preferred_element_type=f32)
                to = slice(e * half, (e + 1) * half)
                for m in range(modes):
                    for q in range(2):
                        upper = h[m * share : m * share + short, q * half : (q + 1) * half]
                        lower = h[m * share + short : (m + 1) * share, q * half : (q + 1) * half]
                        at = slice(q * half + c * short, q * half + (c + 1) * short)
                        mids[m, 0, at, to] = (upper + lower).astype(bf16)
                        mids[m, 1, at, to] = (upper - lower).astype(bf16)

        def along_rows(e):
            strength = 0.0
            for m in range(modes):
                f = jnp.dot(table_ref[inverse_of[e]], mids[m, e], preferred_element_type=f32)
                far[m, e] = f.astype(far.dtype)
                strength = strength + (f[:half] * f[:half] + f[half:] * f[half:])
            ratio = 1.0 - measured_ref[j, e].astype(f32) * jnp.minimum(lax.rsqrt(strength), 2.0)
            ratios[e] = ratio.astype(bf16)

        def skewed(*stages):
            for t in range(modes + len(stages) - 1):
                for n in reversed(range(len(stages))):
                    if 0 <= t - n < modes:
                        stages[n](t - n)

        skewed(wave, along_columns)
        for e in range(2):
            along_rows(e)

        def error(m):
            for e in range(2):
                ratio = ratios[e]
                mids[m, e, 0:half, :] = far[m, e, 0:half, :] * ratio
                mids[m, e, half:size, :] = far[m, e, half:size, :] * ratio

        def back_rows(m):
            parts = [jnp.dot(table_ref[along[e]], mids[m, e], preferred_element_type=f32) for e in range(2)]
            for h, both in enumerate((parts[0] + parts[1], parts[0] - parts[1])):
                for e in range(2):
                    for q in range(2):
                        to, at = slice(q * half, (q + 1) * half), slice(e * half, (e + 1) * half)
                        for n in range(half // share):
                            waves[e, h * (half // share) + n, m * share : (m + 1) * share, to] = both[
                                q * half + n * share : q * half + (n + 1) * share, at
                            ].astype(bf16)

        def back_columns(c):
            back = [jnp.dot(waves[e, c], table_ref[inverse_of[e]], preferred_element_type=f32) for e in range(2)]
            for i in range(share // span):
                start = c * share + i * span
                at = slice(start, start + span)
                for k in range(2):
                    to = slice(k * half, (k + 1) * half)
                    re, im = patch[0, at, to], patch[1, at, to]
                    sums = [0.0, 0.0]
                    for m in range(modes):
                        here = slice(m * share + i * span, m * share + (i + 1) * span)
                        b0, b1 = back[0][here], back[1][here]
                        mixed = b0 + b1 if k == 0 else b0 - b1
                        ur, ui = mixed[:, :half], mixed[:, half:]
                        pr, pi = probe[m, 0, at, to], probe[m, 1, at, to]
                        sums[0] = sums[0] + (pr * ur + pi * ui)
                        sums[1] = sums[1] + (pr * ui - pi * ur)
                        pgrad[m, 0, k, at, :] += re * ur + im * ui
                        pgrad[m, 1, k, at, :] += re * ui - im * ur
                    for p in range(2):
                        gs[p, k, 8 + start : 8 + start + span, :] = sums[p]

        skewed(error, back_rows)
        skewed(back_columns)

        down, across = jnp.zeros((8, LANES), f32), jnp.zeros((8, LANES), f32)
        for i in range(size // span):
            for p in range(2):
                for k in range(tiles):
                    at, after = pl.ds(row + i * span, span), pl.ds(row + i * span + 1, span)
                    g = gs[p, k, 8 + i * span : 8 + (i + 1) * span, :]
                    dy = g * (rowx[p, k, after, :] - rowx[p, k, at, :])
                    upper = slope[p, k, at, :]
                    dx = g * (upper + fy * (slope[p, k, after, :] - upper))
                    down = down + jnp.sum(dy.reshape(span // 8, 8, LANES), 0)
                    across = across + jnp.sum(dx.reshape(span // 8, 8, LANES), 0)
        moved_ref[0, j] = jnp.sum(down) / size
        moved_ref[1, j] = jnp.sum(across) / size

        base = pl.multiple_of(top // 8 * 8, 8)
        lag = top - base

        there = lax.broadcasted_iota(jnp.int32, (size, reach), 1)
        gone = there - lax.broadcasted_iota(jnp.int32, (size, reach), 0) - col
        spread = ((1.0 - fx) * (gone == 0).astype(f32) + fx * (gone == 1).astype(f32)).astype(bf16)
        for p in range(2):
            g = []
            for k in range(tiles):
                here = gs[p, k, pl.ds(8 - lag, tall), :]
                before = gs[p, k, pl.ds(7 - lag, tall), :]
                g.append((here + fy * (before - here)).astype(bf16))
            wide = jnp.dot(jnp.concatenate(g, axis=1), spread, preferred_element_type=f32)
            for k in range(tiles + 1):
                acc[first + k, p, pl.ds(base, tall), :] += wide[:, k * LANES : (k + 1) * LANES]

    @pl.loop(0, count_ref[0])
    def _(j):
        tile = left_ref[j] // LANES

        @pl.when((tile >= low) & (tile < high))
        def _():
            one(j)

    outs = [
        pltpu.make_async_copy(acc.at[pl.ds(0, keep), :, pl.ds(0, rows), :], grad_hbm, out_sems.at[0]),
    ]
    if not carried:
        outs.append(pltpu.make_async_copy(acc.at[pl.ds(keep, over_hbm.shape[0])], over_hbm, out_sems.at[2]))
    for out in outs:
        out.start()

    if carried:

        @pl.loop(0, keep)
        def _(k):
            for p in range(2):
                below_ref[k, p] = acc[k, p, rows : rows + size, :].astype(bf16)

    else:

        @pl.loop(0, size // span)
        def _(i):
            at = pl.multiple_of(i * span, span)
            for k in range(keep):
                for p in range(2):
                    temp[pl.ds(2 * k + p, span, stride=2 * keep + 1), :] = acc[k, p, pl.ds(rows + at, span), :]
            for y in range(span):
                below_ref[pl.ds(pl.multiple_of((at + y) * 2 * keep, ROWS), 2 * keep), :] = temp[
                    y * (2 * keep + 1) : y * (2 * keep + 1) + 2 * keep, :
                ].astype(bf16)

    for out in outs:
        out.wait()


def step(modes, size, rows, slots, first_tile, low, high, keep, count, own, rim, carried, common):
    f32, bf16 = jnp.float32, jnp.bfloat16
    tiles = size // LANES
    deep = rows + size + 8
    vmem = pl.BlockSpec(memory_space=pltpu.VMEM)
    smem = pl.BlockSpec(memory_space=pltpu.SMEM)
    hbm = pl.BlockSpec(memory_space=pl.ANY)
    planes = (modes, 2, tiles, size, LANES)
    out_shape = [
        jax.ShapeDtypeStruct((keep, 2, rows, LANES), f32),
        jax.ShapeDtypeStruct((keep, 2, size, LANES) if carried else (2 * keep * size, LANES), bf16),
        jax.ShapeDtypeStruct(planes, f32),
        jax.ShapeDtypeStruct((2, slots), f32),
    ]
    out_specs = [hbm, vmem, vmem, smem]
    if not carried:
        out_shape.append(jax.ShapeDtypeStruct((count - keep, 2, deep, LANES), f32))
        out_specs.append(hbm)
    own_arrays, own_parts = zip(*own)
    rim_arrays, rim_parts = zip(*rim)
    return pl.pallas_call(
        functools.partial(
            step_kernel, modes, size, rows, first_tile, low, high, keep, own_parts, rim_parts, bool(carried)
        ),
        out_shape=tuple(out_shape),
        in_specs=[smem] * 4 + [hbm] * (3 + len(own) + len(rim)) + ([hbm, hbm, smem] if carried else []),
        out_specs=tuple(out_specs),
        scratch_shapes=[
            pltpu.VMEM((count, 2, rows + size, LANES), bf16),
            pltpu.VMEM((count, 2, deep, LANES), f32),
            pltpu.VMEM((modes, 2, size, size), f32),
            pltpu.VMEM((slots, 2, size // 2, size), bf16),
            pltpu.VMEM((4, size, size), bf16),
            pltpu.VMEM((2, tiles, size + 32, LANES), f32),
            pltpu.VMEM((2, tiles, size + 32, LANES), f32),
            pltpu.VMEM((2, size, size), f32),
            pltpu.VMEM((2, modes, size, size), bf16),
            pltpu.VMEM((modes, 2, size, size), bf16),
            pltpu.VMEM((modes, 2, size, size), bf16),
            pltpu.VMEM((2, size // 2, size), bf16),
            pltpu.VMEM((2, tiles, size + 32, LANES), f32),
            pltpu.VMEM((32 * (2 * keep + 1) + 7, LANES), f32),
            pltpu.SemaphoreType.DMA((12,)),
            pltpu.SemaphoreType.DMA((3,)),
        ],
        compiler_params=pltpu.CompilerParams(vmem_limit_bytes=30 << 20),
        cost_estimate=pl.CostEstimate(flops=3 << 30, bytes_accessed=16 << 20, transcendentals=0),
        name="step_b" if carried else "step_a",
    )(*common, *own_arrays, *rim_arrays, *carried)


def sort_kernel(lines, first, x_ref, out_ref, temp):
    n = out_ref.shape[2]
    line = 2 * lines
    start = 2 * first // ROWS * ROWS
    stop = -(-2 * (first + out_ref.shape[0]) // ROWS) * ROWS
    wide = stop - start + 1
    for y in range(n):
        temp[y * wide : (y + 1) * wide - 1, :] = x_ref[y * line + start : y * line + stop, :].astype(jnp.float32)
    for k in range(out_ref.shape[0]):
        for p in range(2):
            plane = temp[pl.ds(2 * (first + k) + p - start, n, stride=wide), :]
            out_ref[k, p] = plane.astype(jnp.bfloat16)


def sorted_planes(x, rows, lines, first, last):
    n = 128 if rows % 128 == 0 else rows
    return pl.pallas_call(
        functools.partial(sort_kernel, lines, first),
        grid=(rows // n,),
        out_shape=jax.ShapeDtypeStruct((last - first, 2, rows, LANES), jnp.bfloat16),
        in_specs=[pl.BlockSpec((n * lines * 2, LANES), lambda i: (i, 0))],
        out_specs=pl.BlockSpec((last - first, 2, n, LANES), lambda i: (0, 0, i, 0)),
        scratch_shapes=[pltpu.VMEM((n * (lines * 2 + 1) + 7, LANES), jnp.float32)],
        cost_estimate=pl.CostEstimate(flops=1 << 20, bytes_accessed=4 << 20, transcendentals=0),
        name="sort",
    )(x)


def prepare_kernel(tiles, x_ref, table_ref, measured_ref, out_ref, table_out, ordered_ref, temp):
    modes, _, size, _ = out_ref.shape
    slots = measured_ref.shape[0]
    span = 32
    table_out[...] = table_ref[0:4]

    @pl.loop(0, modes * (size // span))
    def _(i):
        at = pl.multiple_of(lax.rem(i, size // span) * span, span)
        m = i // (size // span)
        for p in range(2):
            for k in range(tiles):
                out_ref[m, p, pl.ds(at, span), k * LANES : (k + 1) * LANES] = x_ref[
                    pl.ds((i * span * tiles + k) * 2 + p, span, stride=2 * tiles), :
                ]

    @pl.loop(0, slots)
    def _(j):
        ordered = jnp.dot(measured_ref[j], table_ref[4], preferred_element_type=jnp.float32)
        for k in range(tiles):
            temp[k] = ordered[:, k * LANES : (k + 1) * LANES]
        for e in range(2):
            for k in range(tiles):
                ordered_ref[j, e, :, k * LANES : (k + 1) * LANES] = temp[
                    k, pl.ds(e, size // 2, stride=2), :
                ].astype(jnp.bfloat16)


def prepared(x, tables, measured, modes, size):
    vmem = pl.BlockSpec(memory_space=pltpu.VMEM)
    tiles = size // LANES
    return pl.pallas_call(
        functools.partial(prepare_kernel, tiles),
        out_shape=(
            jax.ShapeDtypeStruct((modes, 2, size, size), jnp.float32),
            jax.ShapeDtypeStruct((4, size, size), tables.dtype),
            jax.ShapeDtypeStruct((measured.shape[0], 2, size // 2, size), measured.dtype),
        ),
        in_specs=[vmem, vmem, vmem],
        out_specs=(vmem, vmem, vmem),
        scratch_shapes=[pltpu.VMEM((tiles, size, LANES), jnp.float32)],
        compiler_params=pltpu.CompilerParams(vmem_limit_bytes=16 << 20),
        cost_estimate=pl.CostEstimate(flops=1 << 20, bytes_accessed=8 << 20, transcendentals=0),
        name="prepare",
    )(x, tables, measured)


def tiled(x):
    *lead, two, width = x.shape
    n = math.prod(lead)
    x = x.reshape(n, two, width // LANES, LANES)
    return jnp.transpose(x, (0, 2, 1, 3)).reshape(-1, LANES)


def untiled(x, lead, width):
    n = math.prod(lead)
    x = jnp.transpose(x.reshape(n, width // LANES, 2, LANES), (0, 2, 1, 3))
    return x.reshape(*lead, 2, width)


def shards(object_tiles, probe, measured, offset_row, offset_col, subpixel, live_count):
    rows, _, width = object_tiles.shape
    modes, size = probe.shape[:2]
    slots = measured.shape[0]
    lines, tiles = width // LANES, size // LANES
    mid = lines // 2
    near = mid + tiles
    own = tiled(object_tiles)
    own_a = sorted_planes(own, rows, lines, 0, near)
    own_b = sorted_planes(own, rows, lines, near, lines)
    rim_a = passed_along(own_a[:, :, :size], "row", -1)
    rim_b = passed_along(own_b[:, :, :size], "row", -1)
    planes, tables, ordered = prepared(tiled(probe), dft_tables(size), measured, modes, size)
    common = (live_count, offset_row, offset_col, subpixel, planes, ordered, tables)
    whole = (0, near, 0)
    grad_a, below_a, sum_a, moved_a, over = step(
        modes, size, rows, slots, 0, 0, mid, mid, near, [(own_a, whole)], [(rim_a, whole)], (), common
    )
    landed_a = passed_along(below_a, "row", 1, odd=True)
    kept, rest = (mid, near, 0), (0, lines - near, tiles)
    grad_b, below_b, sums, moved = step(
        modes, size, rows, slots, mid, mid, lines, lines - mid, lines - mid,
        [(own_a, kept), (own_b, rest)], [(rim_a, kept), (rim_b, rest)], (over, sum_a, moved_a), common,
    )
    probe_grad, grad, core_a, landed_b = summed(
        sums.reshape(-1, LANES), (grad_a, grad_b), below_a, below_b, modes, tiles, "row"
    )
    landed = jnp.concatenate(
        [(landed_a + core_a).reshape(size, 2 * mid, LANES), landed_b.reshape(size, 2 * (lines - mid), LANES)], axis=1
    )
    landed = lax.optimization_barrier(landed.reshape(-1, LANES))
    grad = grad.at[: landed.shape[0]].add(landed.astype(jnp.float32))
    return (untiled(grad, (rows,), width), untiled(probe_grad, (modes, size), size), moved)


def solution(mesh):
    in_specs = (
        P(("groups", "row"), None, None),
        P(),
        P(("groups", "row"), None, None),
        P(("groups", "row")),
        P(("groups", "row")),
        P(("groups", "row")),
        P(("groups", "row")),
    )
    out_specs = (
        P(("groups", "row"), None, None),
        P("groups", None, None, None),
        P(None, ("groups", "row")),
    )
    return jax.shard_map(shards, mesh=mesh, in_specs=in_specs, out_specs=out_specs, check_vma=False)
```

```python
import functools
import math

import jax
import jax.numpy as jnp
import numpy as np
from jax import lax
from jax.experimental import pallas as pl
from jax.experimental.pallas import tpu as pltpu
from jax.sharding import PartitionSpec as P

LANES = 128
ROWS = 16


def passed_along(x, axis, by, odd=False):
    length = lax.axis_size(axis)
    pairs = [(i, i + by) for i in range(odd, length, 1 + odd) if 0 <= i + by < length]
    return lax.ppermute(x, axis, pairs)


def total_kernel(
    length, pieces, modes, tiles, mid, x_ref, part_a, part_b, above_ref, below_ref, out_ref, grad_ref, came_a, came_b,
    near, send1, send2, got0, got1, got2, full, flat, temp, sends, recvs, down_sems,
):
    f32, bf16 = jnp.float32, jnp.bfloat16
    lines, width = x_ref.shape
    deep = length // 4
    me = lax.axis_index("row")
    c, b, k = me % 2, (me // 2) % 2, me // 4
    part = lines // pieces
    half, quarter = part // 2, part // 4
    leaf = quarter // deep

    def stage_near(q):
        near[pl.ds(q * half, half)] = x_ref[
            pl.ds(pl.multiple_of(q * part + (1 - c) * half, ROWS), half)
        ].astype(bf16)

    def peer(stage, o):
        if stage in (0, 5):
            return {"row": me + 1 - 2 * c}
        if stage in (1, 4):
            return {"row": me + 2 - 4 * b}
        return {"row": ((k + o) % deep) * 4 + me % 4}

    barrier = pltpu.get_barrier_semaphore()
    others = [(0, 0), (1, 0)] + [(2, o) for o in range(1, deep)]
    for stage, o in others:
        pl.semaphore_signal(barrier, inc=1, device_id=peer(stage, o), device_id_type=pl.DeviceIdType.MESH)

    @pl.when(me > 0)
    def _():
        pl.semaphore_signal(barrier, inc=1, device_id={"row": me - 1}, device_id_type=pl.DeviceIdType.MESH)

    @pl.when(me < length - 1)
    def _():
        pl.semaphore_signal(barrier, inc=1, device_id={"row": me + 1}, device_id_type=pl.DeviceIdType.MESH)

    for q in range(pieces):
        stage_near(q)

    @pl.when(c == 0)
    def _():
        came_a[...] = jnp.zeros_like(came_a)

    @pl.when(me == 0)
    def _():
        came_b[...] = jnp.zeros_like(came_b)

    pl.semaphore_wait(
        barrier, len(others) + (me > 0).astype(jnp.int32) + (me < length - 1).astype(jnp.int32)
    )
    early = flat.shape[0] // 8 * 5
    downs = []
    for n, (src, dst, first, last) in enumerate((
        (flat, came_b, 0, early),
        (flat, came_b, early, flat.shape[0]),
        (above_ref, came_a, 0, above_ref.shape[0]),
    )):
        at = pl.ds(first, last - first)
        downs.append(pltpu.make_async_remote_copy(
            src_ref=src.at[at], dst_ref=dst.at[at],
            send_sem=down_sems.at[n], recv_sem=down_sems.at[3 + n],
            device_id={"row": jnp.minimum(me + 1, length - 1)}, device_id_type=pl.DeviceIdType.MESH,
        ))

    def send_down(n):
        @pl.when((c == 0) if n == 2 else (me < length - 1))
        def _():
            downs[n].start()

    whole = 2 * (mid + part_b.shape[0])
    rows = grad_ref.shape[0] // whole
    block = 32

    def lay_out(part, out, first, line, many, high):
        @pl.loop(0, high // block)
        def _(i):
            at = pl.multiple_of(i * block, block)
            for t in range(many):
                for p in range(2):
                    temp[pl.ds(2 * t + p, block, stride=2 * many + 1), :] = part[t, p, pl.ds(at, block), :].astype(f32)
            for y in range(block):
                out[pl.ds(pl.multiple_of((at + y) * line + 2 * first, ROWS), 2 * many), :] = temp[
                    y * (2 * many + 1) : y * (2 * many + 1) + 2 * many, :
                ].astype(out.dtype)

    base = [0, pieces, 2 * pieces, (2 + deep) * pieces, (2 + 2 * deep) * pieces, (3 + 2 * deep) * pieces]

    def span_of(start, size):
        return pl.ds(pl.multiple_of(start, ROWS), size)

    def place(q, stage):
        start = q * part
        if stage == 0:
            return start
        start = start + c * half
        if stage == 1:
            return start
        start = start + b * quarter
        return start if stage == 2 else start + k * leaf

    def link(stage, q, o=0):
        at = span_of(q * quarter, quarter)
        if stage == 0:
            src, dst = near.at[span_of(q * half, half)], got0.at[span_of(q * half, half)]
        elif stage == 1:
            src, dst = send1.at[at], got1.at[at]
        elif stage == 2:
            src = send2.at[span_of(q * quarter + ((k + o) % deep) * leaf, leaf)]
            dst = got2.at[span_of((q * deep + o) * leaf, leaf)]
        elif stage == 3:
            src = dst = full.at[span_of(place(q, 3), leaf)]
        elif stage == 4:
            src = dst = full.at[span_of(place(q, 2), quarter)]
        else:
            src = dst = full.at[span_of(place(q, 1), half)]
        sem = base[stage] + (q * deep + o if stage in (2, 3) else q)
        return pltpu.make_async_remote_copy(
            src_ref=src, dst_ref=dst, send_sem=sends.at[sem], recv_sem=recvs.at[sem],
            device_id=peer(stage, o), device_id_type=pl.DeviceIdType.MESH,
        )

    started = []

    def begin(stage, q):
        for o in range(1, deep) if stage in (2, 3) else (0,):
            copy = link(stage, q, o)
            copy.start()
            started.append(copy)

    def arrive(stage, q):
        for o in range(1, deep) if stage in (2, 3) else (0,):
            link(stage, q, o).wait_recv()

    def act(stage, q):
        if stage == 0:
            pass
        elif stage == 1:
            arrive(0, q)
            away = q * part + c * half + (1 - b) * quarter
            send1[span_of(q * quarter, quarter)] = (
                x_ref[span_of(away, quarter)] + got0[span_of(q * half + (1 - b) * quarter, quarter)].astype(f32)
            ).astype(bf16)
        elif stage == 2:
            arrive(1, q)
            own = (
                x_ref[span_of(place(q, 2), quarter)]
                + got0[span_of(q * half + b * quarter, quarter)].astype(f32)
                + got1[span_of(q * quarter, quarter)].astype(f32)
            )
            send2[span_of(q * quarter, quarter)] = own.astype(bf16)
        elif stage == 3:
            arrive(2, q)
            own = (
                x_ref[span_of(place(q, 3), leaf)]
                + got0[span_of(q * half + b * quarter + k * leaf, leaf)].astype(f32)
                + got1[span_of(q * quarter + k * leaf, leaf)].astype(f32)
            )
            for o in range(1, deep):
                own = own + got2[span_of((q * deep + o) * leaf, leaf)].astype(f32)
            full[span_of(place(q, 3), leaf)] = own.astype(bf16)
        elif stage == 6:
            arrive(5, q)
            planes = modes * 2 * tiles
            size = lines // planes
            for plane in range(planes * q // pieces, planes * (q + 1) // pieces):
                m, p, tile = plane // (2 * tiles), plane // tiles % 2, plane % tiles
                out_ref[pl.ds((m * size * tiles + tile) * 2 + p, size, stride=2 * tiles), :] = full[
                    pl.ds(plane * size, size), :
                ].astype(f32)
            return
        else:
            arrive(stage - 1, q)
        begin(stage, q)

    for q in range(pieces):
        act(0, q)
    for stage in range(1, 7):
        for q in range(pieces):
            act(stage, q)
        if stage == 1:
            send_down(2)
            lay_out(below_ref, flat, 0, 2 * below_ref.shape[0], below_ref.shape[0], below_ref.shape[2])
            send_down(0)
        elif stage == 2:
            lay_out(part_a, grad_ref, 0, whole, mid, rows)
        elif stage == 3:
            lay_out(part_b, grad_ref, mid, whole, part_b.shape[0], rows)
        elif stage == 4:
            send_down(1)
    for copy in started:
        copy.wait_send()

    @pl.when(c == 0)
    def _():
        downs[2].wait_send()

    @pl.when(c == 1)
    def _():
        downs[2].wait_recv()

    for n in range(2):

        @pl.when(me < length - 1)
        def _():
            downs[n].wait_send()

        @pl.when(me > 0)
        def _():
            downs[n].wait_recv()


def summed(x, grads, above, below, modes, tiles, mid, rows, axis):
    length = lax.axis_size(axis)
    lines, width = x.shape
    f32, bf16 = jnp.float32, jnp.bfloat16
    pieces = next(n for n in (4, 2, 1) if n == 1 or lines % (length * ROWS * n) == 0)
    vmem = pl.BlockSpec(memory_space=pltpu.VMEM)
    count = pieces * (4 + 2 * (length // 4))
    total = 2 * rows * (mid + grads[1].shape[0])
    flat = (2 * below.shape[2] * below.shape[0], width)
    return pl.pallas_call(
        functools.partial(total_kernel, length, pieces, modes, tiles, mid),
        out_shape=(
            jax.ShapeDtypeStruct((lines, width), f32),
            jax.ShapeDtypeStruct((total, width), f32),
            jax.ShapeDtypeStruct(above.shape, bf16),
            jax.ShapeDtypeStruct(flat, bf16),
        ),
        in_specs=[vmem] * 5,
        out_specs=(vmem,) * 4,
        scratch_shapes=[
            pltpu.VMEM((lines // 2, width), bf16),
            pltpu.VMEM((lines // 4, width), bf16),
            pltpu.VMEM((lines // 4, width), bf16),
            pltpu.VMEM((lines // 2, width), bf16),
            pltpu.VMEM((lines // 4, width), bf16),
            pltpu.VMEM((lines // 4, width), bf16),
            pltpu.VMEM((lines, width), bf16),
            pltpu.VMEM(flat, bf16),
            pltpu.VMEM((32 * (2 * max(g.shape[0] for g in grads) + 1) + 7, width), f32),
            pltpu.SemaphoreType.DMA((count,)),
            pltpu.SemaphoreType.DMA((count,)),
            pltpu.SemaphoreType.DMA((6,)),
        ],
        compiler_params=pltpu.CompilerParams(collective_id=0, has_side_effects=True, vmem_limit_bytes=28 << 20),
        name="total",
    )(x, *grads, above, below)


def dft_tables(patch):
    index = np.arange(patch)
    angle = ((index[:, None] * index[None, :]) % patch).astype(np.float64) * (2.0 * math.pi / patch)
    scale = 1.0 / math.sqrt(patch)
    cosine, sine = np.cos(angle) * scale, np.sin(angle) * scale
    half = patch // 2
    tables = []
    for odd in range(2):
        c, s = cosine[:half, odd::2], sine[:half, odd::2]
        tables.append(np.block([[c, -s], [s, c]]))
        tables.append(np.block([[c.T, s.T], [-s.T, c.T]]))
    order = np.concatenate([index[0::2], index[1::2]])
    tables.append((index[:, None] == order[None, :]).astype(np.float64))
    stacked = np.stack(tables).astype(np.float32)
    return jnp.asarray(stacked).astype(jnp.bfloat16)


def step_kernel(
    modes, size, rows, first_tile, low, high, keep, own_parts, rim_parts, carried, *refs
):
    f32, bf16 = jnp.float32, jnp.bfloat16
    refs = list(refs)

    def take(n):
        got, refs[:] = refs[:n], refs[n:]
        return got

    count_ref, top_ref, left_ref, code_ref = take(4)
    probe, measured_ref, table_ref = take(3)
    owns, rims = take(len(own_parts)), take(len(rim_parts))
    if carried:
        handed_hbm, sum_hbm, before_ref = take(3)
    acc, below_ref, pgrad, moved_ref = take(4)
    (ext, rowx, slope, patch, waves, mids, far, ratios, gs,
     temp, sems) = refs
    tiles = size // LANES
    half = size // 2
    slots = measured_ref.shape[0]
    span = 32
    along, inverse_of = (0, 2), (1, 3)
    copies = []

    def fetch(src, dst):
        copy = pltpu.make_async_copy(src, dst, sems.at[len(copies)])
        copy.start()
        copies.append(copy)

    for sources, ranges, row, n in ((owns, own_parts, 0, rows), (rims, rim_parts, rows, size)):
        for source, (start, stop, to) in zip(sources, ranges):
            fetch(
                source.at[pl.ds(start, stop - start)],
                ext.at[pl.ds(to, stop - start), :, pl.ds(row, n), :],
            )
    overlap = 0
    if carried:
        overlap = handed_hbm.shape[0] - (low)
        fetch(handed_hbm.at[pl.ds(low, overlap)], acc.at[pl.ds(0, overlap)])
        fetch(sum_hbm, pgrad)
    else:
        pgrad[...] = jnp.zeros_like(pgrad)
    gs[...] = jnp.zeros_like(gs)

    @pl.loop(overlap, acc.shape[0])
    def _(k):
        for p in range(2):
            acc[k, p] = jnp.zeros(acc.shape[2:], f32)

    for j in range(slots):
        for p in range(2):
            moved_ref[p, j] = before_ref[p, j] if carried else 0.0
    for copy in copies:
        copy.wait()

    def one(j):
        top, left, code = top_ref[j], left_ref[j], code_ref[j]
        first = left // LANES
        col = left - first * LANES
        first = first - first_tile
        base_row = pl.multiple_of(top // ROWS * ROWS, ROWS)
        row = top - base_row
        fy = (code // 4).astype(f32) * 0.25
        fx = (code % 4).astype(f32) * 0.25
        reach = (tiles + 1) * LANES
        tall = size + ROWS
        here = lax.broadcasted_iota(jnp.int32, (reach, size), 0)
        away = here - lax.broadcasted_iota(jnp.int32, (reach, size), 1)
        at_left, at_right = away == col, away == col + 1
        mix = jnp.where(at_left, 1.0 - fx, jnp.where(at_right, fx, 0.0)).astype(bf16)
        tilt = jnp.where(at_left, -1.0, jnp.where(at_right, 1.0, 0.0)).astype(bf16)
        for p in range(2):
            window = jnp.concatenate(
                [ext[first + k, p, pl.ds(base_row, tall), :] for k in range(tiles + 1)], axis=1
            )
            for table, kept in ((mix, rowx), (tilt, slope)):
                cells = jnp.dot(window, table, preferred_element_type=f32)
                for k in range(tiles):
                    kept[p, k, 0:tall, :] = cells[:, k * LANES : (k + 1) * LANES]
        for p in range(2):
            for k in range(tiles):
                for i in range(size // span):
                    upper = rowx[p, k, pl.ds(row + i * span, span), :]
                    lower = rowx[p, k, pl.ds(row + i * span + 1, span), :]
                    patch[p, i * span : (i + 1) * span, k * LANES : (k + 1) * LANES] = upper + fy * (lower - upper)


        share = size // modes
        short = share // 2

        def wave(c):
            for h in range(2):
                at = slice(h * half + c * short, h * half + (c + 1) * short)
                re, im = patch[0, at, :], patch[1, at, :]
                for m in range(modes):
                    here = slice(m * share + h * short, m * share + (h + 1) * short)
                    pr, pi = probe[m, 0, at, :], probe[m, 1, at, :]
                    for q, w in enumerate((pr * re - pi * im, pr * im + pi * re)):
                        to = slice(q * half, (q + 1) * half)
                        waves[0, c, here, to] = (w[:, :half] + w[:, half:]).astype(bf16)
                        waves[1, c, here, to] = (w[:, :half] - w[:, half:]).astype(bf16)

        def along_columns(c):
            for e in range(2):
                h = jnp.dot(waves[e, c], table_ref[along[e]], preferred_element_type=f32)
                to = slice(e * half, (e + 1) * half)
                for m in range(modes):
                    for q in range(2):
                        upper = h[m * share : m * share + short, q * half : (q + 1) * half]
                        lower = h[m * share + short : (m + 1) * share, q * half : (q + 1) * half]
                        at = slice(q * half + c * short, q * half + (c + 1) * short)
                        mids[m, 0, at, to] = (upper + lower).astype(bf16)
                        mids[m, 1, at, to] = (upper - lower).astype(bf16)

        def along_rows(e):
            strength = 0.0
            for m in range(modes):
                f = jnp.dot(table_ref[inverse_of[e]], mids[m, e], preferred_element_type=f32)
                far[m, e] = f.astype(far.dtype)
                strength = strength + (f[:half] * f[:half] + f[half:] * f[half:])
            ratio = 1.0 - measured_ref[j, e].astype(f32) * jnp.minimum(lax.rsqrt(strength), 2.0)
            ratios[e] = ratio.astype(bf16)

        def skewed(*stages):
            for t in range(modes + len(stages) - 1):
                for n in reversed(range(len(stages))):
                    if 0 <= t - n < modes:
                        stages[n](t - n)

        skewed(wave, along_columns)
        for e in range(2):
            along_rows(e)

        def error(m):
            for e in range(2):
                ratio = ratios[e]
                mids[m, e, 0:half, :] = far[m, e, 0:half, :] * ratio
                mids[m, e, half:size, :] = far[m, e, half:size, :] * ratio

        def back_rows(m):
            parts = [jnp.dot(table_ref[along[e]], mids[m, e], preferred_element_type=f32) for e in range(2)]
            for h, both in enumerate((parts[0] + parts[1], parts[0] - parts[1])):
                for e in range(2):
                    for q in range(2):
                        to, at = slice(q * half, (q + 1) * half), slice(e * half, (e + 1) * half)
                        for n in range(half // share):
                            waves[e, h * (half // share) + n, m * share : (m + 1) * share, to] = both[
                                q * half + n * share : q * half + (n + 1) * share, at
                            ].astype(bf16)

        def back_columns(c):
            back = [jnp.dot(waves[e, c], table_ref[inverse_of[e]], preferred_element_type=f32) for e in range(2)]
            for i in range(share // span):
                start = c * share + i * span
                at = slice(start, start + span)
                for k in range(2):
                    to = slice(k * half, (k + 1) * half)
                    re, im = patch[0, at, to], patch[1, at, to]
                    sums = [0.0, 0.0]
                    for m in range(modes):
                        here = slice(m * share + i * span, m * share + (i + 1) * span)
                        b0, b1 = back[0][here], back[1][here]
                        mixed = b0 + b1 if k == 0 else b0 - b1
                        ur, ui = mixed[:, :half], mixed[:, half:]
                        pr, pi = probe[m, 0, at, to], probe[m, 1, at, to]
                        sums[0] = sums[0] + (pr * ur + pi * ui)
                        sums[1] = sums[1] + (pr * ui - pi * ur)
                        pgrad[m, 0, k, at, :] += re * ur + im * ui
                        pgrad[m, 1, k, at, :] += re * ui - im * ur
                    for p in range(2):
                        gs[p, k, 8 + start : 8 + start + span, :] = sums[p]

        skewed(error, back_rows)
        skewed(back_columns)

        down, across = jnp.zeros((8, LANES), f32), jnp.zeros((8, LANES), f32)
        for i in range(size // span):
            for p in range(2):
                for k in range(tiles):
                    at, after = pl.ds(row + i * span, span), pl.ds(row + i * span + 1, span)
                    g = gs[p, k, 8 + i * span : 8 + (i + 1) * span, :]
                    dy = g * (rowx[p, k, after, :] - rowx[p, k, at, :])
                    upper = slope[p, k, at, :]
                    dx = g * (upper + fy * (slope[p, k, after, :] - upper))
                    down = down + jnp.sum(dy.reshape(span // 8, 8, LANES), 0)
                    across = across + jnp.sum(dx.reshape(span // 8, 8, LANES), 0)
        moved_ref[0, j] = jnp.sum(down) / size
        moved_ref[1, j] = jnp.sum(across) / size

        base = pl.multiple_of(top // 8 * 8, 8)
        lag = top - base

        there = lax.broadcasted_iota(jnp.int32, (size, reach), 1)
        gone = there - lax.broadcasted_iota(jnp.int32, (size, reach), 0)
        spread = jnp.where(gone == col, 1.0 - fx, jnp.where(gone == col + 1, fx, 0.0)).astype(bf16)
        for p in range(2):
            g = []
            for k in range(tiles):
                here = gs[p, k, pl.ds(8 - lag, tall), :]
                before = gs[p, k, pl.ds(7 - lag, tall), :]
                g.append((here + fy * (before - here)).astype(bf16))
            wide = jnp.dot(jnp.concatenate(g, axis=1), spread, preferred_element_type=f32)
            for k in range(tiles + 1):
                acc[first + k, p, pl.ds(base, tall), :] += wide[:, k * LANES : (k + 1) * LANES]

    @pl.loop(0, count_ref[0])
    def _(j):
        tile = left_ref[j] // LANES

        @pl.when((tile >= low) & (tile < high))
        def _():
            one(j)

    if carried:

        @pl.loop(0, keep)
        def _(k):
            for p in range(2):
                below_ref[k, p] = acc[k, p, rows : rows + size, :].astype(bf16)

    else:

        @pl.loop(0, size // span)
        def _(i):
            at = pl.multiple_of(i * span, span)
            for k in range(keep):
                for p in range(2):
                    temp[pl.ds(2 * k + p, span, stride=2 * keep + 1), :] = acc[k, p, pl.ds(rows + at, span), :]
            for y in range(span):
                below_ref[pl.ds(pl.multiple_of((at + y) * 2 * keep, ROWS), 2 * keep), :] = temp[
                    y * (2 * keep + 1) : y * (2 * keep + 1) + 2 * keep, :
                ].astype(bf16)


def step(modes, size, rows, slots, first_tile, low, high, keep, count, own, rim, carried, common):
    f32, bf16 = jnp.float32, jnp.bfloat16
    tiles = size // LANES
    deep = rows + size + 8
    vmem = pl.BlockSpec(memory_space=pltpu.VMEM)
    smem = pl.BlockSpec(memory_space=pltpu.SMEM)
    hbm = pl.BlockSpec(memory_space=pl.ANY)
    planes = (modes, 2, tiles, size, LANES)
    out_shape = [
        jax.ShapeDtypeStruct((count, 2, deep, LANES), f32),
        jax.ShapeDtypeStruct((keep, 2, size, LANES) if carried else (2 * keep * size, LANES), bf16),
        jax.ShapeDtypeStruct(planes, f32),
        jax.ShapeDtypeStruct((2, slots), f32),
    ]
    out_specs = [vmem, vmem, vmem, smem]
    own_arrays, own_parts = zip(*own)
    rim_arrays, rim_parts = zip(*rim)
    return pl.pallas_call(
        functools.partial(
            step_kernel, modes, size, rows, first_tile, low, high, keep, own_parts, rim_parts, bool(carried)
        ),
        out_shape=tuple(out_shape),
        in_specs=[smem] * 4 + [vmem] * 3 + [hbm] * (len(own) + len(rim)) + ([hbm, hbm, smem] if carried else []),
        out_specs=tuple(out_specs),
        scratch_shapes=[
            pltpu.VMEM((count, 2, rows + size, LANES), bf16),
            pltpu.VMEM((2, tiles, size + 32, LANES), f32),
            pltpu.VMEM((2, tiles, size + 32, LANES), f32),
            pltpu.VMEM((2, size, size), f32),
            pltpu.VMEM((2, modes, size, size), bf16),
            pltpu.VMEM((modes, 2, size, size), bf16),
            pltpu.VMEM((modes, 2, size, size), bf16),
            pltpu.VMEM((2, size // 2, size), bf16),
            pltpu.VMEM((2, tiles, size + 32, LANES), f32),
            pltpu.VMEM((32 * (2 * keep + 1) + 7, LANES), f32),
            pltpu.SemaphoreType.DMA((12,)),
        ],
        compiler_params=pltpu.CompilerParams(vmem_limit_bytes=30 << 20),
        cost_estimate=pl.CostEstimate(flops=3 << 30, bytes_accessed=16 << 20, transcendentals=0),
        name="step_b" if carried else "step_a",
    )(*common, *own_arrays, *rim_arrays, *carried)


def sort_kernel(lines, first, x_ref, out_ref, temp):
    n = out_ref.shape[2]
    line = 2 * lines
    start = 2 * first // ROWS * ROWS
    stop = -(-2 * (first + out_ref.shape[0]) // ROWS) * ROWS
    wide = stop - start + 1
    for y in range(n):
        temp[y * wide : (y + 1) * wide - 1, :] = x_ref[y * line + start : y * line + stop, :].astype(jnp.float32)
    for k in range(out_ref.shape[0]):
        for p in range(2):
            plane = temp[pl.ds(2 * (first + k) + p - start, n, stride=wide), :]
            out_ref[k, p] = plane.astype(jnp.bfloat16)


def sorted_planes(x, rows, lines, first, last):
    n = 128 if rows % 128 == 0 else rows
    return pl.pallas_call(
        functools.partial(sort_kernel, lines, first),
        grid=(rows // n,),
        out_shape=jax.ShapeDtypeStruct((last - first, 2, rows, LANES), jnp.bfloat16),
        in_specs=[pl.BlockSpec((n * lines * 2, LANES), lambda i: (i, 0))],
        out_specs=pl.BlockSpec((last - first, 2, n, LANES), lambda i: (0, 0, i, 0)),
        scratch_shapes=[pltpu.VMEM((n * (lines * 2 + 1) + 7, LANES), jnp.float32)],
        cost_estimate=pl.CostEstimate(flops=1 << 20, bytes_accessed=4 << 20, transcendentals=0),
        name="sort",
    )(x)


def prepare_kernel(tiles, x_ref, table_ref, measured_ref, out_ref, table_out, ordered_ref, temp):
    modes, _, size, _ = out_ref.shape
    slots = measured_ref.shape[0]
    span = 32
    table_out[...] = table_ref[0:4]

    @pl.loop(0, modes * (size // span))
    def _(i):
        at = pl.multiple_of(lax.rem(i, size // span) * span, span)
        m = i // (size // span)
        for p in range(2):
            for k in range(tiles):
                out_ref[m, p, pl.ds(at, span), k * LANES : (k + 1) * LANES] = x_ref[
                    pl.ds((i * span * tiles + k) * 2 + p, span, stride=2 * tiles), :
                ]

    @pl.loop(0, slots)
    def _(j):
        ordered = jnp.dot(measured_ref[j], table_ref[4], preferred_element_type=jnp.float32)
        for k in range(tiles):
            temp[k] = ordered[:, k * LANES : (k + 1) * LANES]
        for e in range(2):
            for k in range(tiles):
                ordered_ref[j, e, :, k * LANES : (k + 1) * LANES] = temp[
                    k, pl.ds(e, size // 2, stride=2), :
                ].astype(jnp.bfloat16)


def prepared(x, tables, measured, modes, size):
    vmem = pl.BlockSpec(memory_space=pltpu.VMEM)
    tiles = size // LANES
    return pl.pallas_call(
        functools.partial(prepare_kernel, tiles),
        out_shape=(
            jax.ShapeDtypeStruct((modes, 2, size, size), jnp.float32),
            jax.ShapeDtypeStruct((4, size, size), tables.dtype),
            jax.ShapeDtypeStruct((measured.shape[0], 2, size // 2, size), measured.dtype),
        ),
        in_specs=[vmem, vmem, vmem],
        out_specs=(vmem, vmem, vmem),
        scratch_shapes=[pltpu.VMEM((tiles, size, LANES), jnp.float32)],
        compiler_params=pltpu.CompilerParams(vmem_limit_bytes=16 << 20),
        cost_estimate=pl.CostEstimate(flops=1 << 20, bytes_accessed=8 << 20, transcendentals=0),
        name="prepare",
    )(x, tables, measured)


def tiled(x):
    *lead, two, width = x.shape
    n = math.prod(lead)
    x = x.reshape(n, two, width // LANES, LANES)
    return jnp.transpose(x, (0, 2, 1, 3)).reshape(-1, LANES)


def untiled(x, lead, width):
    n = math.prod(lead)
    x = jnp.transpose(x.reshape(n, width // LANES, 2, LANES), (0, 2, 1, 3))
    return x.reshape(*lead, 2, width)


def shards(object_tiles, probe, measured, offset_row, offset_col, subpixel, live_count):
    rows, _, width = object_tiles.shape
    modes, size = probe.shape[:2]
    slots = measured.shape[0]
    lines, tiles = width // LANES, size // LANES
    mid = lines // 2
    near = mid + tiles
    own = tiled(object_tiles)
    own_a = sorted_planes(own, rows, lines, 0, near)
    own_b = sorted_planes(own, rows, lines, near, lines)
    rim_a = passed_along(own_a[:, :, :size], "row", -1)
    rim_b = passed_along(own_b[:, :, :size], "row", -1)
    planes, tables, ordered = prepared(tiled(probe), dft_tables(size), measured, modes, size)
    common = (live_count, offset_row, offset_col, subpixel, planes, ordered, tables)
    whole = (0, near, 0)
    grad_a, below_a, sum_a, moved_a = step(
        modes, size, rows, slots, 0, 0, mid, mid, near, [(own_a, whole)], [(rim_a, whole)], (), common
    )
    landed_a = passed_along(below_a, "row", 1, odd=True)
    kept, rest = (mid, near, 0), (0, lines - near, tiles)
    grad_b, below_b, sums, moved = step(
        modes, size, rows, slots, mid, mid, lines, lines - mid, lines - mid,
        [(own_a, kept), (own_b, rest)], [(rim_a, kept), (rim_b, rest)], (grad_a, sum_a, moved_a), common,
    )
    probe_grad, grad, core_a, landed_b = summed(
        sums.reshape(-1, LANES), (grad_a, grad_b), below_a, below_b, modes, tiles, mid, rows, "row"
    )
    landed = jnp.concatenate(
        [(landed_a + core_a).reshape(size, 2 * mid, LANES), landed_b.reshape(size, 2 * (lines - mid), LANES)], axis=1
    )
    landed = lax.optimization_barrier(landed.reshape(-1, LANES))
    grad = grad.at[: landed.shape[0]].add(landed.astype(jnp.float32))
    return (untiled(grad, (rows,), width), untiled(probe_grad, (modes, size), size), moved)


def solution(mesh):
    in_specs = (
        P(("groups", "row"), None, None),
        P(),
        P(("groups", "row"), None, None),
        P(("groups", "row")),
        P(("groups", "row")),
        P(("groups", "row")),
        P(("groups", "row")),
    )
    out_specs = (
        P(("groups", "row"), None, None),
        P("groups", None, None, None),
        P(None, ("groups", "row")),
    )
    return jax.shard_map(shards, mesh=mesh, in_specs=in_specs, out_specs=out_specs, check_vma=False)
```

```python
import functools
import math

import jax
import jax.numpy as jnp
import numpy as np
from jax import lax
from jax.experimental import pallas as pl
from jax.experimental.pallas import tpu as pltpu
from jax.sharding import PartitionSpec as P

LANES = 128
ROWS = 16


def passed_along(x, axis, by, odd=False):
    length = lax.axis_size(axis)
    pairs = [(i, i + by) for i in range(odd, length, 1 + odd) if 0 <= i + by < length]
    return lax.ppermute(x, axis, pairs)


def total_kernel(
    length, pieces, modes, tiles, mid, x_ref, part_a, part_b, above_ref, below_ref, out_ref, grad_ref, came_a, came_b,
    near, send1, send2, got0, got1, got2, full, flat, temp, sends, recvs, down_sems,
):
    f32, bf16 = jnp.float32, jnp.bfloat16
    lines, width = x_ref.shape
    deep = length // 4
    me = lax.axis_index("row")
    c, b, k = me % 2, (me // 2) % 2, me // 4
    part = lines // pieces
    half, quarter = part // 2, part // 4
    leaf = quarter // deep

    def stage_near(q):
        near[pl.ds(q * half, half)] = x_ref[
            pl.ds(pl.multiple_of(q * part + (1 - c) * half, ROWS), half)
        ].astype(bf16)

    def peer(stage, o):
        if stage in (0, 5):
            return {"row": me + 1 - 2 * c}
        if stage in (1, 4):
            return {"row": me + 2 - 4 * b}
        return {"row": ((k + o) % deep) * 4 + me % 4}

    barrier = pltpu.get_barrier_semaphore()
    others = [(0, 0), (1, 0)] + [(2, o) for o in range(1, deep)]
    for stage, o in others:
        pl.semaphore_signal(barrier, inc=1, device_id=peer(stage, o), device_id_type=pl.DeviceIdType.MESH)

    @pl.when(me > 0)
    def _():
        pl.semaphore_signal(barrier, inc=1, device_id={"row": me - 1}, device_id_type=pl.DeviceIdType.MESH)

    @pl.when(me < length - 1)
    def _():
        pl.semaphore_signal(barrier, inc=1, device_id={"row": me + 1}, device_id_type=pl.DeviceIdType.MESH)

    for q in range(pieces):
        stage_near(q)

    @pl.when(c == 0)
    def _():
        came_a[...] = jnp.zeros_like(came_a)

    @pl.when(me == 0)
    def _():
        came_b[...] = jnp.zeros_like(came_b)

    pl.semaphore_wait(
        barrier, len(others) + (me > 0).astype(jnp.int32) + (me < length - 1).astype(jnp.int32)
    )
    early = flat.shape[0] // 8 * 5
    downs = []
    for n, (src, dst, first, last) in enumerate((
        (flat, came_b, 0, early),
        (flat, came_b, early, flat.shape[0]),
        (above_ref, came_a, 0, above_ref.shape[0]),
    )):
        at = pl.ds(first, last - first)
        downs.append(pltpu.make_async_remote_copy(
            src_ref=src.at[at], dst_ref=dst.at[at],
            send_sem=down_sems.at[n], recv_sem=down_sems.at[3 + n],
            device_id={"row": jnp.minimum(me + 1, length - 1)}, device_id_type=pl.DeviceIdType.MESH,
        ))

    def send_down(n):
        @pl.when((c == 0) if n == 2 else (me < length - 1))
        def _():
            downs[n].start()

    whole = 2 * (mid + part_b.shape[0])
    rows = grad_ref.shape[0] // whole
    block = 32

    def lay_out(part, out, first, line, many, high):
        @pl.loop(0, high // block)
        def _(i):
            at = pl.multiple_of(i * block, block)
            for t in range(many):
                for p in range(2):
                    temp[pl.ds(2 * t + p, block, stride=2 * many + 1), :] = part[t, p, pl.ds(at, block), :].astype(f32)
            for y in range(block):
                out[pl.ds(pl.multiple_of((at + y) * line + 2 * first, ROWS), 2 * many), :] = temp[
                    y * (2 * many + 1) : y * (2 * many + 1) + 2 * many, :
                ].astype(out.dtype)

    base = [0, pieces, 2 * pieces, (2 + deep) * pieces, (2 + 2 * deep) * pieces, (3 + 2 * deep) * pieces]

    def span_of(start, size):
        return pl.ds(pl.multiple_of(start, ROWS), size)

    def place(q, stage):
        start = q * part
        if stage == 0:
            return start
        start = start + c * half
        if stage == 1:
            return start
        start = start + b * quarter
        return start if stage == 2 else start + k * leaf

    def link(stage, q, o=0):
        at = span_of(q * quarter, quarter)
        if stage == 0:
            src, dst = near.at[span_of(q * half, half)], got0.at[span_of(q * half, half)]
        elif stage == 1:
            src, dst = send1.at[at], got1.at[at]
        elif stage == 2:
            src = send2.at[span_of(q * quarter + ((k + o) % deep) * leaf, leaf)]
            dst = got2.at[span_of((q * deep + o) * leaf, leaf)]
        elif stage == 3:
            src = dst = full.at[span_of(place(q, 3), leaf)]
        elif stage == 4:
            src = dst = full.at[span_of(place(q, 2), quarter)]
        else:
            src = dst = full.at[span_of(place(q, 1), half)]
        sem = base[stage] + (q * deep + o if stage in (2, 3) else q)
        return pltpu.make_async_remote_copy(
            src_ref=src, dst_ref=dst, send_sem=sends.at[sem], recv_sem=recvs.at[sem],
            device_id=peer(stage, o), device_id_type=pl.DeviceIdType.MESH,
        )

    started = []

    def begin(stage, q):
        for o in range(1, deep) if stage in (2, 3) else (0,):
            copy = link(stage, q, o)
            copy.start()
            started.append(copy)

    def arrive(stage, q):
        for o in range(1, deep) if stage in (2, 3) else (0,):
            link(stage, q, o).wait_recv()

    def act(stage, q):
        if stage == 0:
            pass
        elif stage == 1:
            arrive(0, q)
            away = q * part + c * half + (1 - b) * quarter
            send1[span_of(q * quarter, quarter)] = (
                x_ref[span_of(away, quarter)] + got0[span_of(q * half + (1 - b) * quarter, quarter)].astype(f32)
            ).astype(bf16)
        elif stage == 2:
            arrive(1, q)
            own = (
                x_ref[span_of(place(q, 2), quarter)]
                + got0[span_of(q * half + b * quarter, quarter)].astype(f32)
                + got1[span_of(q * quarter, quarter)].astype(f32)
            )
            send2[span_of(q * quarter, quarter)] = own.astype(bf16)
        elif stage == 3:
            arrive(2, q)
            own = (
                x_ref[span_of(place(q, 3), leaf)]
                + got0[span_of(q * half + b * quarter + k * leaf, leaf)].astype(f32)
                + got1[span_of(q * quarter + k * leaf, leaf)].astype(f32)
            )
            for o in range(1, deep):
                own = own + got2[span_of((q * deep + o) * leaf, leaf)].astype(f32)
            full[span_of(place(q, 3), leaf)] = own.astype(bf16)
        elif stage == 6:
            arrive(5, q)
            planes = modes * 2 * tiles
            size = lines // planes
            for plane in range(planes * q // pieces, planes * (q + 1) // pieces):
                m, p, tile = plane // (2 * tiles), plane // tiles % 2, plane % tiles
                out_ref[pl.ds((m * size * tiles + tile) * 2 + p, size, stride=2 * tiles), :] = full[
                    pl.ds(plane * size, size), :
                ].astype(f32)
            return
        else:
            arrive(stage - 1, q)
        begin(stage, q)

    for q in range(pieces):
        act(0, q)
    for stage in range(1, 7):
        for q in range(pieces):
            act(stage, q)
        if stage == 1:
            send_down(2)
            lay_out(below_ref, flat, 0, 2 * below_ref.shape[0], below_ref.shape[0], below_ref.shape[2])
            send_down(0)
        elif stage == 2:
            lay_out(part_a, grad_ref, 0, whole, mid, rows)
        elif stage == 3:
            lay_out(part_b, grad_ref, mid, whole, part_b.shape[0], rows)
        elif stage == 4:
            send_down(1)
    for copy in started:
        copy.wait_send()

    @pl.when(c == 0)
    def _():
        downs[2].wait_send()

    @pl.when(c == 1)
    def _():
        downs[2].wait_recv()

    for n in range(2):

        @pl.when(me < length - 1)
        def _():
            downs[n].wait_send()

        @pl.when(me > 0)
        def _():
            downs[n].wait_recv()


def summed(x, grads, above, below, modes, tiles, mid, rows, axis):
    length = lax.axis_size(axis)
    lines, width = x.shape
    f32, bf16 = jnp.float32, jnp.bfloat16
    pieces = next(n for n in (4, 2, 1) if n == 1 or lines % (length * ROWS * n) == 0)
    vmem = pl.BlockSpec(memory_space=pltpu.VMEM)
    count = pieces * (4 + 2 * (length // 4))
    total = 2 * rows * (mid + grads[1].shape[0])
    flat = (2 * below.shape[2] * below.shape[0], width)
    return pl.pallas_call(
        functools.partial(total_kernel, length, pieces, modes, tiles, mid),
        out_shape=(
            jax.ShapeDtypeStruct((lines, width), f32),
            jax.ShapeDtypeStruct((total, width), f32),
            jax.ShapeDtypeStruct(above.shape, bf16),
            jax.ShapeDtypeStruct(flat, bf16),
        ),
        in_specs=[vmem] * 5,
        out_specs=(vmem,) * 4,
        scratch_shapes=[
            pltpu.VMEM((lines // 2, width), bf16),
            pltpu.VMEM((lines // 4, width), bf16),
            pltpu.VMEM((lines // 4, width), bf16),
            pltpu.VMEM((lines // 2, width), bf16),
            pltpu.VMEM((lines // 4, width), bf16),
            pltpu.VMEM((lines // 4, width), bf16),
            pltpu.VMEM((lines, width), bf16),
            pltpu.VMEM(flat, bf16),
            pltpu.VMEM((32 * (2 * max(g.shape[0] for g in grads) + 1) + 7, width), f32),
            pltpu.SemaphoreType.DMA((count,)),
            pltpu.SemaphoreType.DMA((count,)),
            pltpu.SemaphoreType.DMA((6,)),
        ],
        compiler_params=pltpu.CompilerParams(collective_id=0, has_side_effects=True, vmem_limit_bytes=28 << 20),
        name="total",
    )(x, *grads, above, below)


def dft_tables(patch):
    index = np.arange(patch)
    angle = ((index[:, None] * index[None, :]) % patch).astype(np.float64) * (2.0 * math.pi / patch)
    scale = 1.0 / math.sqrt(patch)
    cosine, sine = np.cos(angle) * scale, np.sin(angle) * scale
    half = patch // 2
    tables = []
    for odd in range(2):
        c, s = cosine[:half, odd::2], sine[:half, odd::2]
        tables.append(np.block([[c, -s], [s, c]]))
        tables.append(np.block([[c.T, s.T], [-s.T, c.T]]))
    order = np.concatenate([index[0::2], index[1::2]])
    tables.append((index[:, None] == order[None, :]).astype(np.float64))
    stacked = np.stack(tables).astype(np.float32)
    return jnp.asarray(stacked).astype(jnp.bfloat16)


def step_kernel(
    modes, size, rows, first_tile, low, high, keep, own_parts, rim_parts, carried, *refs
):
    f32, bf16 = jnp.float32, jnp.bfloat16
    refs = list(refs)

    def take(n):
        got, refs[:] = refs[:n], refs[n:]
        return got

    count_ref, top_ref, left_ref, code_ref = take(4)
    probe, measured_ref, table_ref = take(3)
    owns, rims = take(len(own_parts)), take(len(rim_parts))
    if carried:
        handed_hbm, sum_hbm, before_ref = take(3)
    acc, below_ref, pgrad, moved_ref = take(4)
    (ext, rowx, slope, patch, waves, mids, far, ratios, gs,
     temp, sems) = refs
    tiles = size // LANES
    half = size // 2
    slots = measured_ref.shape[0]
    span = 32
    along, inverse_of = (0, 2), (1, 3)
    copies = []

    def fetch(src, dst):
        copy = pltpu.make_async_copy(src, dst, sems.at[len(copies)])
        copy.start()
        copies.append(copy)

    for sources, ranges, row, n in ((owns, own_parts, 0, rows), (rims, rim_parts, rows, size)):
        for source, (start, stop, to) in zip(sources, ranges):
            fetch(
                source.at[pl.ds(start, stop - start)],
                ext.at[pl.ds(to, stop - start), :, pl.ds(row, n), :],
            )
    overlap = 0
    if carried:
        overlap = handed_hbm.shape[0] - (low)
        fetch(handed_hbm.at[pl.ds(low, overlap)], acc.at[pl.ds(0, overlap)])
        fetch(sum_hbm, pgrad)
    else:
        pgrad[...] = jnp.zeros_like(pgrad)
    gs[...] = jnp.zeros_like(gs)

    @pl.loop(overlap, acc.shape[0])
    def _(k):
        for p in range(2):
            acc[k, p] = jnp.zeros(acc.shape[2:], f32)

    for j in range(slots):
        for p in range(2):
            moved_ref[p, j] = before_ref[p, j] if carried else 0.0
    for copy in copies:
        copy.wait()

    def one(j):
        top, left, code = top_ref[j], left_ref[j], code_ref[j]
        first = left // LANES
        col = left - first * LANES
        first = first - first_tile
        base_row = pl.multiple_of(top // ROWS * ROWS, ROWS)
        row = top - base_row
        fy = (code // 4).astype(f32) * 0.25
        fx = (code % 4).astype(f32) * 0.25
        reach = (tiles + 1) * LANES
        tall = size + ROWS
        here = lax.broadcasted_iota(jnp.int32, (reach, size), 0)
        away = here - lax.broadcasted_iota(jnp.int32, (reach, size), 1)
        at_left, at_right = away == col, away == col + 1
        mix = jnp.where(at_left, 1.0 - fx, jnp.where(at_right, fx, 0.0)).astype(bf16)
        tilt = jnp.where(at_left, -1.0, jnp.where(at_right, 1.0, 0.0)).astype(bf16)
        for p in range(2):
            window = jnp.concatenate(
                [ext[first + k, p, pl.ds(base_row, tall), :] for k in range(tiles + 1)], axis=1
            )
            for table, kept in ((mix, rowx), (tilt, slope)):
                cells = jnp.dot(window, table, preferred_element_type=f32)
                for k in range(tiles):
                    kept[p, k, 0:tall, :] = cells[:, k * LANES : (k + 1) * LANES]
        for p in range(2):
            for k in range(tiles):
                for i in range(size // span):
                    upper = rowx[p, k, pl.ds(row + i * span, span), :]
                    lower = rowx[p, k, pl.ds(row + i * span + 1, span), :]
                    patch[p, i * span : (i + 1) * span, k * LANES : (k + 1) * LANES] = upper + fy * (lower - upper)


        share = size // modes
        short = share // 2

        def wave(c):
            for h in range(2):
                at = slice(h * half + c * short, h * half + (c + 1) * short)
                re, im = patch[0, at, :], patch[1, at, :]
                for m in range(modes):
                    here = slice(m * share + h * short, m * share + (h + 1) * short)
                    pr, pi = probe[m, 0, at, :], probe[m, 1, at, :]
                    for q, w in enumerate((pr * re - pi * im, pr * im + pi * re)):
                        to = slice(q * half, (q + 1) * half)
                        waves[0, c, here, to] = (w[:, :half] + w[:, half:]).astype(bf16)
                        waves[1, c, here, to] = (w[:, :half] - w[:, half:]).astype(bf16)

        def along_columns(c):
            for e in range(2):
                h = jnp.dot(waves[e, c], table_ref[along[e]], preferred_element_type=f32)
                to = slice(e * half, (e + 1) * half)
                for m in range(modes):
                    for q in range(2):
                        upper = h[m * share : m * share + short, q * half : (q + 1) * half]
                        lower = h[m * share + short : (m + 1) * share, q * half : (q + 1) * half]
                        at = slice(q * half + c * short, q * half + (c + 1) * short)
                        mids[m, 0, at, to] = (upper + lower).astype(bf16)
                        mids[m, 1, at, to] = (upper - lower).astype(bf16)

        def along_rows(e):
            strength = 0.0
            for m in range(modes):
                f = jnp.dot(table_ref[inverse_of[e]], mids[m, e], preferred_element_type=f32)
                far[m, e] = f.astype(far.dtype)
                strength = strength + (f[:half] * f[:half] + f[half:] * f[half:])
            ratio = 1.0 - measured_ref[j, e].astype(f32) * jnp.minimum(lax.rsqrt(strength), 2.0)
            ratios[e] = ratio.astype(bf16)

        def skewed(*stages):
            for t in range(modes + len(stages) - 1):
                for n in reversed(range(len(stages))):
                    if 0 <= t - n < modes:
                        stages[n](t - n)

        skewed(wave, along_columns)
        for e in range(2):
            along_rows(e)

        def error(m):
            for e in range(2):
                ratio = ratios[e]
                mids[m, e, 0:half, :] = far[m, e, 0:half, :] * ratio
                mids[m, e, half:size, :] = far[m, e, half:size, :] * ratio

        def back_rows(m):
            parts = [jnp.dot(table_ref[along[e]], mids[m, e], preferred_element_type=f32) for e in range(2)]
            for h, both in enumerate((parts[0] + parts[1], parts[0] - parts[1])):
                for e in range(2):
                    for q in range(2):
                        to, at = slice(q * half, (q + 1) * half), slice(e * half, (e + 1) * half)
                        for n in range(half // share):
                            waves[e, h * (half // share) + n, m * share : (m + 1) * share, to] = both[
                                q * half + n * share : q * half + (n + 1) * share, at
                            ].astype(bf16)

        def back_columns(c):
            back = [jnp.dot(waves[e, c], table_ref[inverse_of[e]], preferred_element_type=f32) for e in range(2)]
            for i in range(share // span):
                start = c * share + i * span
                at = slice(start, start + span)
                for k in range(2):
                    to = slice(k * half, (k + 1) * half)
                    re, im = patch[0, at, to], patch[1, at, to]
                    sums = [0.0, 0.0]
                    for m in range(modes):
                        here = slice(m * share + i * span, m * share + (i + 1) * span)
                        b0, b1 = back[0][here], back[1][here]
                        mixed = b0 + b1 if k == 0 else b0 - b1
                        ur, ui = mixed[:, :half], mixed[:, half:]
                        pr, pi = probe[m, 0, at, to], probe[m, 1, at, to]
                        sums[0] = sums[0] + (pr * ur + pi * ui)
                        sums[1] = sums[1] + (pr * ui - pi * ur)
                        pgrad[m, 0, k, at, :] += re * ur + im * ui
                        pgrad[m, 1, k, at, :] += re * ui - im * ur
                    for p in range(2):
                        gs[p, k, 8 + start : 8 + start + span, :] = sums[p]

        skewed(error, back_rows)
        skewed(back_columns)

        down, across = jnp.zeros((8, LANES), f32), jnp.zeros((8, LANES), f32)
        for i in range(size // span):
            for p in range(2):
                for k in range(tiles):
                    at, after = pl.ds(row + i * span, span), pl.ds(row + i * span + 1, span)
                    g = gs[p, k, 8 + i * span : 8 + (i + 1) * span, :]
                    dy = g * (rowx[p, k, after, :] - rowx[p, k, at, :])
                    upper = slope[p, k, at, :]
                    dx = g * (upper + fy * (slope[p, k, after, :] - upper))
                    down = down + jnp.sum(dy.reshape(span // 8, 8, LANES), 0)
                    across = across + jnp.sum(dx.reshape(span // 8, 8, LANES), 0)
        moved_ref[0, j] = jnp.sum(down) / size
        moved_ref[1, j] = jnp.sum(across) / size

        base = pl.multiple_of(top // 8 * 8, 8)
        lag = top - base

        for p in range(2):
            g = []
            for k in range(tiles):
                here = gs[p, k, pl.ds(8 - lag, tall), :]
                before = gs[p, k, pl.ds(7 - lag, tall), :]
                g.append((here + fy * (before - here)).astype(bf16))
            wide = lax.dot_general(
                jnp.concatenate(g, axis=1), mix, (((1,), (1,)), ((), ())), preferred_element_type=f32
            )
            for k in range(tiles + 1):
                acc[first + k, p, pl.ds(base, tall), :] += wide[:, k * LANES : (k + 1) * LANES]

    @pl.loop(0, count_ref[0])
    def _(j):
        tile = left_ref[j] // LANES

        @pl.when((tile >= low) & (tile < high))
        def _():
            one(j)

    if carried:

        @pl.loop(0, keep)
        def _(k):
            for p in range(2):
                below_ref[k, p] = acc[k, p, rows : rows + size, :].astype(bf16)

    else:

        @pl.loop(0, size // span)
        def _(i):
            at = pl.multiple_of(i * span, span)
            for k in range(keep):
                for p in range(2):
                    temp[pl.ds(2 * k + p, span, stride=2 * keep + 1), :] = acc[k, p, pl.ds(rows + at, span), :]
            for y in range(span):
                below_ref[pl.ds(pl.multiple_of((at + y) * 2 * keep, ROWS), 2 * keep), :] = temp[
                    y * (2 * keep + 1) : y * (2 * keep + 1) + 2 * keep, :
                ].astype(bf16)


def step(modes, size, rows, slots, first_tile, low, high, keep, count, own, rim, carried, common):
    f32, bf16 = jnp.float32, jnp.bfloat16
    tiles = size // LANES
    deep = rows + size + 8
    vmem = pl.BlockSpec(memory_space=pltpu.VMEM)
    smem = pl.BlockSpec(memory_space=pltpu.SMEM)
    hbm = pl.BlockSpec(memory_space=pl.ANY)
    planes = (modes, 2, tiles, size, LANES)
    out_shape = [
        jax.ShapeDtypeStruct((count, 2, deep, LANES), f32),
        jax.ShapeDtypeStruct((keep, 2, size, LANES) if carried else (2 * keep * size, LANES), bf16),
        jax.ShapeDtypeStruct(planes, f32),
        jax.ShapeDtypeStruct((2, slots), f32),
    ]
    out_specs = [vmem, vmem, vmem, smem]
    own_arrays, own_parts = zip(*own)
    rim_arrays, rim_parts = zip(*rim)
    return pl.pallas_call(
        functools.partial(
            step_kernel, modes, size, rows, first_tile, low, high, keep, own_parts, rim_parts, bool(carried)
        ),
        out_shape=tuple(out_shape),
        in_specs=[smem] * 4 + [vmem] * 3 + [hbm] * (len(own) + len(rim)) + ([hbm, hbm, smem] if carried else []),
        out_specs=tuple(out_specs),
        scratch_shapes=[
            pltpu.VMEM((count, 2, rows + size, LANES), bf16),
            pltpu.VMEM((2, tiles, size + 32, LANES), f32),
            pltpu.VMEM((2, tiles, size + 32, LANES), f32),
            pltpu.VMEM((2, size, size), f32),
            pltpu.VMEM((2, modes, size, size), bf16),
            pltpu.VMEM((modes, 2, size, size), bf16),
            pltpu.VMEM((modes, 2, size, size), bf16),
            pltpu.VMEM((2, size // 2, size), bf16),
            pltpu.VMEM((2, tiles, size + 32, LANES), f32),
            pltpu.VMEM((32 * (2 * keep + 1) + 7, LANES), f32),
            pltpu.SemaphoreType.DMA((12,)),
        ],
        compiler_params=pltpu.CompilerParams(vmem_limit_bytes=30 << 20),
        cost_estimate=pl.CostEstimate(flops=3 << 30, bytes_accessed=16 << 20, transcendentals=0),
        name="step_b" if carried else "step_a",
    )(*common, *own_arrays, *rim_arrays, *carried)


def sort_kernel(lines, first, x_ref, out_ref, temp):
    n = out_ref.shape[2]
    line = 2 * lines
    start = 2 * first // ROWS * ROWS
    stop = -(-2 * (first + out_ref.shape[0]) // ROWS) * ROWS
    wide = stop - start + 1
    for y in range(n):
        temp[y * wide : (y + 1) * wide - 1, :] = x_ref[y * line + start : y * line + stop, :].astype(jnp.float32)
    for k in range(out_ref.shape[0]):
        for p in range(2):
            plane = temp[pl.ds(2 * (first + k) + p - start, n, stride=wide), :]
            out_ref[k, p] = plane.astype(jnp.bfloat16)


def sorted_planes(x, rows, lines, first, last):
    n = 128 if rows % 128 == 0 else rows
    return pl.pallas_call(
        functools.partial(sort_kernel, lines, first),
        grid=(rows // n,),
        out_shape=jax.ShapeDtypeStruct((last - first, 2, rows, LANES), jnp.bfloat16),
        in_specs=[pl.BlockSpec((n * lines * 2, LANES), lambda i: (i, 0))],
        out_specs=pl.BlockSpec((last - first, 2, n, LANES), lambda i: (0, 0, i, 0)),
        scratch_shapes=[pltpu.VMEM((n * (lines * 2 + 1) + 7, LANES), jnp.float32)],
        cost_estimate=pl.CostEstimate(flops=1 << 20, bytes_accessed=4 << 20, transcendentals=0),
        name="sort",
    )(x)


def prepare_kernel(tiles, x_ref, table_ref, measured_ref, out_ref, table_out, ordered_ref, temp):
    modes, _, size, _ = out_ref.shape
    slots = measured_ref.shape[0]
    span = 32
    table_out[...] = table_ref[0:4]

    @pl.loop(0, modes * (size // span))
    def _(i):
        at = pl.multiple_of(lax.rem(i, size // span) * span, span)
        m = i // (size // span)
        for p in range(2):
            for k in range(tiles):
                out_ref[m, p, pl.ds(at, span), k * LANES : (k + 1) * LANES] = x_ref[
                    pl.ds((i * span * tiles + k) * 2 + p, span, stride=2 * tiles), :
                ]

    @pl.loop(0, slots)
    def _(j):
        ordered = jnp.dot(measured_ref[j], table_ref[4], preferred_element_type=jnp.float32)
        for k in range(tiles):
            temp[k] = ordered[:, k * LANES : (k + 1) * LANES]
        for e in range(2):
            for k in range(tiles):
                ordered_ref[j, e, :, k * LANES : (k + 1) * LANES] = temp[
                    k, pl.ds(e, size // 2, stride=2), :
                ].astype(jnp.bfloat16)


def prepared(x, tables, measured, modes, size):
    vmem = pl.BlockSpec(memory_space=pltpu.VMEM)
    tiles = size // LANES
    return pl.pallas_call(
        functools.partial(prepare_kernel, tiles),
        out_shape=(
            jax.ShapeDtypeStruct((modes, 2, size, size), jnp.float32),
            jax.ShapeDtypeStruct((4, size, size), tables.dtype),
            jax.ShapeDtypeStruct((measured.shape[0], 2, size // 2, size), measured.dtype),
        ),
        in_specs=[vmem, vmem, vmem],
        out_specs=(vmem, vmem, vmem),
        scratch_shapes=[pltpu.VMEM((tiles, size, LANES), jnp.float32)],
        compiler_params=pltpu.CompilerParams(vmem_limit_bytes=16 << 20),
        cost_estimate=pl.CostEstimate(flops=1 << 20, bytes_accessed=8 << 20, transcendentals=0),
        name="prepare",
    )(x, tables, measured)


def tiled(x):
    *lead, two, width = x.shape
    n = math.prod(lead)
    x = x.reshape(n, two, width // LANES, LANES)
    return jnp.transpose(x, (0, 2, 1, 3)).reshape(-1, LANES)


def untiled(x, lead, width):
    n = math.prod(lead)
    x = jnp.transpose(x.reshape(n, width // LANES, 2, LANES), (0, 2, 1, 3))
    return x.reshape(*lead, 2, width)


def shards(object_tiles, probe, measured, offset_row, offset_col, subpixel, live_count):
    rows, _, width = object_tiles.shape
    modes, size = probe.shape[:2]
    slots = measured.shape[0]
    lines, tiles = width // LANES, size // LANES
    mid = lines // 2
    near = mid + tiles
    own = tiled(object_tiles)
    own_a = sorted_planes(own, rows, lines, 0, near)
    own_b = sorted_planes(own, rows, lines, near, lines)
    rim_a = passed_along(own_a[:, :, :size], "row", -1)
    rim_b = passed_along(own_b[:, :, :size], "row", -1)
    planes, tables, ordered = prepared(tiled(probe), dft_tables(size), measured, modes, size)
    common = (live_count, offset_row, offset_col, subpixel, planes, ordered, tables)
    whole = (0, near, 0)
    grad_a, below_a, sum_a, moved_a = step(
        modes, size, rows, slots, 0, 0, mid, mid, near, [(own_a, whole)], [(rim_a, whole)], (), common
    )
    landed_a = passed_along(below_a, "row", 1, odd=True)
    kept, rest = (mid, near, 0), (0, lines - near, tiles)
    grad_b, below_b, sums, moved = step(
        modes, size, rows, slots, mid, mid, lines, lines - mid, lines - mid,
        [(own_a, kept), (own_b, rest)], [(rim_a, kept), (rim_b, rest)], (grad_a, sum_a, moved_a), common,
    )
    probe_grad, grad, core_a, landed_b = summed(
        sums.reshape(-1, LANES), (grad_a, grad_b), below_a, below_b, modes, tiles, mid, rows, "row"
    )
    landed = jnp.concatenate(
        [(landed_a + core_a).reshape(size, 2 * mid, LANES), landed_b.reshape(size, 2 * (lines - mid), LANES)], axis=1
    )
    landed = lax.optimization_barrier(landed.reshape(-1, LANES))
    grad = grad.at[: landed.shape[0]].add(landed.astype(jnp.float32))
    return (untiled(grad, (rows,), width), untiled(probe_grad, (modes, size), size), moved)


def solution(mesh):
    in_specs = (
        P(("groups", "row"), None, None),
        P(),
        P(("groups", "row"), None, None),
        P(("groups", "row")),
        P(("groups", "row")),
        P(("groups", "row")),
        P(("groups", "row")),
    )
    out_specs = (
        P(("groups", "row"), None, None),
        P("groups", None, None, None),
        P(None, ("groups", "row")),
    )
    return jax.shard_map(shards, mesh=mesh, in_specs=in_specs, out_specs=out_specs, check_vma=False)
```

```python
import functools
import math

import jax
import jax.numpy as jnp
import numpy as np
from jax import lax
from jax.experimental import pallas as pl
from jax.experimental.pallas import tpu as pltpu
from jax.sharding import PartitionSpec as P

LANES = 128
ROWS = 16


def passed_along(x, axis, by, odd=False):
    length = lax.axis_size(axis)
    pairs = [(i, i + by) for i in range(odd, length, 1 + odd) if 0 <= i + by < length]
    return lax.ppermute(x, axis, pairs)


def total_kernel(
    length, pieces, modes, tiles, mid, x_ref, part_a, part_b, above_ref, below_ref, out_ref, grad_ref, came_a, came_b,
    near, send1, send2, got0, got1, got2, full, flat, temp, sends, recvs, down_sems,
):
    f32, bf16 = jnp.float32, jnp.bfloat16
    lines, width = x_ref.shape
    deep = length // 4
    me = lax.axis_index("row")
    c, b, k = me % 2, (me // 2) % 2, me // 4
    part = lines // pieces
    half, quarter = part // 2, part // 4
    leaf = quarter // deep

    def stage_near(q):
        near[pl.ds(q * half, half)] = x_ref[
            pl.ds(pl.multiple_of(q * part + (1 - c) * half, ROWS), half)
        ].astype(bf16)

    def peer(stage, o):
        if stage in (0, 5):
            return {"row": me + 1 - 2 * c}
        if stage in (1, 4):
            return {"row": me + 2 - 4 * b}
        return {"row": ((k + o) % deep) * 4 + me % 4}

    barrier = pltpu.get_barrier_semaphore()
    others = [(0, 0), (1, 0)] + [(2, o) for o in range(1, deep)]
    for stage, o in others:
        pl.semaphore_signal(barrier, inc=1, device_id=peer(stage, o), device_id_type=pl.DeviceIdType.MESH)

    @pl.when(me > 0)
    def _():
        pl.semaphore_signal(barrier, inc=1, device_id={"row": me - 1}, device_id_type=pl.DeviceIdType.MESH)

    @pl.when(me < length - 1)
    def _():
        pl.semaphore_signal(barrier, inc=1, device_id={"row": me + 1}, device_id_type=pl.DeviceIdType.MESH)

    for q in range(pieces):
        stage_near(q)

    pl.semaphore_wait(
        barrier, len(others) + (me > 0).astype(jnp.int32) + (me < length - 1).astype(jnp.int32)
    )
    early = flat.shape[0] // 8 * 5
    downs = []
    for n, (src, dst, first, last) in enumerate((
        (flat, came_b, 0, early),
        (flat, came_b, early, flat.shape[0]),
        (above_ref, came_a, 0, above_ref.shape[0]),
    )):
        at = pl.ds(first, last - first)
        downs.append(pltpu.make_async_remote_copy(
            src_ref=src.at[at], dst_ref=dst.at[at],
            send_sem=down_sems.at[n], recv_sem=down_sems.at[3 + n],
            device_id={"row": jnp.minimum(me + 1, length - 1)}, device_id_type=pl.DeviceIdType.MESH,
        ))

    def send_down(n):
        @pl.when((c == 0) if n == 2 else (me < length - 1))
        def _():
            downs[n].start()

    whole = 2 * (mid + part_b.shape[0])
    rows = grad_ref.shape[0] // whole
    block = 32

    def lay_out(part, out, first, line, many, high):
        @pl.loop(0, high // block)
        def _(i):
            at = pl.multiple_of(i * block, block)
            for t in range(many):
                for p in range(2):
                    temp[pl.ds(2 * t + p, block, stride=2 * many + 1), :] = part[t, p, pl.ds(at, block), :].astype(f32)
            for y in range(block):
                out[pl.ds(pl.multiple_of((at + y) * line + 2 * first, ROWS), 2 * many), :] = temp[
                    y * (2 * many + 1) : y * (2 * many + 1) + 2 * many, :
                ].astype(out.dtype)

    base = [0, pieces, 2 * pieces, (2 + deep) * pieces, (2 + 2 * deep) * pieces, (3 + 2 * deep) * pieces]

    def span_of(start, size):
        return pl.ds(pl.multiple_of(start, ROWS), size)

    def place(q, stage):
        start = q * part
        if stage == 0:
            return start
        start = start + c * half
        if stage == 1:
            return start
        start = start + b * quarter
        return start if stage == 2 else start + k * leaf

    def link(stage, q, o=0):
        at = span_of(q * quarter, quarter)
        if stage == 0:
            src, dst = near.at[span_of(q * half, half)], got0.at[span_of(q * half, half)]
        elif stage == 1:
            src, dst = send1.at[at], got1.at[at]
        elif stage == 2:
            src = send2.at[span_of(q * quarter + ((k + o) % deep) * leaf, leaf)]
            dst = got2.at[span_of((q * deep + o) * leaf, leaf)]
        elif stage == 3:
            src = dst = full.at[span_of(place(q, 3), leaf)]
        elif stage == 4:
            src = dst = full.at[span_of(place(q, 2), quarter)]
        else:
            src = dst = full.at[span_of(place(q, 1), half)]
        sem = base[stage] + (q * deep + o if stage in (2, 3) else q)
        return pltpu.make_async_remote_copy(
            src_ref=src, dst_ref=dst, send_sem=sends.at[sem], recv_sem=recvs.at[sem],
            device_id=peer(stage, o), device_id_type=pl.DeviceIdType.MESH,
        )

    started = []

    def begin(stage, q):
        for o in range(1, deep) if stage in (2, 3) else (0,):
            copy = link(stage, q, o)
            copy.start()
            started.append(copy)

    def arrive(stage, q):
        for o in range(1, deep) if stage in (2, 3) else (0,):
            link(stage, q, o).wait_recv()

    def act(stage, q):
        if stage == 0:
            pass
        elif stage == 1:
            arrive(0, q)
            away = q * part + c * half + (1 - b) * quarter
            send1[span_of(q * quarter, quarter)] = (
                x_ref[span_of(away, quarter)] + got0[span_of(q * half + (1 - b) * quarter, quarter)].astype(f32)
            ).astype(bf16)
        elif stage == 2:
            arrive(1, q)
            own = (
                x_ref[span_of(place(q, 2), quarter)]
                + got0[span_of(q * half + b * quarter, quarter)].astype(f32)
                + got1[span_of(q * quarter, quarter)].astype(f32)
            )
            send2[span_of(q * quarter, quarter)] = own.astype(bf16)
        elif stage == 3:
            arrive(2, q)
            own = (
                x_ref[span_of(place(q, 3), leaf)]
                + got0[span_of(q * half + b * quarter + k * leaf, leaf)].astype(f32)
                + got1[span_of(q * quarter + k * leaf, leaf)].astype(f32)
            )
            for o in range(1, deep):
                own = own + got2[span_of((q * deep + o) * leaf, leaf)].astype(f32)
            full[span_of(place(q, 3), leaf)] = own.astype(bf16)
        elif stage == 6:
            arrive(5, q)
            planes = modes * 2 * tiles
            size = lines // planes
            for plane in range(planes * q // pieces, planes * (q + 1) // pieces):
                m, p, tile = plane // (2 * tiles), plane // tiles % 2, plane % tiles
                out_ref[pl.ds((m * size * tiles + tile) * 2 + p, size, stride=2 * tiles), :] = full[
                    pl.ds(plane * size, size), :
                ].astype(f32)
            return
        else:
            arrive(stage - 1, q)
        begin(stage, q)

    for q in range(pieces):
        act(0, q)
    for stage in range(1, 7):
        for q in range(pieces):
            act(stage, q)
        if stage == 1:
            send_down(2)
            lay_out(below_ref, flat, 0, 2 * below_ref.shape[0], below_ref.shape[0], below_ref.shape[2])
            send_down(0)
        elif stage == 2:
            lay_out(part_a, grad_ref, 0, whole, mid, rows)

            @pl.when(c == 0)
            def _():
                came_a[...] = jnp.zeros_like(came_a)

            @pl.when(me == 0)
            def _():
                came_b[...] = jnp.zeros_like(came_b)

        elif stage == 3:
            lay_out(part_b, grad_ref, mid, whole, part_b.shape[0], rows)
        elif stage == 4:
            send_down(1)
    for copy in started:
        copy.wait_send()

    @pl.when(c == 0)
    def _():
        downs[2].wait_send()

    @pl.when(c == 1)
    def _():
        downs[2].wait_recv()

    for n in range(2):

        @pl.when(me < length - 1)
        def _():
            downs[n].wait_send()

        @pl.when(me > 0)
        def _():
            downs[n].wait_recv()


def summed(x, grads, above, below, modes, tiles, mid, rows, axis):
    length = lax.axis_size(axis)
    lines, width = x.shape
    f32, bf16 = jnp.float32, jnp.bfloat16
    pieces = next(n for n in (4, 2, 1) if n == 1 or lines % (length * ROWS * n) == 0)
    vmem = pl.BlockSpec(memory_space=pltpu.VMEM)
    count = pieces * (4 + 2 * (length // 4))
    total = 2 * rows * (mid + grads[1].shape[0])
    flat = (2 * below.shape[2] * below.shape[0], width)
    return pl.pallas_call(
        functools.partial(total_kernel, length, pieces, modes, tiles, mid),
        out_shape=(
            jax.ShapeDtypeStruct((lines, width), f32),
            jax.ShapeDtypeStruct((total, width), f32),
            jax.ShapeDtypeStruct(above.shape, bf16),
            jax.ShapeDtypeStruct(flat, bf16),
        ),
        in_specs=[vmem] * 5,
        out_specs=(vmem,) * 4,
        scratch_shapes=[
            pltpu.VMEM((lines // 2, width), bf16),
            pltpu.VMEM((lines // 4, width), bf16),
            pltpu.VMEM((lines // 4, width), bf16),
            pltpu.VMEM((lines // 2, width), bf16),
            pltpu.VMEM((lines // 4, width), bf16),
            pltpu.VMEM((lines // 4, width), bf16),
            pltpu.VMEM((lines, width), bf16),
            pltpu.VMEM(flat, bf16),
            pltpu.VMEM((32 * (2 * max(g.shape[0] for g in grads) + 1) + 7, width), f32),
            pltpu.SemaphoreType.DMA((count,)),
            pltpu.SemaphoreType.DMA((count,)),
            pltpu.SemaphoreType.DMA((6,)),
        ],
        compiler_params=pltpu.CompilerParams(collective_id=0, has_side_effects=True, vmem_limit_bytes=28 << 20),
        name="total",
    )(x, *grads, above, below)


def dft_tables(patch):
    index = np.arange(patch)
    angle = ((index[:, None] * index[None, :]) % patch).astype(np.float64) * (2.0 * math.pi / patch)
    scale = 1.0 / math.sqrt(patch)
    cosine, sine = np.cos(angle) * scale, np.sin(angle) * scale
    half = patch // 2
    tables = []
    for odd in range(2):
        c, s = cosine[:half, odd::2], sine[:half, odd::2]
        tables.append(np.block([[c, -s], [s, c]]))
        tables.append(np.block([[c.T, s.T], [-s.T, c.T]]))
    order = np.concatenate([index[0::2], index[1::2]])
    tables.append((index[:, None] == order[None, :]).astype(np.float64))
    stacked = np.stack(tables).astype(np.float32)
    return jnp.asarray(stacked).astype(jnp.bfloat16)


def step_kernel(
    modes, size, rows, first_tile, low, high, keep, own_parts, rim_parts, carried, *refs
):
    f32, bf16 = jnp.float32, jnp.bfloat16
    refs = list(refs)

    def take(n):
        got, refs[:] = refs[:n], refs[n:]
        return got

    count_ref, top_ref, left_ref, code_ref = take(4)
    probe, measured_ref, table_ref = take(3)
    owns, rims = take(len(own_parts)), take(len(rim_parts))
    if carried:
        handed_hbm, sum_hbm, before_ref = take(3)
    acc, below_ref, pgrad, moved_ref = take(4)
    (ext, rowx, slope, patch, waves, mids, far, ratios, gs,
     temp, sems) = refs
    tiles = size // LANES
    half = size // 2
    slots = measured_ref.shape[0]
    span = 32
    along, inverse_of = (0, 2), (1, 3)
    copies = []

    def fetch(src, dst):
        copy = pltpu.make_async_copy(src, dst, sems.at[len(copies)])
        copy.start()
        copies.append(copy)

    for sources, ranges, row, n in ((owns, own_parts, 0, rows), (rims, rim_parts, rows, size)):
        for source, (start, stop, to) in zip(sources, ranges):
            fetch(
                source.at[pl.ds(start, stop - start)],
                ext.at[pl.ds(to, stop - start), :, pl.ds(row, n), :],
            )
    overlap = 0
    if carried:
        overlap = handed_hbm.shape[0] - (low)
        fetch(handed_hbm.at[pl.ds(low, overlap)], acc.at[pl.ds(0, overlap)])
        fetch(sum_hbm, pgrad)
    else:
        pgrad[...] = jnp.zeros_like(pgrad)
    gs[...] = jnp.zeros_like(gs)

    @pl.loop(overlap, acc.shape[0])
    def _(k):
        for p in range(2):
            acc[k, p] = jnp.zeros(acc.shape[2:], f32)

    for j in range(slots):
        for p in range(2):
            moved_ref[p, j] = before_ref[p, j] if carried else 0.0
    for copy in copies:
        copy.wait()

    def one(j):
        top, left, code = top_ref[j], left_ref[j], code_ref[j]
        first = left // LANES
        col = left - first * LANES
        first = first - first_tile
        base_row = pl.multiple_of(top // ROWS * ROWS, ROWS)
        row = top - base_row
        fy = (code // 4).astype(f32) * 0.25
        fx = (code % 4).astype(f32) * 0.25
        reach = (tiles + 1) * LANES
        tall = size + ROWS
        here = lax.broadcasted_iota(jnp.int32, (reach, size), 0)
        away = here - lax.broadcasted_iota(jnp.int32, (reach, size), 1)
        at_left, at_right = away == col, away == col + 1
        mix = jnp.where(at_left, 1.0 - fx, jnp.where(at_right, fx, 0.0)).astype(bf16)
        tilt = jnp.where(at_left, -1.0, jnp.where(at_right, 1.0, 0.0)).astype(bf16)
        for p in range(2):
            window = jnp.concatenate(
                [ext[first + k, p, pl.ds(base_row, tall), :] for k in range(tiles + 1)], axis=1
            )
            for table, kept in ((mix, rowx), (tilt, slope)):
                cells = jnp.dot(window, table, preferred_element_type=f32)
                for k in range(tiles):
                    kept[p, k, 0:tall, :] = cells[:, k * LANES : (k + 1) * LANES]
        for p in range(2):
            for k in range(tiles):
                for i in range(size // span):
                    upper = rowx[p, k, pl.ds(row + i * span, span), :]
                    lower = rowx[p, k, pl.ds(row + i * span + 1, span), :]
                    patch[p, i * span : (i + 1) * span, k * LANES : (k + 1) * LANES] = upper + fy * (lower - upper)


        share = size // modes
        short = share // 2

        def wave(c):
            for h in range(2):
                at = slice(h * half + c * short, h * half + (c + 1) * short)
                re, im = patch[0, at, :], patch[1, at, :]
                for m in range(modes):
                    here = slice(m * share + h * short, m * share + (h + 1) * short)
                    pr, pi = probe[m, 0, at, :], probe[m, 1, at, :]
                    for q, w in enumerate((pr * re - pi * im, pr * im + pi * re)):
                        to = slice(q * half, (q + 1) * half)
                        waves[0, c, here, to] = (w[:, :half] + w[:, half:]).astype(bf16)
                        waves[1, c, here, to] = (w[:, :half] - w[:, half:]).astype(bf16)

        def along_columns(c):
            for e in range(2):
                h = jnp.dot(waves[e, c], table_ref[along[e]], preferred_element_type=f32)
                to = slice(e * half, (e + 1) * half)
                for m in range(modes):
                    for q in range(2):
                        upper = h[m * share : m * share + short, q * half : (q + 1) * half]
                        lower = h[m * share + short : (m + 1) * share, q * half : (q + 1) * half]
                        at = slice(q * half + c * short, q * half + (c + 1) * short)
                        mids[m, 0, at, to] = (upper + lower).astype(bf16)
                        mids[m, 1, at, to] = (upper - lower).astype(bf16)

        def along_rows(e):
            strength = 0.0
            for m in range(modes):
                f = jnp.dot(table_ref[inverse_of[e]], mids[m, e], preferred_element_type=f32)
                far[m, e] = f.astype(far.dtype)
                strength = strength + (f[:half] * f[:half] + f[half:] * f[half:])
            ratio = 1.0 - measured_ref[j, e].astype(f32) * jnp.minimum(lax.rsqrt(strength), 2.0)
            ratios[e] = ratio.astype(bf16)

        def skewed(*stages):
            for t in range(modes + len(stages) - 1):
                for n in reversed(range(len(stages))):
                    if 0 <= t - n < modes:
                        stages[n](t - n)

        skewed(wave, along_columns)
        for e in range(2):
            along_rows(e)

        def error(m):
            for e in range(2):
                ratio = ratios[e]
                mids[m, e, 0:half, :] = far[m, e, 0:half, :] * ratio
                mids[m, e, half:size, :] = far[m, e, half:size, :] * ratio

        def back_rows(m):
            parts = [jnp.dot(table_ref[along[e]], mids[m, e], preferred_element_type=f32) for e in range(2)]
            for h, both in enumerate((parts[0] + parts[1], parts[0] - parts[1])):
                for e in range(2):
                    for q in range(2):
                        to, at = slice(q * half, (q + 1) * half), slice(e * half, (e + 1) * half)
                        for n in range(half // share):
                            waves[e, h * (half // share) + n, m * share : (m + 1) * share, to] = both[
                                q * half + n * share : q * half + (n + 1) * share, at
                            ].astype(bf16)

        def back_columns(c):
            back = [jnp.dot(waves[e, c], table_ref[inverse_of[e]], preferred_element_type=f32) for e in range(2)]
            for i in range(share // span):
                start = c * share + i * span
                at = slice(start, start + span)
                for k in range(2):
                    to = slice(k * half, (k + 1) * half)
                    re, im = patch[0, at, to], patch[1, at, to]
                    sums = [0.0, 0.0]
                    for m in range(modes):
                        here = slice(m * share + i * span, m * share + (i + 1) * span)
                        b0, b1 = back[0][here], back[1][here]
                        mixed = b0 + b1 if k == 0 else b0 - b1
                        ur, ui = mixed[:, :half], mixed[:, half:]
                        pr, pi = probe[m, 0, at, to], probe[m, 1, at, to]
                        sums[0] = sums[0] + (pr * ur + pi * ui)
                        sums[1] = sums[1] + (pr * ui - pi * ur)
                        pgrad[m, 0, k, at, :] += re * ur + im * ui
                        pgrad[m, 1, k, at, :] += re * ui - im * ur
                    for p in range(2):
                        gs[p, k, 8 + start : 8 + start + span, :] = sums[p]

        skewed(error, back_rows)
        skewed(back_columns)

        down, across = jnp.zeros((8, LANES), f32), jnp.zeros((8, LANES), f32)
        for i in range(size // span):
            for p in range(2):
                for k in range(tiles):
                    at, after = pl.ds(row + i * span, span), pl.ds(row + i * span + 1, span)
                    g = gs[p, k, 8 + i * span : 8 + (i + 1) * span, :]
                    dy = g * (rowx[p, k, after, :] - rowx[p, k, at, :])
                    upper = slope[p, k, at, :]
                    dx = g * (upper + fy * (slope[p, k, after, :] - upper))
                    down = down + jnp.sum(dy.reshape(span // 8, 8, LANES), 0)
                    across = across + jnp.sum(dx.reshape(span // 8, 8, LANES), 0)
        moved_ref[0, j] = jnp.sum(down) / size
        moved_ref[1, j] = jnp.sum(across) / size

        base = pl.multiple_of(top // 8 * 8, 8)
        lag = top - base

        for p in range(2):
            g = []
            for k in range(tiles):
                here = gs[p, k, pl.ds(8 - lag, tall), :]
                before = gs[p, k, pl.ds(7 - lag, tall), :]
                g.append((here + fy * (before - here)).astype(bf16))
            wide = lax.dot_general(
                jnp.concatenate(g, axis=1), mix, (((1,), (1,)), ((), ())), preferred_element_type=f32
            )
            for k in range(tiles + 1):
                acc[first + k, p, pl.ds(base, tall), :] += wide[:, k * LANES : (k + 1) * LANES]

    @pl.loop(0, count_ref[0])
    def _(j):
        tile = left_ref[j] // LANES

        @pl.when((tile >= low) & (tile < high))
        def _():
            one(j)

    if carried:

        @pl.loop(0, keep)
        def _(k):
            for p in range(2):
                below_ref[k, p] = acc[k, p, rows : rows + size, :].astype(bf16)

    else:

        @pl.loop(0, size // span)
        def _(i):
            at = pl.multiple_of(i * span, span)
            for k in range(keep):
                for p in range(2):
                    temp[pl.ds(2 * k + p, span, stride=2 * keep + 1), :] = acc[k, p, pl.ds(rows + at, span), :]
            for y in range(span):
                below_ref[pl.ds(pl.multiple_of((at + y) * 2 * keep, ROWS), 2 * keep), :] = temp[
                    y * (2 * keep + 1) : y * (2 * keep + 1) + 2 * keep, :
                ].astype(bf16)


def step(modes, size, rows, slots, first_tile, low, high, keep, count, own, rim, carried, common):
    f32, bf16 = jnp.float32, jnp.bfloat16
    tiles = size // LANES
    deep = rows + size + 8
    vmem = pl.BlockSpec(memory_space=pltpu.VMEM)
    smem = pl.BlockSpec(memory_space=pltpu.SMEM)
    hbm = pl.BlockSpec(memory_space=pl.ANY)
    planes = (modes, 2, tiles, size, LANES)
    out_shape = [
        jax.ShapeDtypeStruct((count, 2, deep, LANES), f32),
        jax.ShapeDtypeStruct((keep, 2, size, LANES) if carried else (2 * keep * size, LANES), bf16),
        jax.ShapeDtypeStruct(planes, f32),
        jax.ShapeDtypeStruct((2, slots), f32),
    ]
    out_specs = [vmem, vmem, vmem, smem]
    own_arrays, own_parts = zip(*own)
    rim_arrays, rim_parts = zip(*rim)
    return pl.pallas_call(
        functools.partial(
            step_kernel, modes, size, rows, first_tile, low, high, keep, own_parts, rim_parts, bool(carried)
        ),
        out_shape=tuple(out_shape),
        in_specs=[smem] * 4 + [vmem] * 3 + [hbm] * (len(own) + len(rim)) + ([hbm, hbm, smem] if carried else []),
        out_specs=tuple(out_specs),
        scratch_shapes=[
            pltpu.VMEM((count, 2, rows + size, LANES), bf16),
            pltpu.VMEM((2, tiles, size + 32, LANES), f32),
            pltpu.VMEM((2, tiles, size + 32, LANES), f32),
            pltpu.VMEM((2, size, size), f32),
            pltpu.VMEM((2, modes, size, size), bf16),
            pltpu.VMEM((modes, 2, size, size), bf16),
            pltpu.VMEM((modes, 2, size, size), bf16),
            pltpu.VMEM((2, size // 2, size), bf16),
            pltpu.VMEM((2, tiles, size + 32, LANES), f32),
            pltpu.VMEM((32 * (2 * keep + 1) + 7, LANES), f32),
            pltpu.SemaphoreType.DMA((12,)),
        ],
        compiler_params=pltpu.CompilerParams(vmem_limit_bytes=30 << 20),
        cost_estimate=pl.CostEstimate(flops=3 << 30, bytes_accessed=16 << 20, transcendentals=0),
        name="step_b" if carried else "step_a",
    )(*common, *own_arrays, *rim_arrays, *carried)


def sort_kernel(lines, first, x_ref, out_ref, temp):
    n = out_ref.shape[2]
    line = 2 * lines
    start = 2 * first // ROWS * ROWS
    stop = -(-2 * (first + out_ref.shape[0]) // ROWS) * ROWS
    wide = stop - start + 1
    for y in range(n):
        temp[y * wide : (y + 1) * wide - 1, :] = x_ref[y * line + start : y * line + stop, :].astype(jnp.float32)
    for k in range(out_ref.shape[0]):
        for p in range(2):
            plane = temp[pl.ds(2 * (first + k) + p - start, n, stride=wide), :]
            out_ref[k, p] = plane.astype(jnp.bfloat16)


def sorted_planes(x, rows, lines, first, last):
    n = 128 if rows % 128 == 0 else rows
    return pl.pallas_call(
        functools.partial(sort_kernel, lines, first),
        grid=(rows // n,),
        out_shape=jax.ShapeDtypeStruct((last - first, 2, rows, LANES), jnp.bfloat16),
        in_specs=[pl.BlockSpec((n * lines * 2, LANES), lambda i: (i, 0))],
        out_specs=pl.BlockSpec((last - first, 2, n, LANES), lambda i: (0, 0, i, 0)),
        scratch_shapes=[pltpu.VMEM((n * (lines * 2 + 1) + 7, LANES), jnp.float32)],
        cost_estimate=pl.CostEstimate(flops=1 << 20, bytes_accessed=4 << 20, transcendentals=0),
        name="sort",
    )(x)


def prepare_kernel(tiles, x_ref, table_ref, measured_ref, out_ref, table_out, ordered_ref, temp):
    modes, _, size, _ = out_ref.shape
    slots = measured_ref.shape[0]
    span = 32
    table_out[...] = table_ref[0:4]

    @pl.loop(0, modes * (size // span))
    def _(i):
        at = pl.multiple_of(lax.rem(i, size // span) * span, span)
        m = i // (size // span)
        for p in range(2):
            for k in range(tiles):
                out_ref[m, p, pl.ds(at, span), k * LANES : (k + 1) * LANES] = x_ref[
                    pl.ds((i * span * tiles + k) * 2 + p, span, stride=2 * tiles), :
                ]

    @pl.loop(0, slots)
    def _(j):
        ordered = jnp.dot(measured_ref[j], table_ref[4], preferred_element_type=jnp.float32)
        for k in range(tiles):
            temp[k] = ordered[:, k * LANES : (k + 1) * LANES]
        for e in range(2):
            for k in range(tiles):
                ordered_ref[j, e, :, k * LANES : (k + 1) * LANES] = temp[
                    k, pl.ds(e, size // 2, stride=2), :
                ].astype(jnp.bfloat16)


def prepared(x, tables, measured, modes, size):
    vmem = pl.BlockSpec(memory_space=pltpu.VMEM)
    tiles = size // LANES
    return pl.pallas_call(
        functools.partial(prepare_kernel, tiles),
        out_shape=(
            jax.ShapeDtypeStruct((modes, 2, size, size), jnp.float32),
            jax.ShapeDtypeStruct((4, size, size), tables.dtype),
            jax.ShapeDtypeStruct((measured.shape[0], 2, size // 2, size), measured.dtype),
        ),
        in_specs=[vmem, vmem, vmem],
        out_specs=(vmem, vmem, vmem),
        scratch_shapes=[pltpu.VMEM((tiles, size, LANES), jnp.float32)],
        compiler_params=pltpu.CompilerParams(vmem_limit_bytes=16 << 20),
        cost_estimate=pl.CostEstimate(flops=1 << 20, bytes_accessed=8 << 20, transcendentals=0),
        name="prepare",
    )(x, tables, measured)


def tiled(x):
    *lead, two, width = x.shape
    n = math.prod(lead)
    x = x.reshape(n, two, width // LANES, LANES)
    return jnp.transpose(x, (0, 2, 1, 3)).reshape(-1, LANES)


def untiled(x, lead, width):
    n = math.prod(lead)
    x = jnp.transpose(x.reshape(n, width // LANES, 2, LANES), (0, 2, 1, 3))
    return x.reshape(*lead, 2, width)


def shards(object_tiles, probe, measured, offset_row, offset_col, subpixel, live_count):
    rows, _, width = object_tiles.shape
    modes, size = probe.shape[:2]
    slots = measured.shape[0]
    lines, tiles = width // LANES, size // LANES
    mid = lines // 2
    near = mid + tiles
    own = tiled(object_tiles)
    own_a = sorted_planes(own, rows, lines, 0, near)
    own_b = sorted_planes(own, rows, lines, near, lines)
    rim_a = passed_along(own_a[:, :, :size], "row", -1)
    rim_b = passed_along(own_b[:, :, :size], "row", -1)
    planes, tables, ordered = prepared(tiled(probe), dft_tables(size), measured, modes, size)
    common = (live_count, offset_row, offset_col, subpixel, planes, ordered, tables)
    whole = (0, near, 0)
    grad_a, below_a, sum_a, moved_a = step(
        modes, size, rows, slots, 0, 0, mid, mid, near, [(own_a, whole)], [(rim_a, whole)], (), common
    )
    landed_a = passed_along(below_a, "row", 1, odd=True)
    kept, rest = (mid, near, 0), (0, lines - near, tiles)
    grad_b, below_b, sums, moved = step(
        modes, size, rows, slots, mid, mid, lines, lines - mid, lines - mid,
        [(own_a, kept), (own_b, rest)], [(rim_a, kept), (rim_b, rest)], (grad_a, sum_a, moved_a), common,
    )
    probe_grad, grad, core_a, landed_b = summed(
        sums.reshape(-1, LANES), (grad_a, grad_b), below_a, below_b, modes, tiles, mid, rows, "row"
    )
    landed = jnp.concatenate(
        [(landed_a + core_a).reshape(size, 2 * mid, LANES), landed_b.reshape(size, 2 * (lines - mid), LANES)], axis=1
    )
    landed = lax.optimization_barrier(landed.reshape(-1, LANES))
    grad = grad.at[: landed.shape[0]].add(landed.astype(jnp.float32))
    return (untiled(grad, (rows,), width), untiled(probe_grad, (modes, size), size), moved)


def solution(mesh):
    in_specs = (
        P(("groups", "row"), None, None),
        P(),
        P(("groups", "row"), None, None),
        P(("groups", "row")),
        P(("groups", "row")),
        P(("groups", "row")),
        P(("groups", "row")),
    )
    out_specs = (
        P(("groups", "row"), None, None),
        P("groups", None, None, None),
        P(None, ("groups", "row")),
    )
    return jax.shard_map(shards, mesh=mesh, in_specs=in_specs, out_specs=out_specs, check_vma=False)
```
